32 devices in a mesh: probe: 4 (over y, core), store: 8 (over z, x).
Axes of the slice: x: 2, y: 2, z: 4, core: 2. Of those that a mesh axis runs over, the one named last changes fastest.
Arguments:
- probe_field: bfloat16 [96, 128, 8, 128], P('probe', 'store'), may hold values from -6 to 6
- bounds: int32 [96, 2], P('probe'), may hold values from 0 to 128, as said below
- courant: float32 [128, 8, 128], P('store'), may hold values from 0.1 to 0.2
- snapshots: bfloat16 [8, 128, 8, 128], P(None, 'store', 'probe'), may hold values from -0.5 to 0.5
- snap_times: int32 [8], replicated, may hold values from 0 to 7, each once
- basis_panels: bfloat16 [96, 128, 8, 128], P('probe', 'store'), may hold values from -0.015625 to 0.015625
Outputs:
- response: float32 [96, 128, 8, 128], P('probe', 'store')
- projection: float32 [96, 96], P(None, 'probe')
The draws below stay inside these ranges and needn't reach their ends.
Inputs may be any that keep to these rules, and one draw needn't show every extreme that they name: 0 <= bounds[k, 0] < bounds[k, 1] <= 128 for every probe k, and each region holds at least 32 rows.
All inputs are finite; a program needn't handle non-finite values.
Results may differ from the reference program's by a relative error of at most 0.0031.
Values may be sent and summed in bfloat16 or wider, within the bound.
No kernel may reach another device: no remote copies, remote signals or barrier semaphores. Data moves between devices by JAX's collectives and lax.ppermute only.
A program may use at most 64 MiB of HBM per device.

```python
import jax
import jax.numpy as jnp
from jax import lax

PROBES = 96
BASIS = 96
PY = 8
PZ = 128
NT = 8
NX = 128


def draw_bounds(key, part):
    key_low, key_span, key_first, key_second = jax.random.split(jax.random.fold_in(key, 17), 4)
    lower = jax.random.randint(key_low, (PROBES,), 0, NX // 2)
    extent = jax.random.randint(key_span, (PROBES,), NX // 4, NX // 2 + 1)
    upper = lower + extent
    first_pick = jax.random.randint(key_first, (), 0, PROBES)
    second_pick = (first_pick + 1 + jax.random.randint(key_second, (), 0, PROBES - 1)) % PROBES
    lower = lower.at[first_pick].set(0)
    upper = upper.at[second_pick].set(NX)
    return jnp.stack([lower, upper], axis=1).astype(jnp.int32)


def draw_probe_field(key, part):
    key_rough = jax.random.fold_in(jax.random.fold_in(key, 31), 0)
    shape_full = (PROBES, NX, PY, PZ)
    values = jnp.clip(jax.random.normal(key_rough, shape_full, jnp.float32), -6.0, 6.0)
    return values.astype(jnp.bfloat16)


def draw_snapshots(key, part):
    key_rough = jax.random.fold_in(jax.random.fold_in(key, 53), 0)
    shape_full = (NT, NX, PY, PZ)
    values = jnp.clip(0.08 * jax.random.normal(key_rough, shape_full, jnp.float32), -0.5, 0.5)
    return values.astype(jnp.bfloat16)


def block_levels(own_key, shape, cuts, least, largest):
    gain = 1.0
    for dim, blocks in cuts:
        draws = jax.random.uniform(jax.random.fold_in(jax.random.fold_in(own_key, 6), dim), (blocks,), jnp.float32, least / len(cuts), largest / len(cuts))
        gain = gain * jnp.repeat(jnp.exp(draws), shape[dim] // blocks).reshape((-1,) + (1,) * (len(shape) - 1 - dim))
    return gain


def centred(key, shape, deviation, limit, shards=(), kind=jnp.bfloat16):
    entries = jax.random.normal(key, shape, jnp.float32) * deviation
    if len(shards) > 0:
        entries = block_levels(key, shape, shards, -0.22, 0.18) * entries
    return jnp.clip(entries, min=-limit, max=limit).astype(kind)


def setup_inputs(seed: int = 0) -> dict:
    seeds = jax.random.split(jax.random.key(seed), 7)
    return {
        "probe_field": draw_probe_field(jax.random.fold_in(seeds[6], 71), 0),
        "bounds": draw_bounds(jax.random.fold_in(seeds[6], 71), 0),
        "courant": jnp.clip(0.1 + 0.1 * jax.random.uniform(seeds[2], (NX, PY, PZ), jnp.float32) ** block_levels(seeds[2], (NX, PY, PZ), ((0, 8),), -0.2, 0.2), 0.1, 0.2),
        "snapshots": draw_snapshots(jax.random.fold_in(seeds[6], 71), 0),
        "snap_times": jax.random.permutation(seeds[4], NT).astype(jnp.int32),
        "basis_panels": centred(seeds[5], (BASIS, NX, PY, PZ), (NX * PY * PZ) ** -0.5, 0.015625, ((0, 4), (1, 8))),
    }


stencil_taps = (-205.0 / 72.0, 8.0 / 5.0, -1.0 / 5.0, 8.0 / 315.0, -1.0 / 560.0)


def laplace(full):
    extent_x = full.shape[-3] - 8
    extent_y = full.shape[-2] - 8
    extent_z = full.shape[-1] - 8
    centre = full[..., 4:4 + extent_x, 4:4 + extent_y, 4:4 + extent_z]
    totals = 3.0 * stencil_taps[0] * centre
    for distance in range(1, 5):
        along = full[..., 4 + distance:4 + distance + extent_x, 4:4 + extent_y, 4:4 + extent_z]
        along = along + full[..., 4 - distance:4 - distance + extent_x, 4:4 + extent_y, 4:4 + extent_z]
        along = along + full[..., 4:4 + extent_x, 4 + distance:4 + distance + extent_y, 4:4 + extent_z]
        along = along + full[..., 4:4 + extent_x, 4 - distance:4 - distance + extent_y, 4:4 + extent_z]
        along = along + full[..., 4:4 + extent_x, 4:4 + extent_y, 4 + distance:4 + distance + extent_z]
        along = along + full[..., 4:4 + extent_x, 4:4 + extent_y, 4 - distance:4 - distance + extent_z]
        totals = totals + stencil_taps[distance] * along
    return totals


def reference(probe_field, bounds, courant, snapshots, snap_times, basis_panels):
    depth_index = jnp.arange(NX, dtype=jnp.int32)

    def single_probe(inputs_pair):
        values_in, limits = inputs_pair
        inside = ((depth_index >= limits[0]) & (depth_index < limits[1])).astype(jnp.float32)
        perturb = values_in.astype(jnp.float32) * inside[:, None, None]

        def advance(state_pair, slot_index):
            earlier, current = state_pair
            source = perturb * snapshots[slot_index].astype(jnp.float32)
            advanced = 2.0 * current - earlier + courant * laplace(jnp.pad(current, 4)) + source
            return (current, advanced), None

        empty_field = jnp.zeros((NX, PY, PZ), jnp.float32)
        (earlier, current), unused = lax.scan(advance, (empty_field, empty_field), snap_times)
        return current

    response = lax.map(single_probe, (probe_field, bounds))
    response_low = response.astype(jnp.bfloat16)
    projection = lax.dot_general(basis_panels.reshape(BASIS, -1), response_low.reshape(PROBES, -1),
                                 (((1,), (1,)), ((), ())), preferred_element_type=jnp.float32)
    return response, projection
```

```python
import functools

import jax
import jax.numpy as jnp
import numpy as np
from jax import lax
from jax.experimental import pallas as pl
from jax.experimental.pallas import tpu as pltpu
from jax.sharding import PartitionSpec as P

taps = (-205.0 / 72.0, 8.0 / 5.0, -1.0 / 5.0, 8.0 / 315.0, -1.0 / 560.0)
SPAN = 24


def tables(cells_y, cells_z):
    ratio = [0.0] + [t / taps[1] for t in taps[1:]]
    left = np.zeros((SPAN, cells_y, SPAN + 8, cells_y), np.float32)
    for i in range(SPAN):
        for d in range(1, 5):
            for y in range(cells_y):
                left[i, y, i + 4 + d, y] = ratio[d]
                left[i, y, i + 4 - d, y] = ratio[d]
                if y + d < cells_y:
                    left[i, y, i + 4, y + d] = ratio[d]
                if y - d >= 0:
                    left[i, y, i + 4, y - d] = ratio[d]
    right = np.zeros((cells_z, cells_z), np.float32)
    for z in range(cells_z):
        for d in range(1, 5):
            if z + d < cells_z:
                right[z, z + d] = ratio[d]
            if z - d >= 0:
                right[z, z - d] = ratio[d]
    left = left.reshape(SPAN * cells_y, (SPAN + 8) * cells_y)
    return left, np.concatenate([right, right], axis=0)


def spans(rows):
    out = []
    while rows > 0:
        out.append(min(SPAN, rows))
        rows -= out[-1]
    return out


def march(steps, rows, halo, wide, par_ref, *refs):
    pieces = refs[0:6]
    extras = refs[6:12]
    left_ref, right_ref, own_ref, send_ref = refs[12:16]
    pert, snap, scale, gain, fields, split = refs[16:22]
    total = 2 * rows + 2 * halo
    cy = 8
    par = par_ref[0]
    even = (halo, halo + rows, halo + 2 * rows, 0, halo - rows, halo + 3 * rows)
    odd = (halo + rows, halo, halo - rows, halo + 3 * rows, halo + 2 * rows, 0)
    counts = (rows, rows, rows, halo - rows, rows, halo - rows)
    starts = [e + par * (o - e) for e, o in zip(even, odd)]

    def put(piece, value):
        at = pl.multiple_of(starts[piece] * cy, 32)
        return pl.ds(at, counts[piece] * cy), value

    @pl.when(pl.program_id(0) == 0)
    def _():
        for j in range(6):
            where = pl.ds(pl.multiple_of(starts[j] * cy, 32), counts[j] * cy)
            flat = (counts[j] * cy, 128)
            for t in range(steps):
                snap[t, where, :] = extras[j][t].reshape(flat).astype(jnp.float32)
            c = extras[j][steps].astype(jnp.float32) + extras[j][steps + 1].astype(jnp.float32)
            c = c.reshape(flat)
            scale[where, :] = 2.0 + (3.0 * taps[0]) * c
            gain[where, :] = taps[1] * c

    for j in range(6):
        where = pl.ds(pl.multiple_of(starts[j] * cy, 32), counts[j] * cy)
        pert[where, :] = pieces[j][0].reshape(counts[j] * cy, 128).astype(jnp.float32)

    def keep(slot, where, value):
        high = value.astype(jnp.bfloat16)
        low = (value - high.astype(jnp.float32)).astype(jnp.bfloat16)
        split[slot, where, 0:128] = high
        split[slot, where, 128:256] = low

    at = 0
    for m in spans(total):
        where = pl.ds(at * cy, m * cy)
        first = pert[where, :] * snap[0, where, :]
        fields[0, where, :] = first
        keep(0, where, first)
        at += m

    def advanced(n, row, m):
        now, before = (n + 1) % 2, n % 2
        where = pl.ds(row * cy, m * cy) if isinstance(row, int) else pl.ds(pl.multiple_of(row * cy, 32), m * cy)
        low = (row - 4) * cy
        around = pl.ds(low, (m + 8) * cy) if isinstance(row, int) else pl.ds(pl.multiple_of(low, 32), (m + 8) * cy)
        both = jnp.dot(
            left_ref[0 : m * cy, 0 : (m + 8) * cy],
            split[now, around, :],
            preferred_element_type=jnp.float32,
        )
        along = jnp.dot(split[now, where, :], right_ref[...], preferred_element_type=jnp.float32)
        total_taps = both[:, 0:128] + both[:, 128:256] + along
        value = scale[where, :] * fields[now, where, :] + gain[where, :] * total_taps
        value = value + pert[where, :] * snap[n, where, :]
        if n > 1:
            value = value - fields[before, where, :]
        return where, value

    for n in range(1, steps - 1):
        at = 4 * n
        for m in spans(total - 8 * n):
            where, value = advanced(n, at, m)
            fields[n % 2, where, :] = value
            keep(n % 2, where, value)
            at += m
    _, value = advanced(steps - 1, starts[0], rows)
    own_ref[0] = value.reshape(rows, cy, 128)
    _, value = advanced(steps - 1, starts[1], rows)
    send_ref[0] = value.reshape(rows, cy, 128).astype(jnp.bfloat16)


def propagate(par, pieces, extras, steps, rows, halo):
    half, _, cy, cz = pieces[0].shape
    left, right = tables(cy, cz)
    left, right = jnp.asarray(left, jnp.bfloat16), jnp.asarray(right, jnp.bfloat16)
    counts = (rows, rows, rows, halo - rows, rows, halo - rows)
    total = 2 * rows + 2 * halo
    fixed = lambda *shape: pl.BlockSpec(shape, lambda k, p: (0,) * len(shape), pipeline_mode=pl.Buffered(1))
    block = lambda count: pl.BlockSpec((1, count, cy, cz), lambda k, p: (k, 0, 0, 0))
    grid_spec = pltpu.PrefetchScalarGridSpec(
        num_scalar_prefetch=1,
        grid=(half,),
        in_specs=[block(c) for c in counts]
        + [fixed(steps + 2, c, cy, cz) for c in counts]
        + [fixed(*left.shape), fixed(*right.shape)],
        out_specs=[block(rows), block(rows)],
        scratch_shapes=[
            pltpu.VMEM((total * cy, cz), jnp.float32),
            pltpu.VMEM((steps, total * cy, cz), jnp.float32),
            pltpu.VMEM((total * cy, cz), jnp.float32),
            pltpu.VMEM((total * cy, cz), jnp.float32),
            pltpu.VMEM((2, total * cy, cz), jnp.float32),
            pltpu.VMEM((2, total * cy, 2 * cz), jnp.bfloat16),
        ],
    )
    return pl.pallas_call(
        functools.partial(march, steps, rows, halo, half),
        grid_spec=grid_spec,
        out_shape=[
            jax.ShapeDtypeStruct((half, rows, cy, cz), jnp.float32),
            jax.ShapeDtypeStruct((half, rows, cy, cz), jnp.bfloat16),
        ],
        compiler_params=pltpu.CompilerParams(vmem_limit_bytes=40 << 20),
        name="march",
    )(par[None], *pieces, *extras, left, right)


def local(probe_field, bounds, courant, snapshots, snap_times, basis_panels):
    probes_here, rows, cy, cz = probe_field.shape
    steps = snap_times.shape[0]
    half = probes_here // 2
    halo = 4 * (steps - 1)
    far = halo - rows
    devices = lax.axis_size("store")
    place = lax.axis_index("store")
    par = (place % 2).astype(jnp.int32)
    swap = [(i, i ^ 1) for i in range(devices)]
    perm_a = [(i, i - 2) for i in range(2, devices, 2)] + [(i, i + 2) for i in range(1, devices - 2, 2)]
    perm_b = [(i, i + 2) for i in range(0, devices - 2, 2)] + [(i, i - 2) for i in range(3, devices, 2)]
    hop = lambda x, pairs: lax.ppermute(x, "store", pairs)
    cut = lambda x, start: lax.dynamic_slice_in_dim(x, start, far, axis=1)
    near = rows - far

    def around(own, other):
        partner = hop(other, swap)
        return (
            own,
            partner,
            hop(own, perm_a),
            hop(cut(own, near * (1 - par)), perm_b),
            hop(partner, perm_b),
            hop(cut(partner, near * par), perm_a),
        )

    row = place * rows + jnp.arange(rows, dtype=jnp.int32)
    inside = (row[None, :] >= bounds[:, 0:1]) & (row[None, :] < bounds[:, 1:2])
    perturb = jnp.where(inside[:, :, None, None], probe_field, jnp.zeros_like(probe_field))
    mine = lax.dynamic_slice_in_dim(perturb, half * par, half, axis=0)
    theirs = lax.dynamic_slice_in_dim(perturb, half * (1 - par), half, axis=0)

    all_snaps = lax.all_gather(snapshots, "probe", axis=2, tiled=True)
    all_snaps = jnp.take(all_snaps, snap_times, axis=0)
    high = lax.reduce_precision(courant, 8, 7)
    extra = jnp.concatenate(
        [all_snaps, high.astype(jnp.bfloat16)[None], (courant - high).astype(jnp.bfloat16)[None]], axis=0
    )
    extras = around(extra, extra)
    pieces = around(mine, theirs)
    own, send = propagate(par, pieces, extras, steps, rows, halo)
    back = hop(send, swap).astype(jnp.float32)
    first = par == 0
    response = jnp.concatenate([jnp.where(first, own, back), jnp.where(first, back, own)], axis=0)
    low = response.astype(jnp.bfloat16).reshape(probes_here, -1)

    member = lax.axis_index("probe")
    members = lax.axis_size("probe")
    panels = [basis_panels]
    span = 1
    while span < members:
        pairs = [(i, i ^ span) for i in range(members)]
        panels = panels + [lax.ppermute(x, "probe", pairs) for x in panels]
        span *= 2
    parts = [
        lax.dot_general(
            x.reshape(x.shape[0], -1), low, (((1,), (1,)), ((), ())), preferred_element_type=jnp.float32
        )
        for x in panels
    ]
    parts = jnp.stack(parts)
    order = jnp.arange(members) ^ member
    product = jnp.take(parts, order, axis=0).reshape(-1, probes_here)
    span = 1
    while span < devices:
        product = product + hop(product, [(i, i ^ span) for i in range(devices)])
        span *= 2
    return response, product


def solution(mesh):
    placed = (
        P("probe", "store", None, None),
        P("probe", None),
        P("store", None, None),
        P(None, "store", "probe", None),
        P(),
        P("probe", "store", None, None),
    )
    return jax.shard_map(
        local,
        mesh=mesh,
        in_specs=placed,
        out_specs=(P("probe", "store", None, None), P(None, "probe")),
        check_vma=False,
    )
```

```python
import functools

import jax
import jax.numpy as jnp
import numpy as np
from jax import lax
from jax.experimental import pallas as pl
from jax.experimental.pallas import tpu as pltpu
from jax.sharding import PartitionSpec as P

taps = (-205.0 / 72.0, 8.0 / 5.0, -1.0 / 5.0, 8.0 / 315.0, -1.0 / 560.0)
SPAN = 24
PACK = 2
AHEAD = 1


def tables(cells_y, cells_z):
    ratio = [0.0] + [t / taps[1] for t in taps[1:]]
    left = np.zeros((SPAN, cells_y, SPAN + 8, cells_y), np.float32)
    for i in range(SPAN):
        for d in range(1, 5):
            for y in range(cells_y):
                left[i, y, i + 4 + d, y] = ratio[d]
                left[i, y, i + 4 - d, y] = ratio[d]
                if y + d < cells_y:
                    left[i, y, i + 4, y + d] = ratio[d]
                if y - d >= 0:
                    left[i, y, i + 4, y - d] = ratio[d]
    right = np.zeros((cells_z, cells_z), np.float32)
    for z in range(cells_z):
        for d in range(1, 5):
            if z + d < cells_z:
                right[z, z + d] = ratio[d]
            if z - d >= 0:
                right[z, z - d] = ratio[d]
    left = left.reshape(SPAN * cells_y, (SPAN + 8) * cells_y)
    return left, np.concatenate([right, right], axis=0)


def spans(rows):
    out = []
    while rows > 0:
        out.append(min(SPAN, rows))
        rows -= out[-1]
    return out


def shares(steps, rows, halo):
    return (steps + 1) // 2, (-(-(halo - rows) // 4) + 1) // 2


def march(steps, rows, halo, scalars, *refs):
    pieces = refs[0:6]
    extras = refs[6:10]
    left_ref, right_ref, own_ref, send_ref = refs[10:14]
    pert, snap, scale, gain, fields, split = refs[14:20]
    total = 2 * rows + 2 * halo
    cy = 8
    far = halo - rows
    par, core = scalars[0], scalars[1]
    even = (halo, halo + rows, halo + 2 * rows, 0, halo - rows, halo + 3 * rows)
    odd = (halo + rows, halo, halo - rows, halo + 3 * rows, halo + 2 * rows, 0)
    counts = (rows, rows, rows, far, rows, far)
    starts = [e + par * (o - e) for e, o in zip(even, odd)]
    near_half, far_half = shares(steps, rows, halo)

    @pl.when(pl.program_id(0) == 0)
    def _():
        for side, order in ((0, (0, 2, 3)), (1, (1, 4, 5))):
            at = 0
            for j, kept in zip(order, (near_half, near_half, far_half)):
                where = pl.ds(pl.multiple_of(starts[j] * cy, 32), counts[j] * cy)
                flat = (counts[j] * cy, 128)
                for t in range(kept + 1):
                    mine = extras[side][at : at + counts[j]].reshape(flat).astype(jnp.float32)
                    other = extras[side + 2][at : at + counts[j]].reshape(flat).astype(jnp.float32)
                    at += counts[j]
                    if t < kept:
                        snap[2 * t + core, where, :] = mine
                        snap[2 * t + 1 - core, where, :] = other
                    else:
                        scale[where, :] = 2.0 + (3.0 * taps[0]) * (mine + other)
                        gain[where, :] = taps[1] * (mine + other)

    for q in range(PACK):
        probe = pl.program_id(0) * PACK + q
        low = scalars[2 + 2 * probe]
        high = scalars[3 + 2 * probe]
        for j in range(6):
            where = pl.ds(pl.multiple_of(starts[j] * cy, 32), counts[j] * cy)
            value = pieces[j][q].astype(jnp.float32)
            plane = lax.broadcasted_iota(jnp.int32, value.shape, 0) + starts[j]
            value = jnp.where((plane >= low) & (plane < high), value, 0.0)
            pert[q, where, :] = value.reshape(counts[j] * cy, 128)

    def keep(q, slot, where, value):
        high = value.astype(jnp.bfloat16)
        low = (value - high.astype(jnp.float32)).astype(jnp.bfloat16)
        split[q, slot, where, 0:128] = high
        split[q, slot, where, 128:256] = low

    at = 0
    for m in spans(total):
        where = pl.ds(at * cy, m * cy)
        for q in range(PACK):
            first = pert[q, where, :] * snap[0, where, :]
            fields[q, 0, where, :] = first
            keep(q, 0, where, first)
        at += m

    def slab(row, count):
        if isinstance(row, int):
            return pl.ds(row * cy, count * cy)
        return pl.ds(pl.multiple_of(row * cy, 32), count * cy)

    def products(q, n, row, m):
        now = (n + 1) % 2
        both = jnp.dot(
            left_ref[0 : m * cy, 0 : (m + 8) * cy],
            split[q, now, slab(row - 4, m + 8), :],
            preferred_element_type=jnp.float32,
        )
        along = jnp.dot(split[q, now, slab(row, m), :], right_ref[...], preferred_element_type=jnp.float32)
        return both, along

    def advanced(q, n, row, m, both, along):
        now, before = (n + 1) % 2, n % 2
        where = slab(row, m)
        total_taps = both[:, 0:128] + both[:, 128:256] + along
        value = scale[where, :] * fields[q, now, where, :] + gain[where, :] * total_taps
        value = value + pert[q, where, :] * snap[n, where, :]
        if n > 1:
            value = value - fields[q, before, where, :]
        if n < steps - 1:
            fields[q, before, where, :] = value
            keep(q, before, where, value)
        elif row is starts[0]:
            own_ref[q] = value.reshape(rows, cy, 128)
        else:
            send_ref[q] = value.reshape(rows, cy, 128).astype(jnp.bfloat16)

    items = []
    for n in range(1, steps - 1):
        at = 4 * n
        for m in spans(total - 8 * n):
            items += [(q, n, at, m) for q in range(PACK)]
            at += m
    for row in starts[0:2]:
        items += [(q, steps - 1, row, rows) for q in range(PACK)]
    queue = []
    for item in items:
        queue.append((item, products(*item)))
        if len(queue) > AHEAD:
            first, made = queue.pop(0)
            advanced(*first, *made)
    for first, made in queue:
        advanced(*first, *made)


def propagate(scalars, pieces, extras, steps, rows, halo):
    half, _, cy, cz = pieces[0].shape
    left, right = tables(cy, cz)
    left, right = jnp.asarray(left, jnp.bfloat16), jnp.asarray(right, jnp.bfloat16)
    counts = (rows, rows, rows, halo - rows, rows, halo - rows)
    total = 2 * rows + 2 * halo
    fixed = lambda *shape: pl.BlockSpec(shape, lambda k, p: (0,) * len(shape), pipeline_mode=pl.Buffered(1))
    block = lambda count: pl.BlockSpec((PACK, count, cy, cz), lambda k, p: (k, 0, 0, 0))
    grid_spec = pltpu.PrefetchScalarGridSpec(
        num_scalar_prefetch=1,
        grid=(half // PACK,),
        in_specs=[block(c) for c in counts]
        + [fixed(*x.shape) for x in extras]
        + [fixed(*left.shape), fixed(*right.shape)],
        out_specs=[block(rows), block(rows)],
        scratch_shapes=[
            pltpu.VMEM((PACK, total * cy, cz), jnp.float32),
            pltpu.VMEM((steps + steps % 2, total * cy, cz), jnp.float32),
            pltpu.VMEM((total * cy, cz), jnp.float32),
            pltpu.VMEM((total * cy, cz), jnp.float32),
            pltpu.VMEM((PACK, 2, total * cy, cz), jnp.float32),
            pltpu.VMEM((PACK, 2, total * cy, 2 * cz), jnp.bfloat16),
        ],
    )
    cells = half * total * cy * cz
    return pl.pallas_call(
        functools.partial(march, steps, rows, halo),
        grid_spec=grid_spec,
        out_shape=[
            jax.ShapeDtypeStruct((half, rows, cy, cz), jnp.float32),
            jax.ShapeDtypeStruct((half, rows, cy, cz), jnp.bfloat16),
        ],
        compiler_params=pltpu.CompilerParams(vmem_limit_bytes=40 << 20),
        cost_estimate=pl.CostEstimate(flops=cells * 4000, bytes_accessed=cells * 4, transcendentals=0),
        name="march",
    )(scalars, *pieces, *extras, left, right)


def local(probe_field, bounds, courant, snapshots, snap_times, basis_panels):
    probes_here, rows, cy, cz = probe_field.shape
    steps = snap_times.shape[0]
    half = probes_here // 2
    halo = 4 * (steps - 1)
    far = halo - rows
    devices = lax.axis_size("store")
    place = lax.axis_index("store")
    member = lax.axis_index("probe")
    members = lax.axis_size("probe")
    par = (place % 2).astype(jnp.int32)
    core = (member % 2).astype(jnp.int32)
    swap = [(i, i ^ 1) for i in range(devices)]
    perm_a = [(i, i - 2) for i in range(2, devices, 2)] + [(i, i + 2) for i in range(1, devices - 2, 2)]
    perm_b = [(i, i + 2) for i in range(0, devices - 2, 2)] + [(i, i - 2) for i in range(3, devices, 2)]
    hop = lambda x, pairs: lax.ppermute(x, "store", pairs)
    cores = lambda x: lax.ppermute(x, "probe", [(i, i ^ 1) for i in range(members)])
    cut = lambda x, start: lax.dynamic_slice_in_dim(x, start, far, axis=1)
    near = rows - far

    all_snaps = lax.all_gather(snapshots, "probe", axis=2, tiled=True)
    near_half, far_half = shares(steps, rows, halo)
    chosen = jnp.minimum(2 * jnp.arange(near_half) + core, steps - 1)
    picked = jnp.take(all_snaps, jnp.take(snap_times, chosen, mode="clip"), axis=0, mode="clip")
    high = lax.reduce_precision(courant, 8, 7)
    rate = jnp.where(core == 0, high, courant - high).astype(jnp.bfloat16)[None]
    extra = jnp.concatenate([picked, rate], axis=0)
    extra_a = hop(extra, perm_a)
    extra_b = hop(cut(jnp.concatenate([picked[:far_half], rate], axis=0), near * (1 - par)), perm_b)
    planes = lambda x: x.reshape(-1, cy, cz)
    bundle = jnp.concatenate([planes(extra), planes(extra_a), planes(extra_b)], axis=0)
    bundle_x = hop(bundle, swap)
    extras = (bundle, bundle_x, cores(bundle), cores(bundle_x))

    mine = lax.dynamic_slice_in_dim(probe_field, half * par, half, axis=0)
    theirs = lax.dynamic_slice_in_dim(probe_field, half * (1 - par), half, axis=0)
    partner = hop(theirs, swap)
    pieces = (
        mine,
        partner,
        hop(mine, perm_a),
        hop(cut(mine, near * (1 - par)), perm_b),
        hop(partner, perm_b),
        hop(cut(partner, near * par), perm_a),
    )
    base = (place // 2) * 2 * rows - halo
    mine_bounds = lax.dynamic_slice_in_dim(bounds, half * par, half, axis=0) - base
    scalars = jnp.concatenate([jnp.stack([par, core]), mine_bounds.reshape(-1)]).astype(jnp.int32)
    own, send = propagate(scalars, pieces, extras, steps, rows, halo)
    back = hop(send, swap).astype(jnp.float32)
    first = par == 0
    response = jnp.concatenate([jnp.where(first, own, back), jnp.where(first, back, own)], axis=0)
    low = response.astype(jnp.bfloat16).reshape(probes_here, -1)

    panels = [basis_panels]
    span = members // 2
    while span:
        pairs = [(i, i ^ span) for i in range(members)]
        panels = [y for x in panels for y in (x, lax.ppermute(x, "probe", pairs))]
        span //= 2
    parts = [
        lax.dot_general(
            x.reshape(x.shape[0], -1), low, (((1,), (1,)), ((), ())), preferred_element_type=jnp.float32
        )
        for x in panels
    ]
    parts = jnp.stack(parts)
    order = jnp.arange(members) ^ member
    product = jnp.take(parts, order, axis=0, mode="clip").reshape(-1, probes_here)
    span = 1
    while span < devices:
        product = product + hop(product, [(i, i ^ span) for i in range(devices)])
        span *= 2
    return response, product


def solution(mesh):
    placed = (
        P("probe", "store", None, None),
        P("probe", None),
        P("store", None, None),
        P(None, "store", "probe", None),
        P(),
        P("probe", "store", None, None),
    )
    return jax.shard_map(
        local,
        mesh=mesh,
        in_specs=placed,
        out_specs=(P("probe", "store", None, None), P(None, "probe")),
        check_vma=False,
    )
```

```python
import functools

import jax
import jax.numpy as jnp
import numpy as np
from jax import lax
from jax.experimental import pallas as pl
from jax.experimental.pallas import tpu as pltpu
from jax.sharding import PartitionSpec as P

taps = (-205.0 / 72.0, 8.0 / 5.0, -1.0 / 5.0, 8.0 / 315.0, -1.0 / 560.0)
SPAN = 24
PACK = 2
AHEAD = 1


def tables(cells_y, cells_z):
    ratio = [0.0] + [t / taps[1] for t in taps[1:]]
    left = np.zeros((SPAN, cells_y, SPAN + 8, cells_y), np.float32)
    for i in range(SPAN):
        for d in range(1, 5):
            for y in range(cells_y):
                left[i, y, i + 4 + d, y] = ratio[d]
                left[i, y, i + 4 - d, y] = ratio[d]
                if y + d < cells_y:
                    left[i, y, i + 4, y + d] = ratio[d]
                if y - d >= 0:
                    left[i, y, i + 4, y - d] = ratio[d]
    right = np.zeros((cells_z, cells_z), np.float32)
    for z in range(cells_z):
        for d in range(1, 5):
            if z + d < cells_z:
                right[z, z + d] = ratio[d]
            if z - d >= 0:
                right[z, z - d] = ratio[d]
    left = left.reshape(SPAN * cells_y, (SPAN + 8) * cells_y)
    return left, np.concatenate([right, right], axis=0)


def spans(rows):
    out = []
    while rows > 0:
        out.append(min(SPAN, rows))
        rows -= out[-1]
    return out


def shares(steps, rows, halo):
    return (steps + 1) // 2, (-(-(halo - rows) // 4) + 1) // 2


def march(steps, rows, halo, begin, scalars, *refs):
    pieces = refs[0:6]
    extras = refs[6:10]
    left_ref, right_ref, own_ref, send_ref = refs[10:14]
    pert, snap, scale, gain, fields, split = refs[14:20]
    total = 2 * rows + 2 * halo
    cy = 8
    far = halo - rows
    par, core = scalars[0], scalars[1]
    even = (halo, halo + rows, halo + 2 * rows, 0, halo - rows, halo + 3 * rows)
    odd = (halo + rows, halo, halo - rows, halo + 3 * rows, halo + 2 * rows, 0)
    counts = (rows, rows, rows, far, rows, far)
    starts = [e + par * (o - e) for e, o in zip(even, odd)]
    near_half, far_half = shares(steps, rows, halo)

    @pl.when(pl.program_id(0) == 0)
    def _():
        for side, order in ((0, (0, 2, 3)), (1, (1, 4, 5))):
            at = 0
            for j, kept in zip(order, (near_half, near_half, far_half)):
                where = pl.ds(pl.multiple_of(starts[j] * cy, 32), counts[j] * cy)
                flat = (counts[j] * cy, 128)
                for t in range(kept + 1):
                    mine = extras[side][at : at + counts[j]].reshape(flat).astype(jnp.float32)
                    other = extras[side + 2][at : at + counts[j]].reshape(flat).astype(jnp.float32)
                    at += counts[j]
                    if t < kept:
                        snap[2 * t + core, where, :] = mine
                        snap[2 * t + 1 - core, where, :] = other
                    else:
                        scale[where, :] = 2.0 + (3.0 * taps[0]) * (mine + other)
                        gain[where, :] = taps[1] * (mine + other)

    for q in range(PACK):
        probe = begin + pl.program_id(0) * PACK + q
        low = scalars[2 + 2 * probe]
        high = scalars[3 + 2 * probe]
        for j in range(6):
            where = pl.ds(pl.multiple_of(starts[j] * cy, 32), counts[j] * cy)
            value = pieces[j][probe].astype(jnp.float32)
            plane = lax.broadcasted_iota(jnp.int32, value.shape, 0) + starts[j]
            value = jnp.where((plane >= low) & (plane < high), value, 0.0)
            pert[q, where, :] = value.reshape(counts[j] * cy, 128)

    def keep(q, slot, where, value):
        high = value.astype(jnp.bfloat16)
        low = (value - high.astype(jnp.float32)).astype(jnp.bfloat16)
        split[q, slot, where, 0:128] = high
        split[q, slot, where, 128:256] = low

    at = 0
    for m in spans(total):
        where = pl.ds(at * cy, m * cy)
        for q in range(PACK):
            first = pert[q, where, :] * snap[0, where, :]
            fields[q, 0, where, :] = first
            keep(q, 0, where, first)
        at += m

    def slab(row, count):
        if isinstance(row, int):
            return pl.ds(row * cy, count * cy)
        return pl.ds(pl.multiple_of(row * cy, 32), count * cy)

    def products(q, n, row, m):
        now = (n + 1) % 2
        both = jnp.dot(
            left_ref[0 : m * cy, 0 : (m + 8) * cy],
            split[q, now, slab(row - 4, m + 8), :],
            preferred_element_type=jnp.float32,
        )
        along = jnp.dot(split[q, now, slab(row, m), :], right_ref[...], preferred_element_type=jnp.float32)
        return both, along

    def advanced(q, n, row, m, both, along):
        now, before = (n + 1) % 2, n % 2
        where = slab(row, m)
        total_taps = both[:, 0:128] + both[:, 128:256] + along
        value = scale[where, :] * fields[q, now, where, :] + gain[where, :] * total_taps
        value = value + pert[q, where, :] * snap[n, where, :]
        if n > 1:
            value = value - fields[q, before, where, :]
        if n < steps - 1:
            fields[q, before, where, :] = value
            keep(q, before, where, value)
        elif row is starts[0]:
            own_ref[pl.program_id(0) * PACK + q] = value.reshape(rows, cy, 128)
        else:
            send_ref[pl.program_id(0) * PACK + q] = value.reshape(rows, cy, 128).astype(jnp.bfloat16)

    items = []
    for n in range(1, steps - 1):
        at = 4 * n
        for m in spans(total - 8 * n):
            items += [(q, n, at, m) for q in range(PACK)]
            at += m
    for row in starts[0:2]:
        items += [(q, steps - 1, row, rows) for q in range(PACK)]
    queue = []
    for item in items:
        queue.append((item, products(*item)))
        if len(queue) > AHEAD:
            first, made = queue.pop(0)
            advanced(*first, *made)
    for first, made in queue:
        advanced(*first, *made)


def propagate(scalars, pieces, extras, begin, count, steps, rows, halo):
    _, _, cy, cz = pieces[0].shape
    left, right = tables(cy, cz)
    left, right = jnp.asarray(left, jnp.bfloat16), jnp.asarray(right, jnp.bfloat16)
    total = 2 * rows + 2 * halo
    whole = pl.BlockSpec(memory_space=pltpu.VMEM)
    grid_spec = pltpu.PrefetchScalarGridSpec(
        num_scalar_prefetch=1,
        grid=(count // PACK,),
        in_specs=[whole] * (len(pieces) + len(extras) + 2),
        out_specs=[whole, whole],
        scratch_shapes=[
            pltpu.VMEM((PACK, total * cy, cz), jnp.float32),
            pltpu.VMEM((steps + steps % 2, total * cy, cz), jnp.float32),
            pltpu.VMEM((total * cy, cz), jnp.float32),
            pltpu.VMEM((total * cy, cz), jnp.float32),
            pltpu.VMEM((PACK, 2, total * cy, cz), jnp.float32),
            pltpu.VMEM((PACK, 2, total * cy, 2 * cz), jnp.bfloat16),
        ],
    )
    cells = count * total * cy * cz
    return pl.pallas_call(
        functools.partial(march, steps, rows, halo, begin),
        grid_spec=grid_spec,
        out_shape=[
            jax.ShapeDtypeStruct((count, rows, cy, cz), jnp.float32),
            jax.ShapeDtypeStruct((count, rows, cy, cz), jnp.bfloat16),
        ],
        compiler_params=pltpu.CompilerParams(vmem_limit_bytes=40 << 20),
        cost_estimate=pl.CostEstimate(flops=cells * 8000, bytes_accessed=cells * 4, transcendentals=0),
        name="march",
    )(scalars, *pieces, *extras, left, right)


def local(probe_field, bounds, courant, snapshots, snap_times, basis_panels):
    probes_here, rows, cy, cz = probe_field.shape
    steps = snap_times.shape[0]
    half = probes_here // 2
    halo = 4 * (steps - 1)
    far = halo - rows
    devices = lax.axis_size("store")
    place = lax.axis_index("store")
    member = lax.axis_index("probe")
    members = lax.axis_size("probe")
    par = (place % 2).astype(jnp.int32)
    core = (member % 2).astype(jnp.int32)
    swap = [(i, i ^ 1) for i in range(devices)]
    perm_a = [(i, i - 2) for i in range(2, devices, 2)] + [(i, i + 2) for i in range(1, devices - 2, 2)]
    perm_b = [(i, i + 2) for i in range(0, devices - 2, 2)] + [(i, i - 2) for i in range(3, devices, 2)]
    hop = lambda x, pairs: lax.ppermute(x, "store", pairs)
    cores = lambda x: lax.ppermute(x, "probe", [(i, i ^ 1) for i in range(members)])
    cut = lambda x, start: lax.dynamic_slice_in_dim(x, start, far, axis=1)
    near = rows - far

    all_snaps = lax.all_gather(snapshots, "probe", axis=2, tiled=True)
    near_half, far_half = shares(steps, rows, halo)
    chosen = jnp.minimum(2 * jnp.arange(near_half) + core, steps - 1)
    picked = jnp.take(all_snaps, jnp.take(snap_times, chosen, mode="clip"), axis=0, mode="clip")
    high = lax.reduce_precision(courant, 8, 7)
    rate = jnp.where(core == 0, high, courant - high).astype(jnp.bfloat16)[None]
    extra = jnp.concatenate([picked, rate], axis=0)
    mine = lax.dynamic_slice_in_dim(probe_field, half * par, half, axis=0)
    theirs = lax.dynamic_slice_in_dim(probe_field, half * (1 - par), half, axis=0)
    partner = hop(theirs, swap)
    side_a = hop(mine, perm_a)
    side_b = hop(cut(mine, near * (1 - par)), perm_b)
    extra, side_a, side_b = lax.optimization_barrier((extra, side_a, side_b))
    extra_a = hop(extra, perm_a)
    tail = jnp.concatenate([extra[:far_half], extra[near_half:]], axis=0)
    extra_b = hop(cut(tail, near * (1 - par)), perm_b)
    planes = lambda x: x.reshape(-1, cy, cz)
    bundle = jnp.concatenate([planes(extra), planes(extra_a), planes(extra_b)], axis=0)
    bundle_x = hop(bundle, swap)
    extras = (bundle, bundle_x, cores(bundle), cores(bundle_x))
    pieces = (
        mine,
        partner,
        side_a,
        side_b,
        hop(partner, perm_b),
        hop(cut(partner, near * par), perm_a),
    )
    base = (place // 2) * 2 * rows - halo
    mine_bounds = lax.dynamic_slice_in_dim(bounds, half * par, half, axis=0) - base
    scalars = jnp.concatenate([jnp.stack([par, core]), mine_bounds.reshape(-1)]).astype(jnp.int32)
    first = par == 0
    own, back = [], []
    for begin, count in ((0, half // 2), (half // 2, half - half // 2)):
        kept, sent = propagate(scalars, pieces, extras, begin, count, steps, rows, halo)
        own.append(kept)
        back.append(hop(sent, swap))
    panels = [basis_panels]
    span = members // 2
    while span:
        pairs = [(i, i ^ span) for i in range(members)]
        panels = [y for x in panels for y in (x, lax.ppermute(x, "probe", pairs))]
        span //= 2
    panels = jnp.concatenate(panels, axis=0)
    dots = lambda x: lax.dot_general(
        panels, x, (((1, 2, 3), (1, 2, 3)), ((), ())), preferred_element_type=jnp.float32
    )
    own = jnp.concatenate(own, axis=0)
    mine_part = dots(own.astype(jnp.bfloat16))
    back = jnp.concatenate(back, axis=0)
    back_part = dots(back)
    back = back.astype(jnp.float32)
    response = jnp.concatenate([jnp.where(first, own, back), jnp.where(first, back, own)], axis=0)
    product = jnp.concatenate(
        [jnp.where(first, mine_part, back_part), jnp.where(first, back_part, mine_part)], axis=1
    )
    product = product.reshape(members, -1, probes_here)
    span = 1
    while span < members:
        swapped = product.reshape(-1, 2, span, *product.shape[1:])[:, ::-1].reshape(product.shape)
        product = jnp.where((member // span) % 2 == 1, swapped, product)
        span *= 2
    product = product.reshape(-1, probes_here)
    span = 1
    while span < devices:
        product = product + hop(product, [(i, i ^ span) for i in range(devices)])
        span *= 2
    return response, product


def solution(mesh):
    placed = (
        P("probe", "store", None, None),
        P("probe", None),
        P("store", None, None),
        P(None, "store", "probe", None),
        P(),
        P("probe", "store", None, None),
    )
    return jax.shard_map(
        local,
        mesh=mesh,
        in_specs=placed,
        out_specs=(P("probe", "store", None, None), P(None, "probe")),
        check_vma=False,
    )
```

```python
import functools

import jax
import jax.numpy as jnp
import numpy as np
from jax import lax
from jax.experimental import pallas as pl
from jax.experimental.pallas import tpu as pltpu
from jax.sharding import PartitionSpec as P

taps = (-205.0 / 72.0, 8.0 / 5.0, -1.0 / 5.0, 8.0 / 315.0, -1.0 / 560.0)
SPAN = 24
PACK = 2
AHEAD = 1


def tables(cells_y, cells_z):
    ratio = [0.0] + [t / taps[1] for t in taps[1:]]
    left = np.zeros((SPAN, cells_y, SPAN + 8, cells_y), np.float32)
    for i in range(SPAN):
        for d in range(1, 5):
            for y in range(cells_y):
                left[i, y, i + 4 + d, y] = ratio[d]
                left[i, y, i + 4 - d, y] = ratio[d]
                if y + d < cells_y:
                    left[i, y, i + 4, y + d] = ratio[d]
                if y - d >= 0:
                    left[i, y, i + 4, y - d] = ratio[d]
    right = np.zeros((cells_z, cells_z), np.float32)
    for z in range(cells_z):
        for d in range(1, 5):
            if z + d < cells_z:
                right[z, z + d] = ratio[d]
            if z - d >= 0:
                right[z, z - d] = ratio[d]
    left = left.reshape(SPAN * cells_y, (SPAN + 8) * cells_y)
    return left, np.concatenate([right, right], axis=0)


def spans(rows):
    out = []
    while rows > 0:
        out.append(min(SPAN, rows))
        rows -= out[-1]
    return out


def shares(steps, rows, halo):
    return (steps + 1) // 2, (-(-(halo - rows) // 4) + 1) // 2


def march(steps, rows, halo, begin, scalars, *refs):
    pieces = refs[0:6]
    near_ref, near_x_ref, other_ref, first_ref, second_ref = refs[6:11]
    left_ref, right_ref, own_ref, send_ref = refs[11:15]
    pert, snap, scale, gain, fields, split = refs[15:21]
    total = 2 * rows + 2 * halo
    cy = 8
    far = halo - rows
    par, core = scalars[0], scalars[1]
    probes = pieces[0].shape[0]
    even = (halo, halo + rows, halo + 2 * rows, 0, halo - rows, halo + 3 * rows)
    odd = (halo + rows, halo, halo - rows, halo + 3 * rows, halo + 2 * rows, 0)
    counts = (rows, rows, rows, far, rows, far)
    starts = [e + par * (o - e) for e, o in zip(even, odd)]
    near_half, far_half = shares(steps, rows, halo)

    @pl.when(pl.program_id(0) == 0)
    def _():
        sizes = [(near_half + 1) * rows, (near_half + 1) * rows, (far_half + 1) * far]
        for j in range(6):
            kept = far_half if j in (3, 5) else near_half
            where = pl.ds(pl.multiple_of(starts[j] * cy, 32), counts[j] * cy)
            for t in range(kept + 1):
                at = t * counts[j]
                if j == 0:
                    mine, other = near_ref[t], other_ref[t]
                else:
                    mine = near_x_ref[t] if j == 1 else pieces[j][probes + t]
                    held = first_ref if j < 4 else second_ref
                    at += sum(sizes[: j - 1]) if j < 4 else sum(sizes[1 : j - 3])
                    other = held[at : at + counts[j]]
                mine = mine.reshape(counts[j] * cy, 128).astype(jnp.float32)
                other = other.reshape(counts[j] * cy, 128).astype(jnp.float32)
                if t < kept:
                    snap[2 * t + core, where, :] = mine
                    snap[2 * t + 1 - core, where, :] = other
                else:
                    scale[where, :] = 2.0 + (3.0 * taps[0]) * (mine + other)
                    gain[where, :] = taps[1] * (mine + other)

    for q in range(PACK):
        probe = begin + pl.program_id(0) * PACK + q
        low = scalars[2 + 2 * probe]
        high = scalars[3 + 2 * probe]
        for j in range(6):
            where = pl.ds(pl.multiple_of(starts[j] * cy, 32), counts[j] * cy)
            value = pieces[j][probe].astype(jnp.float32)
            plane = lax.broadcasted_iota(jnp.int32, value.shape, 0) + starts[j]
            value = jnp.where((plane >= low) & (plane < high), value, 0.0)
            pert[q, where, :] = value.reshape(counts[j] * cy, 128)

    def keep(q, slot, where, value):
        high = value.astype(jnp.bfloat16)
        low = (value - high.astype(jnp.float32)).astype(jnp.bfloat16)
        split[q, slot, where, 0:128] = high
        split[q, slot, where, 128:256] = low

    at = 0
    for m in spans(total):
        where = pl.ds(at * cy, m * cy)
        for q in range(PACK):
            first = pert[q, where, :] * snap[0, where, :]
            fields[q, 0, where, :] = first
            keep(q, 0, where, first)
        at += m

    def slab(row, count):
        if isinstance(row, int):
            return pl.ds(row * cy, count * cy)
        return pl.ds(pl.multiple_of(row * cy, 32), count * cy)

    def products(q, n, row, m):
        now = (n + 1) % 2
        both = jnp.dot(
            left_ref[0 : m * cy, 0 : (m + 8) * cy],
            split[q, now, slab(row - 4, m + 8), :],
            preferred_element_type=jnp.float32,
        )
        along = jnp.dot(split[q, now, slab(row, m), :], right_ref[...], preferred_element_type=jnp.float32)
        return both, along

    def advanced(q, n, row, m, both, along):
        now, before = (n + 1) % 2, n % 2
        where = slab(row, m)
        total_taps = both[:, 0:128] + both[:, 128:256] + along
        value = scale[where, :] * fields[q, now, where, :] + gain[where, :] * total_taps
        value = value + pert[q, where, :] * snap[n, where, :]
        if n > 1:
            value = value - fields[q, before, where, :]
        if n < steps - 1:
            fields[q, before, where, :] = value
            keep(q, before, where, value)
        elif row is starts[0]:
            own_ref[pl.program_id(0) * PACK + q] = value.reshape(rows, cy, 128)
        else:
            send_ref[pl.program_id(0) * PACK + q] = value.reshape(rows, cy, 128).astype(jnp.bfloat16)

    items = []
    for n in range(1, steps - 1):
        at = 4 * n
        for m in spans(total - 8 * n):
            items += [(q, n, at, m) for q in range(PACK)]
            at += m
    for row in starts[0:2]:
        items += [(q, steps - 1, row, rows) for q in range(PACK)]
    queue = []
    for item in items:
        queue.append((item, products(*item)))
        if len(queue) > AHEAD:
            first, made = queue.pop(0)
            advanced(*first, *made)
    for first, made in queue:
        advanced(*first, *made)


def propagate(scalars, pieces, extras, begin, count, steps, rows, halo):
    _, _, cy, cz = pieces[0].shape
    left, right = tables(cy, cz)
    left, right = jnp.asarray(left, jnp.bfloat16), jnp.asarray(right, jnp.bfloat16)
    total = 2 * rows + 2 * halo
    whole = pl.BlockSpec(memory_space=pltpu.VMEM)
    grid_spec = pltpu.PrefetchScalarGridSpec(
        num_scalar_prefetch=1,
        grid=(count // PACK,),
        in_specs=[whole] * (len(pieces) + len(extras) + 2),
        out_specs=[whole, whole],
        scratch_shapes=[
            pltpu.VMEM((PACK, total * cy, cz), jnp.float32),
            pltpu.VMEM((steps + steps % 2, total * cy, cz), jnp.float32),
            pltpu.VMEM((total * cy, cz), jnp.float32),
            pltpu.VMEM((total * cy, cz), jnp.float32),
            pltpu.VMEM((PACK, 2, total * cy, cz), jnp.float32),
            pltpu.VMEM((PACK, 2, total * cy, 2 * cz), jnp.bfloat16),
        ],
    )
    cells = count * total * cy * cz
    return pl.pallas_call(
        functools.partial(march, steps, rows, halo, begin),
        grid_spec=grid_spec,
        out_shape=[
            jax.ShapeDtypeStruct((count, rows, cy, cz), jnp.float32),
            jax.ShapeDtypeStruct((count, rows, cy, cz), jnp.bfloat16),
        ],
        compiler_params=pltpu.CompilerParams(vmem_limit_bytes=20 << 20),
        cost_estimate=pl.CostEstimate(flops=cells * 8000, bytes_accessed=cells * 4, transcendentals=0),
        name="march",
    )(scalars, *pieces, *extras, left, right)


def local(probe_field, bounds, courant, snapshots, snap_times, basis_panels):
    probes_here, rows, cy, cz = probe_field.shape
    steps = snap_times.shape[0]
    half = probes_here // 2
    halo = 4 * (steps - 1)
    far = halo - rows
    devices = lax.axis_size("store")
    place = lax.axis_index("store")
    member = lax.axis_index("probe")
    members = lax.axis_size("probe")
    par = (place % 2).astype(jnp.int32)
    core = (member % 2).astype(jnp.int32)
    swap = [(i, i ^ 1) for i in range(devices)]
    perm_a = [(i, i - 2) for i in range(2, devices, 2)] + [(i, i + 2) for i in range(1, devices - 2, 2)]
    perm_b = [(i, i + 2) for i in range(0, devices - 2, 2)] + [(i, i - 2) for i in range(3, devices, 2)]
    hop = lambda x, pairs: lax.ppermute(x, "store", pairs)
    cores = lambda x: lax.ppermute(x, "probe", [(i, i ^ 1) for i in range(members)])
    cut = lambda x, start: lax.dynamic_slice_in_dim(x, start, far, axis=1)
    near = rows - far

    all_snaps = lax.all_gather(snapshots, "probe", axis=2, tiled=True)
    near_half, far_half = shares(steps, rows, halo)
    chosen = jnp.minimum(2 * jnp.arange(near_half) + core, steps - 1)
    picked = jnp.take(all_snaps, jnp.take(snap_times, chosen, mode="clip"), axis=0, mode="clip")
    high = lax.reduce_precision(courant, 8, 7)
    rate = jnp.where(core == 0, high, courant - high).astype(jnp.bfloat16)[None]
    extra = jnp.concatenate([picked, rate], axis=0)
    trim = lambda x: jnp.concatenate([x[:far_half], x[near_half:]], axis=0)
    planes = lambda *xs: jnp.concatenate([x.reshape(-1, cy, cz) for x in xs], axis=0)
    mine = lax.dynamic_slice_in_dim(probe_field, half * par, half, axis=0)
    theirs = lax.dynamic_slice_in_dim(probe_field, half * (1 - par), half, axis=0)
    partner = hop(theirs, swap)
    side_a = hop(jnp.concatenate([mine, extra], axis=0), perm_a)
    side_b = hop(cut(jnp.concatenate([mine, trim(extra)], axis=0), near * (1 - par)), perm_b)
    extra_x = hop(lax.optimization_barrier((extra, partner))[0], swap)
    side_c = hop(jnp.concatenate([partner, extra_x], axis=0), perm_b)
    side_d = hop(cut(jnp.concatenate([partner, trim(extra_x)], axis=0), near * par), perm_a)
    pieces = (mine, partner, side_a, side_b, side_c, side_d)
    extras = (
        extra,
        extra_x,
        cores(extra),
        cores(planes(extra_x, side_a[half:], side_b[half:])),
        cores(planes(side_c[half:], side_d[half:])),
    )
    base = (place // 2) * 2 * rows - halo
    mine_bounds = lax.dynamic_slice_in_dim(bounds, half * par, half, axis=0) - base
    scalars = jnp.concatenate([jnp.stack([par, core]), mine_bounds.reshape(-1)]).astype(jnp.int32)
    basis_later = lax.optimization_barrier((basis_panels, extra_x))[0]
    crossed = lax.ppermute(basis_later, "probe", [(i, i ^ 2) for i in range(members)])
    first = par == 0
    own, back = [], []
    for begin, count in ((0, half // 2), (half // 2, half - half // 2)):
        kept, sent = propagate(scalars, pieces, extras, begin, count, steps, rows, halo)
        own.append(kept)
        back.append(hop(sent, swap))
    panels = [basis_later, cores(basis_later)]
    crossed = lax.optimization_barrier((crossed, own[0]))[0]
    panels = [jnp.concatenate(panels, axis=0), jnp.concatenate([crossed, cores(crossed)], axis=0)]
    dots = lambda x: jnp.concatenate(
        [
            lax.dot_general(y, x, (((1, 2, 3), (1, 2, 3)), ((), ())), preferred_element_type=jnp.float32)
            for y in panels
        ],
        axis=0,
    )
    own = jnp.concatenate(own, axis=0)
    mine_part = dots(own.astype(jnp.bfloat16))
    back = jnp.concatenate(back, axis=0)
    back_part = dots(back)
    back = back.astype(jnp.float32)
    response = jnp.concatenate([jnp.where(first, own, back), jnp.where(first, back, own)], axis=0)
    product = jnp.concatenate(
        [jnp.where(first, mine_part, back_part), jnp.where(first, back_part, mine_part)], axis=1
    )
    product = product.reshape(members, -1, probes_here)
    span = 1
    while span < members:
        swapped = product.reshape(-1, 2, span, *product.shape[1:])[:, ::-1].reshape(product.shape)
        product = jnp.where((member // span) % 2 == 1, swapped, product)
        span *= 2
    product = product.reshape(-1, probes_here)
    span = 1
    while span < devices:
        product = product + hop(product, [(i, i ^ span) for i in range(devices)])
        span *= 2
    return response, product


def solution(mesh):
    placed = (
        P("probe", "store", None, None),
        P("probe", None),
        P("store", None, None),
        P(None, "store", "probe", None),
        P(),
        P("probe", "store", None, None),
    )
    return jax.shard_map(
        local,
        mesh=mesh,
        in_specs=placed,
        out_specs=(P("probe", "store", None, None), P(None, "probe")),
        check_vma=False,
    )
```

```python
import functools

import jax
import jax.numpy as jnp
import numpy as np
from jax import lax
from jax.experimental import pallas as pl
from jax.experimental.pallas import tpu as pltpu
from jax.sharding import PartitionSpec as P

taps = (-205.0 / 72.0, 8.0 / 5.0, -1.0 / 5.0, 8.0 / 315.0, -1.0 / 560.0)
SPAN = 24
PACK = 2
AHEAD = 1


def tables(cells_y, cells_z):
    ratio = [0.0] + [t / taps[1] for t in taps[1:]]
    left = np.zeros((SPAN, cells_y, SPAN + 8, cells_y), np.float32)
    for i in range(SPAN):
        for d in range(1, 5):
            for y in range(cells_y):
                left[i, y, i + 4 + d, y] = ratio[d]
                left[i, y, i + 4 - d, y] = ratio[d]
                if y + d < cells_y:
                    left[i, y, i + 4, y + d] = ratio[d]
                if y - d >= 0:
                    left[i, y, i + 4, y - d] = ratio[d]
    right = np.zeros((cells_z, cells_z), np.float32)
    for z in range(cells_z):
        for d in range(1, 5):
            if z + d < cells_z:
                right[z, z + d] = ratio[d]
            if z - d >= 0:
                right[z, z - d] = ratio[d]
    left = left.reshape(SPAN * cells_y, (SPAN + 8) * cells_y)
    return left, np.concatenate([right, right], axis=0)


def spans(rows):
    out = []
    while rows > 0:
        out.append(min(SPAN, rows))
        rows -= out[-1]
    return out


def shares(steps, rows, halo):
    return (steps + 1) // 2, (-(-(halo - rows) // 4) + 1) // 2


def march(steps, rows, halo, begin, scalars, *refs):
    wide, narrow = refs[0:4], refs[4:6]
    near_refs = refs[6:8]
    c_ref, d_ref, near_other, far_other = refs[8:12]
    left_ref, right_ref, own_ref, send_ref = refs[12:16]
    pert, snap, scale, gain, fields, split = refs[16:22]
    total = 2 * rows + 2 * halo
    cy = 8
    far = halo - rows
    par, core = scalars[0], scalars[1]
    even = (halo, halo + rows, halo + 2 * rows, 0, halo - rows, halo + 3 * rows)
    odd = (halo + rows, halo, halo - rows, halo + 3 * rows, halo + 2 * rows, 0)
    counts = (rows, rows, rows, far, rows, far)
    starts = [e + par * (o - e) for e, o in zip(even, odd)]
    near_half, far_half = shares(steps, rows, halo)

    @pl.when(pl.program_id(0) == 0)
    def _():
        near_size, far_size = (near_half + 1) * rows, (far_half + 1) * far
        c_base = c_ref.shape[0] - near_size - far_size
        d_base = d_ref.shape[0] - near_size - far_size
        held = (
            (d_ref, d_base, near_size + far_size),
            (c_ref, c_base + near_size, near_size),
            (c_ref, c_base, 0),
            (d_ref, d_base + near_size, 2 * near_size + far_size),
        )
        for j in range(6):
            kept = far_half if j in (3, 5) else near_half
            where = pl.ds(pl.multiple_of(starts[j] * cy, 32), counts[j] * cy)
            for t in range(kept + 1):
                at = t * counts[j]
                if j < 2:
                    mine = near_refs[j][t]
                    at += j * near_size
                    other = near_other[at : at + counts[j]]
                else:
                    source, first, second = held[j - 2]
                    mine = source[first + at : first + at + counts[j]]
                    other = far_other[second + at : second + at + counts[j]]
                mine = mine.reshape(counts[j] * cy, 128).astype(jnp.float32)
                other = other.reshape(counts[j] * cy, 128).astype(jnp.float32)
                if t < kept:
                    snap[2 * t + core, where, :] = mine
                    snap[2 * t + 1 - core, where, :] = other
                else:
                    scale[where, :] = 2.0 + (3.0 * taps[0]) * (mine + other)
                    gain[where, :] = taps[1] * (mine + other)

    for q in range(PACK):
        place = pl.program_id(0) * PACK + q
        probe = begin + place
        low = scalars[2 + 2 * probe]
        high = scalars[3 + 2 * probe]
        for j in range(6):
            where = pl.ds(pl.multiple_of(starts[j] * cy, 32), counts[j] * cy)
            if j < 4:
                value = wide[j][probe].astype(jnp.float32)
            else:
                value = narrow[j - 4][pl.ds(place * counts[j], counts[j])].astype(jnp.float32)
            plane = lax.broadcasted_iota(jnp.int32, value.shape, 0) + starts[j]
            value = jnp.where((plane >= low) & (plane < high), value, 0.0)
            pert[q, where, :] = value.reshape(counts[j] * cy, 128)

    def keep(q, slot, where, value):
        high = value.astype(jnp.bfloat16)
        low = (value - high.astype(jnp.float32)).astype(jnp.bfloat16)
        split[q, slot, where, 0:128] = high
        split[q, slot, where, 128:256] = low

    at = 0
    for m in spans(total):
        where = pl.ds(at * cy, m * cy)
        for q in range(PACK):
            first = pert[q, where, :] * snap[0, where, :]
            fields[q, 0, where, :] = first
            keep(q, 0, where, first)
        at += m

    def slab(row, count):
        if isinstance(row, int):
            return pl.ds(row * cy, count * cy)
        return pl.ds(pl.multiple_of(row * cy, 32), count * cy)

    def products(q, n, row, m):
        now = (n + 1) % 2
        both = jnp.dot(
            left_ref[0 : m * cy, 0 : (m + 8) * cy],
            split[q, now, slab(row - 4, m + 8), :],
            preferred_element_type=jnp.float32,
        )
        along = jnp.dot(split[q, now, slab(row, m), :], right_ref[...], preferred_element_type=jnp.float32)
        return both, along

    def advanced(q, n, row, m, both, along):
        now, before = (n + 1) % 2, n % 2
        where = slab(row, m)
        total_taps = both[:, 0:128] + both[:, 128:256] + along
        value = scale[where, :] * fields[q, now, where, :] + gain[where, :] * total_taps
        value = value + pert[q, where, :] * snap[n, where, :]
        if n > 1:
            value = value - fields[q, before, where, :]
        if n < steps - 1:
            fields[q, before, where, :] = value
            keep(q, before, where, value)
        elif row is starts[0]:
            own_ref[pl.program_id(0) * PACK + q] = value.reshape(rows, cy, 128)
        else:
            send_ref[pl.program_id(0) * PACK + q] = value.reshape(rows, cy, 128).astype(jnp.bfloat16)

    items = []
    for n in range(1, steps - 1):
        at = 4 * n
        for m in spans(total - 8 * n):
            items += [(q, n, at, m) for q in range(PACK)]
            at += m
    for row in starts[0:2]:
        items += [(q, steps - 1, row, rows) for q in range(PACK)]
    queue = []
    for item in items:
        queue.append((item, products(*item)))
        if len(queue) > AHEAD:
            first, made = queue.pop(0)
            advanced(*first, *made)
    for first, made in queue:
        advanced(*first, *made)


def propagate(scalars, operands, begin, count, steps, rows, halo):
    _, _, cy, cz = operands[0].shape
    left, right = tables(cy, cz)
    left, right = jnp.asarray(left, jnp.bfloat16), jnp.asarray(right, jnp.bfloat16)
    total = 2 * rows + 2 * halo
    whole = pl.BlockSpec(memory_space=pltpu.VMEM)
    grid_spec = pltpu.PrefetchScalarGridSpec(
        num_scalar_prefetch=1,
        grid=(count // PACK,),
        in_specs=[whole] * (len(operands) + 2),
        out_specs=[whole, whole],
        scratch_shapes=[
            pltpu.VMEM((PACK, total * cy, cz), jnp.float32),
            pltpu.VMEM((steps + steps % 2, total * cy, cz), jnp.float32),
            pltpu.VMEM((total * cy, cz), jnp.float32),
            pltpu.VMEM((total * cy, cz), jnp.float32),
            pltpu.VMEM((PACK, 2, total * cy, cz), jnp.float32),
            pltpu.VMEM((PACK, 2, total * cy, 2 * cz), jnp.bfloat16),
        ],
    )
    cells = count * total * cy * cz
    return pl.pallas_call(
        functools.partial(march, steps, rows, halo, begin),
        grid_spec=grid_spec,
        out_shape=[
            jax.ShapeDtypeStruct((count, rows, cy, cz), jnp.float32),
            jax.ShapeDtypeStruct((count, rows, cy, cz), jnp.bfloat16),
        ],
        compiler_params=pltpu.CompilerParams(vmem_limit_bytes=20 << 20),
        cost_estimate=pl.CostEstimate(flops=cells * 8000 if begin else 0, bytes_accessed=cells * 4 if begin else 0, transcendentals=0),
        name="march",
    )(scalars, *operands, left, right)


def local(probe_field, bounds, courant, snapshots, snap_times, basis_panels):
    probes_here, rows, cy, cz = probe_field.shape
    steps = snap_times.shape[0]
    half = probes_here // 2
    halo = 4 * (steps - 1)
    far = halo - rows
    devices = lax.axis_size("store")
    place = lax.axis_index("store")
    member = lax.axis_index("probe")
    members = lax.axis_size("probe")
    par = (place % 2).astype(jnp.int32)
    core = (member % 2).astype(jnp.int32)
    swap = [(i, i ^ 1) for i in range(devices)]
    perm_a = [(i, i - 2) for i in range(2, devices, 2)] + [(i, i + 2) for i in range(1, devices - 2, 2)]
    perm_b = [(i, i + 2) for i in range(0, devices - 2, 2)] + [(i, i - 2) for i in range(3, devices, 2)]
    hop = lambda x, pairs: lax.ppermute(x, "store", pairs)
    cores = lambda x: lax.ppermute(x, "probe", [(i, i ^ 1) for i in range(members)])
    cut = lambda x, start: lax.dynamic_slice_in_dim(x, start, far, axis=1)
    near = rows - far

    mine = lax.dynamic_slice_in_dim(probe_field, half * par, half, axis=0)
    theirs = lax.dynamic_slice_in_dim(probe_field, half * (1 - par), half, axis=0)
    partner = hop(theirs, swap)
    side_a = hop(mine, perm_a)
    side_b = hop(cut(mine, near * (1 - par)), perm_b)

    near_half, far_half = shares(steps, rows, halo)

    def picked(parity):
        chosen = jnp.minimum(2 * jnp.arange(near_half) + parity, steps - 1)
        return jnp.take(snapshots, jnp.take(snap_times, chosen, mode="clip"), axis=0, mode="clip")

    joined = picked(core)
    sent = picked(1 - core)
    span = 1
    while span < members:
        got = lax.ppermute(sent, "probe", [(i, i ^ span) for i in range(members)])
        upper = (member // span) % 2 == 1
        joined = jnp.concatenate([jnp.where(upper, got, joined), jnp.where(upper, joined, got)], axis=2)
        sent = joined
        span *= 2
    high = lax.reduce_precision(courant, 8, 7)
    rate = jnp.where(core == 0, high, courant - high).astype(jnp.bfloat16)[None]
    extra = jnp.concatenate([joined, rate], axis=0)
    trim = lambda x: jnp.concatenate([x[:far_half], x[near_half:]], axis=0)
    planes = lambda *xs: jnp.concatenate([x.reshape(-1, cy, cz) for x in xs], axis=0)
    extra_x = hop(lax.optimization_barrier((extra, partner, side_a, side_b))[0], swap)
    part = half // 2
    far_own, far_x = cut(trim(extra), near * (1 - par)), cut(trim(extra_x), near * par)
    far_partner = cut(partner, near * par)
    side_c = [hop(planes(partner[:part], extra_x, far_own), perm_b), hop(planes(partner[part:]), perm_b)]
    side_d = [hop(planes(far_partner[:part], extra, far_x), perm_a), hop(planes(far_partner[part:]), perm_a)]
    near_other = cores(planes(extra, extra_x))
    far_other = cores(planes(side_c[0][part * rows :], side_d[0][part * far :]))
    base = (place // 2) * 2 * rows - halo
    mine_bounds = lax.dynamic_slice_in_dim(bounds, half * par, half, axis=0) - base
    scalars = jnp.concatenate([jnp.stack([par, core]), mine_bounds.reshape(-1)]).astype(jnp.int32)
    crossed = lax.ppermute(basis_panels, "probe", [(i, i ^ 2) for i in range(members)])
    first = par == 0
    own, back = [], []
    for i in range(2):
        operands = (mine, partner, side_a, side_b, side_c[i], side_d[i], extra, extra_x)
        operands += (side_c[0], side_d[0], near_other, far_other)
        kept, sent = propagate(scalars, operands, i * part, part, steps, rows, halo)
        scalars = lax.optimization_barrier((scalars, kept))[0]
        own.append(kept)
        if back:
            sent = lax.optimization_barrier((sent, back[0]))[0]
        back.append(hop(sent, swap))
    beside = cores(basis_panels)
    crossed, beside = lax.optimization_barrier((crossed, beside, own[1]))[:2]
    panels = [basis_panels, beside, crossed, cores(crossed)]
    dots = lambda x: jnp.concatenate(
        [
            lax.dot_general(y, x, (((1, 2, 3), (1, 2, 3)), ((), ())), preferred_element_type=jnp.float32)
            for y in panels
        ],
        axis=0,
    )
    own = jnp.concatenate(own, axis=0)
    mine_part = dots(own.astype(jnp.bfloat16))
    back = jnp.concatenate(back, axis=0)
    back_part = dots(back)
    back = back.astype(jnp.float32)
    response = jnp.concatenate([jnp.where(first, own, back), jnp.where(first, back, own)], axis=0)
    product = jnp.concatenate(
        [jnp.where(first, mine_part, back_part), jnp.where(first, back_part, mine_part)], axis=1
    )
    product = product.reshape(members, -1, probes_here)
    span = 1
    while span < members:
        swapped = product.reshape(-1, 2, span, *product.shape[1:])[:, ::-1].reshape(product.shape)
        product = jnp.where((member // span) % 2 == 1, swapped, product)
        span *= 2
    product = product.reshape(-1, probes_here)
    span = 1
    while span < devices:
        product = product + hop(product, [(i, i ^ span) for i in range(devices)])
        span *= 2
    return response, product


def solution(mesh):
    placed = (
        P("probe", "store", None, None),
        P("probe", None),
        P("store", None, None),
        P(None, "store", "probe", None),
        P(),
        P("probe", "store", None, None),
    )
    return jax.shard_map(
        local,
        mesh=mesh,
        in_specs=placed,
        out_specs=(P("probe", "store", None, None), P(None, "probe")),
        check_vma=False,
    )
```

```python
import functools

import jax
import jax.numpy as jnp
import numpy as np
from jax import lax
from jax.experimental import pallas as pl
from jax.experimental.pallas import tpu as pltpu
from jax.sharding import PartitionSpec as P

taps = (-205.0 / 72.0, 8.0 / 5.0, -1.0 / 5.0, 8.0 / 315.0, -1.0 / 560.0)
SPAN = 24
PACK = 2
AHEAD = 1


def tables(cells_y, cells_z):
    ratio = [0.0] + [t / taps[1] for t in taps[1:]]
    left = np.zeros((SPAN, cells_y, SPAN + 8, cells_y), np.float32)
    for i in range(SPAN):
        for d in range(1, 5):
            for y in range(cells_y):
                left[i, y, i + 4 + d, y] = ratio[d]
                left[i, y, i + 4 - d, y] = ratio[d]
                if y + d < cells_y:
                    left[i, y, i + 4, y + d] = ratio[d]
                if y - d >= 0:
                    left[i, y, i + 4, y - d] = ratio[d]
    right = np.zeros((cells_z, cells_z), np.float32)
    for z in range(cells_z):
        for d in range(1, 5):
            if z + d < cells_z:
                right[z, z + d] = ratio[d]
            if z - d >= 0:
                right[z, z - d] = ratio[d]
    left = left.reshape(SPAN * cells_y, (SPAN + 8) * cells_y)
    return left, np.concatenate([right, right], axis=0)


def spans(rows):
    out = []
    while rows > 0:
        out.append(min(SPAN, rows))
        rows -= out[-1]
    return out


def shares(steps, rows, halo):
    return (steps + 1) // 2, (-(-(halo - rows) // 4) + 1) // 2


def march(steps, rows, halo, begin, bounds_ref, *refs):
    pieces = refs[0:6]
    near_ref, near_x_ref, other_ref, first_ref, second_ref = refs[6:11]
    left_ref, right_ref, own_ref, send_ref = refs[11:15]
    pert, snap, scale, gain, fields, split = refs[15:21]
    total = 2 * rows + 2 * halo
    cy = 8
    far = halo - rows
    place = lax.axis_index("store")
    par, core = place % 2, lax.axis_index("probe") % 2
    base = (place // 2) * 2 * rows - halo
    probes = pieces[0].shape[0]
    even = (halo, halo + rows, halo + 2 * rows, 0, halo - rows, halo + 3 * rows)
    odd = (halo + rows, halo, halo - rows, halo + 3 * rows, halo + 2 * rows, 0)
    counts = (rows, rows, rows, far, rows, far)
    starts = [e + par * (o - e) for e, o in zip(even, odd)]
    near_half, far_half = shares(steps, rows, halo)

    @pl.when(pl.program_id(0) == 0)
    def _():
        sizes = [(near_half + 1) * rows, (near_half + 1) * rows, (far_half + 1) * far]
        for j in range(6):
            kept = far_half if j in (3, 5) else near_half
            where = pl.ds(pl.multiple_of(starts[j] * cy, 32), counts[j] * cy)
            for t in range(kept + 1):
                at = t * counts[j]
                if j == 0:
                    mine, other = near_ref[t], other_ref[t]
                else:
                    mine = near_x_ref[t] if j == 1 else pieces[j][probes + t]
                    held = first_ref if j < 4 else second_ref
                    at += sum(sizes[: j - 1]) if j < 4 else sum(sizes[1 : j - 3])
                    other = held[at : at + counts[j]]
                mine = mine.reshape(counts[j] * cy, 128).astype(jnp.float32)
                other = other.reshape(counts[j] * cy, 128).astype(jnp.float32)
                if t < kept:
                    snap[2 * t + core, where, :] = mine
                    snap[2 * t + 1 - core, where, :] = other
                else:
                    scale[where, :] = 2.0 + (3.0 * taps[0]) * (mine + other)
                    gain[where, :] = taps[1] * (mine + other)

    for q in range(PACK):
        probe = begin + pl.program_id(0) * PACK + q
        low = bounds_ref[probes * par + probe, 0] - base
        high = bounds_ref[probes * par + probe, 1] - base
        for j in range(6):
            where = pl.ds(pl.multiple_of(starts[j] * cy, 32), counts[j] * cy)
            value = pieces[j][probe].astype(jnp.float32)
            plane = lax.broadcasted_iota(jnp.int32, value.shape, 0) + starts[j]
            value = jnp.where((plane >= low) & (plane < high), value, 0.0)
            pert[q, where, :] = value.reshape(counts[j] * cy, 128)

    def keep(q, slot, where, value):
        high = value.astype(jnp.bfloat16)
        low = (value - high.astype(jnp.float32)).astype(jnp.bfloat16)
        split[q, slot, where, 0:128] = high
        split[q, slot, where, 128:256] = low

    at = 0
    for m in spans(total):
        where = pl.ds(at * cy, m * cy)
        for q in range(PACK):
            first = pert[q, where, :] * snap[0, where, :]
            fields[q, 0, where, :] = first
            keep(q, 0, where, first)
        at += m

    def slab(row, count):
        if isinstance(row, int):
            return pl.ds(row * cy, count * cy)
        return pl.ds(pl.multiple_of(row * cy, 32), count * cy)

    def products(q, n, row, m):
        now = (n + 1) % 2
        both = jnp.dot(
            left_ref[0 : m * cy, 0 : (m + 8) * cy],
            split[q, now, slab(row - 4, m + 8), :],
            preferred_element_type=jnp.float32,
        )
        along = jnp.dot(split[q, now, slab(row, m), :], right_ref[...], preferred_element_type=jnp.float32)
        return both, along

    def advanced(q, n, row, m, both, along):
        now, before = (n + 1) % 2, n % 2
        where = slab(row, m)
        total_taps = both[:, 0:128] + both[:, 128:256] + along
        value = scale[where, :] * fields[q, now, where, :] + gain[where, :] * total_taps
        value = value + pert[q, where, :] * snap[n, where, :]
        if n > 1:
            value = value - fields[q, before, where, :]
        if n < steps - 1:
            fields[q, before, where, :] = value
            keep(q, before, where, value)
        elif row is starts[0]:
            own_ref[pl.program_id(0) * PACK + q] = value.reshape(rows, cy, 128)
        else:
            send_ref[pl.program_id(0) * PACK + q] = value.reshape(rows, cy, 128).astype(jnp.bfloat16)

    items = []
    for n in range(1, steps - 1):
        at = 4 * n
        for m in spans(total - 8 * n):
            items += [(q, n, at, m) for q in range(PACK)]
            at += m
    for row in starts[0:2]:
        items += [(q, steps - 1, row, rows) for q in range(PACK)]
    queue = []
    for item in items:
        queue.append((item, products(*item)))
        if len(queue) > AHEAD:
            first, made = queue.pop(0)
            advanced(*first, *made)
    for first, made in queue:
        advanced(*first, *made)


def propagate(bounds, pieces, extras, begin, count, steps, rows, halo):
    _, _, cy, cz = pieces[0].shape
    left, right = tables(cy, cz)
    left, right = jnp.asarray(left, jnp.bfloat16), jnp.asarray(right, jnp.bfloat16)
    total = 2 * rows + 2 * halo
    whole = pl.BlockSpec(memory_space=pltpu.VMEM)
    grid_spec = pltpu.PrefetchScalarGridSpec(
        num_scalar_prefetch=1,
        grid=(count // PACK,),
        in_specs=[whole] * (len(pieces) + len(extras) + 2),
        out_specs=[whole, whole],
        scratch_shapes=[
            pltpu.VMEM((PACK, total * cy, cz), jnp.float32),
            pltpu.VMEM((steps + steps % 2, total * cy, cz), jnp.float32),
            pltpu.VMEM((total * cy, cz), jnp.float32),
            pltpu.VMEM((total * cy, cz), jnp.float32),
            pltpu.VMEM((PACK, 2, total * cy, cz), jnp.float32),
            pltpu.VMEM((PACK, 2, total * cy, 2 * cz), jnp.bfloat16),
        ],
    )
    cells = count * total * cy * cz
    return pl.pallas_call(
        functools.partial(march, steps, rows, halo, begin),
        grid_spec=grid_spec,
        out_shape=[
            jax.ShapeDtypeStruct((count, rows, cy, cz), jnp.float32),
            jax.ShapeDtypeStruct((count, rows, cy, cz), jnp.bfloat16),
        ],
        compiler_params=pltpu.CompilerParams(vmem_limit_bytes=20 << 20),
        cost_estimate=pl.CostEstimate(flops=cells * 8000, bytes_accessed=cells * 4, transcendentals=0),
        name="march",
    )(bounds, *pieces, *extras, left, right)


def local(probe_field, bounds, courant, snapshots, snap_times, basis_panels):
    probes_here, rows, cy, cz = probe_field.shape
    steps = snap_times.shape[0]
    half = probes_here // 2
    halo = 4 * (steps - 1)
    far = halo - rows
    devices = lax.axis_size("store")
    place = lax.axis_index("store")
    member = lax.axis_index("probe")
    members = lax.axis_size("probe")
    par = (place % 2).astype(jnp.int32)
    core = (member % 2).astype(jnp.int32)
    swap = [(i, i ^ 1) for i in range(devices)]
    perm_a = [(i, i - 2) for i in range(2, devices, 2)] + [(i, i + 2) for i in range(1, devices - 2, 2)]
    perm_b = [(i, i + 2) for i in range(0, devices - 2, 2)] + [(i, i - 2) for i in range(3, devices, 2)]
    hop = lambda x, pairs: lax.ppermute(x, "store", pairs)
    cores = lambda x: lax.ppermute(x, "probe", [(i, i ^ 1) for i in range(members)])
    cut = lambda x, start: lax.dynamic_slice_in_dim(x, start, far, axis=1)
    near = rows - far

    all_snaps = lax.all_gather(snapshots, "probe", axis=2, tiled=True)
    near_half, far_half = shares(steps, rows, halo)
    chosen = jnp.minimum(2 * jnp.arange(near_half) + core, steps - 1)
    picked = jnp.take(all_snaps, jnp.take(snap_times, chosen, mode="clip"), axis=0, mode="clip")
    high = lax.reduce_precision(courant, 8, 7)
    rate = jnp.where(core == 0, high, courant - high).astype(jnp.bfloat16)[None]
    extra = jnp.concatenate([picked, rate], axis=0)
    trim = lambda x: jnp.concatenate([x[:far_half], x[near_half:]], axis=0)
    planes = lambda *xs: jnp.concatenate([x.reshape(-1, cy, cz) for x in xs], axis=0)
    mine = lax.dynamic_slice_in_dim(probe_field, half * par, half, axis=0)
    theirs = lax.dynamic_slice_in_dim(probe_field, half * (1 - par), half, axis=0)
    partner = hop(theirs, swap)
    side_a = hop(jnp.concatenate([mine, extra], axis=0), perm_a)
    side_b = hop(cut(jnp.concatenate([mine, trim(extra)], axis=0), near * (1 - par)), perm_b)
    extra_x = hop(lax.optimization_barrier((extra, partner))[0], swap)
    side_c = hop(jnp.concatenate([partner, extra_x], axis=0), perm_b)
    side_d = hop(cut(jnp.concatenate([partner, trim(extra_x)], axis=0), near * par), perm_a)
    pieces = (mine, partner, side_a, side_b, side_c, side_d)
    extras = (
        extra,
        extra_x,
        cores(extra),
        cores(planes(extra_x, side_a[half:], side_b[half:])),
        cores(planes(side_c[half:], side_d[half:])),
    )
    basis_later = basis_panels
    crossed = lax.ppermute(basis_later, "probe", [(i, i ^ 2) for i in range(members)])
    first = par == 0
    own, back = [], []
    for begin, count in ((0, half // 2), (half // 2, half - half // 2)):
        kept, sent = propagate(bounds, pieces, extras, begin, count, steps, rows, halo)
        bounds = lax.optimization_barrier((bounds, kept))[0]
        if back:
            sent = lax.optimization_barrier((sent, back[0]))[0]
        own.append(kept)
        back.append(hop(sent, swap))
    panels = [basis_later, cores(basis_later)]
    crossed = lax.optimization_barrier((crossed, own[0]))[0]
    panels = [jnp.concatenate(panels, axis=0), jnp.concatenate([crossed, cores(crossed)], axis=0)]
    dots = lambda x: jnp.concatenate(
        [
            lax.dot_general(y, x, (((1, 2, 3), (1, 2, 3)), ((), ())), preferred_element_type=jnp.float32)
            for y in panels
        ],
        axis=0,
    )
    own = jnp.concatenate(own, axis=0)
    mine_part = dots(own.astype(jnp.bfloat16))
    back = jnp.concatenate(back, axis=0)
    back_part = dots(back)
    back = back.astype(jnp.float32)
    response = jnp.concatenate([jnp.where(first, own, back), jnp.where(first, back, own)], axis=0)
    product = jnp.concatenate(
        [jnp.where(first, mine_part, back_part), jnp.where(first, back_part, mine_part)], axis=1
    )
    product = product.reshape(members, -1, probes_here)
    span = 1
    while span < members:
        swapped = product.reshape(-1, 2, span, *product.shape[1:])[:, ::-1].reshape(product.shape)
        product = jnp.where((member // span) % 2 == 1, swapped, product)
        span *= 2
    product = product.reshape(-1, probes_here)
    span = 1
    while span < devices:
        product = product + hop(product, [(i, i ^ span) for i in range(devices)])
        span *= 2
    return response, product


def solution(mesh):
    placed = (
        P("probe", "store", None, None),
        P("probe", None),
        P("store", None, None),
        P(None, "store", "probe", None),
        P(),
        P("probe", "store", None, None),
    )
    return jax.shard_map(
        local,
        mesh=mesh,
        in_specs=placed,
        out_specs=(P("probe", "store", None, None), P(None, "probe")),
        check_vma=False,
    )
```

```python
import functools

import jax
import jax.numpy as jnp
import numpy as np
from jax import lax
from jax.experimental import pallas as pl
from jax.experimental.pallas import tpu as pltpu
from jax.sharding import PartitionSpec as P

taps = (-205.0 / 72.0, 8.0 / 5.0, -1.0 / 5.0, 8.0 / 315.0, -1.0 / 560.0)
SPAN = 24
PACK = 2
AHEAD = 1


def tables(cells_y, cells_z):
    def banded(apart, allowed):
        out = jnp.zeros(apart.shape, jnp.float32)
        for d in range(1, 5):
            out = jnp.where(allowed & (apart == d), taps[d] / taps[1], out)
        return out

    shape = (SPAN * cells_y, (SPAN + 8) * cells_y)
    row = lax.broadcasted_iota(jnp.int32, shape, 0)
    column = lax.broadcasted_iota(jnp.int32, shape, 1)
    planes = jnp.abs(column // cells_y - 4 - row // cells_y)
    lines = jnp.abs(column % cells_y - row % cells_y)
    left = banded(planes, lines == 0) + banded(lines, planes == 0)
    shape = (2 * cells_z, cells_z)
    row = lax.broadcasted_iota(jnp.int32, shape, 0) % cells_z
    apart = jnp.abs(row - lax.broadcasted_iota(jnp.int32, shape, 1))
    right = banded(apart, apart > 0)
    return left.astype(jnp.bfloat16), right.astype(jnp.bfloat16)


def spans(rows):
    out = []
    while rows > 0:
        out.append(min(SPAN, rows))
        rows -= out[-1]
    return out


def shares(steps, rows, halo):
    return (steps + 1) // 2, (-(-(halo - rows) // 4) + 1) // 2


def march(steps, rows, halo, begin, bounds_ref, *refs):
    wide, narrow = refs[0:4], refs[4:6]
    c_ref, d_ref = narrow
    near_refs = refs[6:8]
    near_other, far_other, own_ref, send_ref = refs[8:12]
    pert, snap, scale, gain, fields, split, left_ref, right_ref, a_buf, b_buf, sems = refs[12:23]
    count = a_buf.shape[0]
    fetch = [
        pltpu.make_async_copy(wide[j].at[pl.ds(begin, count)], buf, sems.at[j - 2])
        for j, buf in ((2, a_buf), (3, b_buf))
    ]
    total = 2 * rows + 2 * halo
    cy = 8
    far = halo - rows
    place = lax.axis_index("store")
    par, core = place % 2, lax.axis_index("probe") % 2
    base = (place // 2) * 2 * rows - halo
    probes = wide[0].shape[0]
    even = (halo, halo + rows, halo + 2 * rows, 0, halo - rows, halo + 3 * rows)
    odd = (halo + rows, halo, halo - rows, halo + 3 * rows, halo + 2 * rows, 0)
    counts = (rows, rows, rows, far, rows, far)
    starts = [e + par * (o - e) for e, o in zip(even, odd)]
    near_half, far_half = shares(steps, rows, halo)

    @pl.when(pl.program_id(0) == 0)
    def _():
        for copy in fetch:
            copy.start()
        left_ref[...], right_ref[...] = tables(cy, 128)
        near_size, far_size = (near_half + 1) * rows, (far_half + 1) * far
        c_base = c_ref.shape[0] - near_size - far_size
        d_base = d_ref.shape[0] - near_size - far_size
        held = (
            (d_ref, d_base, near_size + far_size),
            (c_ref, c_base + near_size, near_size),
            (c_ref, c_base, 0),
            (d_ref, d_base + near_size, 2 * near_size + far_size),
        )
        for j in range(6):
            kept = far_half if j in (3, 5) else near_half
            where = pl.ds(pl.multiple_of(starts[j] * cy, 32), counts[j] * cy)
            for t in range(kept + 1):
                at = t * counts[j]
                if j < 2:
                    mine = near_refs[j][t]
                    at += j * near_size
                    other = near_other[at : at + counts[j]]
                else:
                    source, first, second = held[j - 2]
                    mine = source[first + at : first + at + counts[j]]
                    other = far_other[second + at : second + at + counts[j]]
                mine = mine.reshape(counts[j] * cy, 128).astype(jnp.float32)
                other = other.reshape(counts[j] * cy, 128).astype(jnp.float32)
                if t < kept:
                    snap[2 * t + core, where, :] = mine
                    snap[2 * t + 1 - core, where, :] = other
                else:
                    scale[where, :] = 2.0 + (3.0 * taps[0]) * (mine + other)
                    gain[where, :] = taps[1] * (mine + other)

        for copy in fetch:
            copy.wait()

    for q in range(PACK):
        probe = begin + pl.program_id(0) * PACK + q
        low = bounds_ref[probes * par + probe, 0] - base
        high = bounds_ref[probes * par + probe, 1] - base
        for j in range(6):
            where = pl.ds(pl.multiple_of(starts[j] * cy, 32), counts[j] * cy)
            if j < 2:
                value = wide[j][probe].astype(jnp.float32)
            elif j < 4:
                value = (a_buf, b_buf)[j - 2][probe - begin].astype(jnp.float32)
            else:
                value = narrow[j - 4][pl.ds(probe * counts[j], counts[j])].astype(jnp.float32)
            plane = lax.broadcasted_iota(jnp.int32, value.shape, 0) + starts[j]
            value = jnp.where((plane >= low) & (plane < high), value, 0.0)
            pert[q, where, :] = value.reshape(counts[j] * cy, 128)

    def keep(q, slot, where, value):
        high = value.astype(jnp.bfloat16)
        low = (value - high.astype(jnp.float32)).astype(jnp.bfloat16)
        split[q, slot, where, 0:128] = high
        split[q, slot, where, 128:256] = low

    at = 0
    for m in spans(total):
        where = pl.ds(at * cy, m * cy)
        for q in range(PACK):
            first = pert[q, where, :] * snap[0, where, :]
            fields[q, 0, where, :] = first
            keep(q, 0, where, first)
        at += m

    def slab(row, count):
        if isinstance(row, int):
            return pl.ds(row * cy, count * cy)
        return pl.ds(pl.multiple_of(row * cy, 32), count * cy)

    def products(q, n, row, m):
        now = (n + 1) % 2
        both = jnp.dot(
            left_ref[0 : m * cy, 0 : (m + 8) * cy],
            split[q, now, slab(row - 4, m + 8), :],
            preferred_element_type=jnp.float32,
        )
        along = jnp.dot(split[q, now, slab(row, m), :], right_ref[...], preferred_element_type=jnp.float32)
        return both, along

    def advanced(q, n, row, m, both, along):
        now, before = (n + 1) % 2, n % 2
        where = slab(row, m)
        total_taps = both[:, 0:128] + both[:, 128:256] + along
        value = scale[where, :] * fields[q, now, where, :] + gain[where, :] * total_taps
        value = value + pert[q, where, :] * snap[n, where, :]
        if n > 1:
            value = value - fields[q, before, where, :]
        if n < steps - 1:
            fields[q, before, where, :] = value
            keep(q, before, where, value)
        elif row is starts[0]:
            own_ref[pl.program_id(0) * PACK + q] = value.reshape(rows, cy, 128)
        else:
            send_ref[pl.program_id(0) * PACK + q] = value.reshape(rows, cy, 128).astype(jnp.bfloat16)

    items = []
    for n in range(1, steps - 1):
        at = 4 * n
        for m in spans(total - 8 * n):
            items += [(q, n, at, m) for q in range(PACK)]
            at += m
    for row in starts[0:2]:
        items += [(q, steps - 1, row, rows) for q in range(PACK)]
    queue = []
    for item in items:
        queue.append((item, products(*item)))
        if len(queue) > AHEAD:
            first, made = queue.pop(0)
            advanced(*first, *made)
    for first, made in queue:
        advanced(*first, *made)


def propagate(bounds, operands, begin, count, steps, rows, halo):
    _, _, cy, cz = operands[0].shape
    total = 2 * rows + 2 * halo
    whole = pl.BlockSpec(memory_space=pltpu.VMEM)
    grid_spec = pltpu.PrefetchScalarGridSpec(
        num_scalar_prefetch=1,
        grid=(count // PACK,),
        in_specs=[whole] * 2 + [pl.BlockSpec(memory_space=pltpu.HBM)] * 2 + [whole] * (len(operands) - 4),
        out_specs=[whole, whole],
        scratch_shapes=[
            pltpu.VMEM((PACK, total * cy, cz), jnp.float32),
            pltpu.VMEM((steps + steps % 2, total * cy, cz), jnp.float32),
            pltpu.VMEM((total * cy, cz), jnp.float32),
            pltpu.VMEM((total * cy, cz), jnp.float32),
            pltpu.VMEM((PACK, 2, total * cy, cz), jnp.float32),
            pltpu.VMEM((PACK, 2, total * cy, 2 * cz), jnp.bfloat16),
            pltpu.VMEM((SPAN * cy, (SPAN + 8) * cy), jnp.bfloat16),
            pltpu.VMEM((2 * cz, cz), jnp.bfloat16),
            pltpu.VMEM((count, rows, cy, cz), jnp.bfloat16),
            pltpu.VMEM((count, halo - rows, cy, cz), jnp.bfloat16),
            pltpu.SemaphoreType.DMA((2,)),
        ],
    )
    cells = count * total * cy * cz
    return pl.pallas_call(
        functools.partial(march, steps, rows, halo, begin),
        grid_spec=grid_spec,
        out_shape=[
            jax.ShapeDtypeStruct((count, rows, cy, cz), jnp.float32),
            jax.ShapeDtypeStruct((count, rows, cy, cz), jnp.bfloat16),
        ],
        compiler_params=pltpu.CompilerParams(vmem_limit_bytes=16 << 20),
        cost_estimate=pl.CostEstimate(flops=cells * 8000, bytes_accessed=cells * 4, transcendentals=0),
        name="march",
    )(bounds, *operands)


def local(probe_field, bounds, courant, snapshots, snap_times, basis_panels):
    probes_here, rows, cy, cz = probe_field.shape
    steps = snap_times.shape[0]
    half = probes_here // 2
    halo = 4 * (steps - 1)
    far = halo - rows
    devices = lax.axis_size("store")
    place = lax.axis_index("store")
    member = lax.axis_index("probe")
    members = lax.axis_size("probe")
    par = (place % 2).astype(jnp.int32)
    core = (member % 2).astype(jnp.int32)
    swap = [(i, i ^ 1) for i in range(devices)]
    perm_a = [(i, i - 2) for i in range(2, devices, 2)] + [(i, i + 2) for i in range(1, devices - 2, 2)]
    perm_b = [(i, i + 2) for i in range(0, devices - 2, 2)] + [(i, i - 2) for i in range(3, devices, 2)]
    hop = lambda x, pairs: lax.ppermute(x, "store", pairs)
    cores = lambda x: lax.ppermute(x, "probe", [(i, i ^ 1) for i in range(members)])
    cut = lambda x, start: lax.dynamic_slice_in_dim(x, start, far, axis=1)
    near = rows - far

    after = lambda x, *first: lax.optimization_barrier((x, *first))[0]
    trim = lambda x: jnp.concatenate([x[:far_half], x[near_half:]], axis=0)
    planes = lambda *xs: jnp.concatenate([x.reshape(-1, cy, cz) for x in xs], axis=0)
    near_half, far_half = shares(steps, rows, halo)

    def picked(parity):
        chosen = jnp.minimum(2 * jnp.arange(near_half) + parity, steps - 1)
        return jnp.take(snapshots, jnp.take(snap_times, chosen, mode="clip"), axis=0, mode="clip")

    joined = picked(core)
    sent = picked(1 - core)
    gots = []
    span = 1
    while span < members:
        got = lax.ppermute(sent, "probe", [(i, i ^ span) for i in range(members)])
        upper = (member // span) % 2 == 1
        joined = jnp.concatenate([jnp.where(upper, got, joined), jnp.where(upper, joined, got)], axis=2)
        sent = joined
        gots.append(got)
        span *= 2
    high = lax.reduce_precision(courant, 8, 7)
    rate = jnp.where(core == 0, high, courant - high).astype(jnp.bfloat16)[None]
    extra = jnp.concatenate([joined, rate], axis=0)

    mine = lax.dynamic_slice_in_dim(probe_field, half * par, half, axis=0)
    theirs = lax.dynamic_slice_in_dim(probe_field, half * (1 - par), half, axis=0)
    partner = hop(theirs, swap)
    side_a = hop(after(mine, gots[0]), perm_a)
    side_b = hop(cut(after(mine, gots[-1]), near * (1 - par)), perm_b)
    extra_x = hop(after(extra, partner), swap)
    far_own, far_x = cut(trim(extra), near * (1 - par)), cut(trim(extra_x), near * par)
    side_c = hop(after(planes(partner, extra_x, far_own), side_b), perm_b)
    side_d = hop(after(planes(cut(partner, near * par), extra, far_x), side_a), perm_a)
    near_other = cores(planes(extra, extra_x))
    far_other = cores(planes(side_c[half * rows :], side_d[half * far :]))
    operands = (mine, partner, side_a, side_b, side_c, side_d, extra, extra_x, near_other, far_other)
    basis_later = basis_panels
    crossed = lax.ppermute(basis_later, "probe", [(i, i ^ 2) for i in range(members)])
    first = par == 0
    own, back = [], []
    for begin, count in ((0, half // 2), (half // 2, half - half // 2)):
        kept, sent = propagate(bounds, operands, begin, count, steps, rows, halo)
        own.append(kept)
        back.append(hop(sent, swap))
    panels = [basis_later, cores(basis_later)]
    crossed = lax.optimization_barrier((crossed, own[0]))[0]
    panels = [jnp.concatenate(panels, axis=0), jnp.concatenate([crossed, cores(crossed)], axis=0)]
    dots = lambda x: jnp.concatenate(
        [
            lax.dot_general(y, x, (((1, 2, 3), (1, 2, 3)), ((), ())), preferred_element_type=jnp.float32)
            for y in panels
        ],
        axis=0,
    )
    own = jnp.concatenate(own, axis=0)
    mine_part = dots(own.astype(jnp.bfloat16))
    back = jnp.concatenate(back, axis=0)
    back_part = dots(back)
    back = back.astype(jnp.float32)
    response = jnp.concatenate([jnp.where(first, own, back), jnp.where(first, back, own)], axis=0)
    product = jnp.concatenate(
        [jnp.where(first, mine_part, back_part), jnp.where(first, back_part, mine_part)], axis=1
    )
    product = product.reshape(members, -1, probes_here)
    span = 1
    while span < members:
        swapped = product.reshape(-1, 2, span, *product.shape[1:])[:, ::-1].reshape(product.shape)
        product = jnp.where((member // span) % 2 == 1, swapped, product)
        span *= 2
    product = product.reshape(-1, probes_here)
    span = 1
    while span < devices:
        product = product + hop(product, [(i, i ^ span) for i in range(devices)])
        span *= 2
    return response, product


def solution(mesh):
    placed = (
        P("probe", "store", None, None),
        P("probe", None),
        P("store", None, None),
        P(None, "store", "probe", None),
        P(),
        P("probe", "store", None, None),
    )
    return jax.shard_map(
        local,
        mesh=mesh,
        in_specs=placed,
        out_specs=(P("probe", "store", None, None), P(None, "probe")),
        check_vma=False,
    )
```

```python
import functools

import jax
import jax.numpy as jnp
import numpy as np
from jax import lax
from jax.experimental import pallas as pl
from jax.experimental.pallas import tpu as pltpu
from jax.sharding import PartitionSpec as P

taps = (-205.0 / 72.0, 8.0 / 5.0, -1.0 / 5.0, 8.0 / 315.0, -1.0 / 560.0)
SPAN = 24
PACK = 2
AHEAD = 1


def tables(cells_y, cells_z):
    def banded(apart, allowed):
        out = jnp.zeros(apart.shape, jnp.float32)
        for d in range(1, 5):
            out = jnp.where(allowed & (apart == d), taps[d] / taps[1], out)
        return out

    shape = (SPAN * cells_y, (SPAN + 8) * cells_y)
    row = lax.broadcasted_iota(jnp.int32, shape, 0)
    column = lax.broadcasted_iota(jnp.int32, shape, 1)
    planes = jnp.abs(column // cells_y - 4 - row // cells_y)
    lines = jnp.abs(column % cells_y - row % cells_y)
    left = banded(planes, lines == 0) + banded(lines, planes == 0)
    shape = (2 * cells_z, cells_z)
    row = lax.broadcasted_iota(jnp.int32, shape, 0) % cells_z
    apart = jnp.abs(row - lax.broadcasted_iota(jnp.int32, shape, 1))
    right = banded(apart, apart > 0)
    return left.astype(jnp.bfloat16), right.astype(jnp.bfloat16)


def spans(rows):
    out = []
    while rows > 0:
        out.append(min(SPAN, rows))
        rows -= out[-1]
    return out


def shares(steps, rows, halo):
    return (steps + 1) // 2, (-(-(halo - rows) // 4) + 1) // 2


def march(steps, rows, halo, begin, bounds_ref, *refs):
    wide, narrow = refs[0:4], refs[4:6]
    c_ref, d_ref = narrow
    near_refs = refs[6:8]
    near_other, far_other, own_ref, send_ref = refs[8:12]
    pert, snap, scale, gain, fields, split, left_ref, right_ref, a_buf, b_buf, sems = refs[12:23]
    count = a_buf.shape[0]
    fetch = [
        pltpu.make_async_copy(wide[j].at[pl.ds(begin, count)], buf, sems.at[j - 2])
        for j, buf in ((2, a_buf), (3, b_buf))
    ]
    total = 2 * rows + 2 * halo
    cy = 8
    far = halo - rows
    place = lax.axis_index("store")
    par, core = place % 2, lax.axis_index("probe") % 2
    base = (place // 2) * 2 * rows - halo
    probes = wide[0].shape[0]
    even = (halo, halo + rows, halo + 2 * rows, 0, halo - rows, halo + 3 * rows)
    odd = (halo + rows, halo, halo - rows, halo + 3 * rows, halo + 2 * rows, 0)
    counts = (rows, rows, rows, far, rows, far)
    starts = [e + par * (o - e) for e, o in zip(even, odd)]
    near_half, far_half = shares(steps, rows, halo)

    @pl.when(pl.program_id(0) == 0)
    def _():
        for copy in fetch:
            copy.start()
        left_ref[...], right_ref[...] = tables(cy, 128)
        near_size, far_size = (near_half + 1) * rows, (far_half + 1) * far
        c_base = c_ref.shape[0] - near_size - far_size
        d_base = d_ref.shape[0] - near_size - far_size
        held = (
            (d_ref, d_base, near_size + far_size),
            (c_ref, c_base + near_size, near_size),
            (c_ref, c_base, 0),
            (d_ref, d_base + near_size, 2 * near_size + far_size),
        )
        for j in range(6):
            kept = far_half if j in (3, 5) else near_half
            where = pl.ds(pl.multiple_of(starts[j] * cy, 32), counts[j] * cy)
            for t in range(kept + 1):
                at = t * counts[j]
                if j < 2:
                    mine = near_refs[j][t]
                    at += j * near_size
                    other = near_other[at : at + counts[j]]
                else:
                    source, first, second = held[j - 2]
                    mine = source[first + at : first + at + counts[j]]
                    other = far_other[second + at : second + at + counts[j]]
                mine = mine.reshape(counts[j] * cy, 128).astype(jnp.float32)
                other = other.reshape(counts[j] * cy, 128).astype(jnp.float32)
                if t < kept:
                    snap[2 * t + core, where, :] = mine
                    snap[2 * t + 1 - core, where, :] = other
                else:
                    scale[where, :] = 2.0 + (3.0 * taps[0]) * (mine + other)
                    gain[where, :] = taps[1] * (mine + other)

        for copy in fetch:
            copy.wait()

    for q in range(PACK):
        probe = begin + pl.program_id(0) * PACK + q
        low = bounds_ref[probes * par + probe, 0] - base
        high = bounds_ref[probes * par + probe, 1] - base
        for j in range(6):
            where = pl.ds(pl.multiple_of(starts[j] * cy, 32), counts[j] * cy)
            if j < 2:
                value = wide[j][probe].astype(jnp.float32)
            elif j < 4:
                value = (a_buf, b_buf)[j - 2][probe - begin].astype(jnp.float32)
            else:
                value = narrow[j - 4][pl.ds(probe * counts[j], counts[j])].astype(jnp.float32)
            plane = lax.broadcasted_iota(jnp.int32, value.shape, 0) + starts[j]
            value = jnp.where((plane >= low) & (plane < high), value, 0.0)
            pert[q, where, :] = value.reshape(counts[j] * cy, 128)

    def keep(q, slot, where, value):
        high = value.astype(jnp.bfloat16)
        low = (value - high.astype(jnp.float32)).astype(jnp.bfloat16)
        split[q, slot, where, 0:128] = high
        split[q, slot, where, 128:256] = low

    at = 0
    for m in spans(total):
        where = pl.ds(at * cy, m * cy)
        for q in range(PACK):
            first = pert[q, where, :] * snap[0, where, :]
            fields[q, 0, where, :] = first
            keep(q, 0, where, first)
        at += m

    def slab(row, count):
        if isinstance(row, int):
            return pl.ds(row * cy, count * cy)
        return pl.ds(pl.multiple_of(row * cy, 32), count * cy)

    def products(q, n, row, m):
        now = (n + 1) % 2
        both = jnp.dot(
            left_ref[0 : m * cy, 0 : (m + 8) * cy],
            split[q, now, slab(row - 4, m + 8), :],
            preferred_element_type=jnp.float32,
        )
        along = jnp.dot(split[q, now, slab(row, m), :], right_ref[...], preferred_element_type=jnp.float32)
        return both, along

    def advanced(q, n, row, m, both, along):
        now, before = (n + 1) % 2, n % 2
        where = slab(row, m)
        total_taps = both[:, 0:128] + both[:, 128:256] + along
        value = scale[where, :] * fields[q, now, where, :] + gain[where, :] * total_taps
        value = value + pert[q, where, :] * snap[n, where, :]
        if n > 1:
            value = value - fields[q, before, where, :]
        if n < steps - 1:
            fields[q, before, where, :] = value
            keep(q, before, where, value)
        elif row is starts[0]:
            own_ref[pl.program_id(0) * PACK + q] = value.reshape(rows, cy, 128)
        else:
            send_ref[pl.program_id(0) * PACK + q] = value.reshape(rows, cy, 128).astype(jnp.bfloat16)

    items = []
    for n in range(1, steps - 1):
        at = 4 * n
        for m in spans(total - 8 * n):
            items += [(q, n, at, m) for q in range(PACK)]
            at += m
    for row in starts[0:2]:
        items += [(q, steps - 1, row, rows) for q in range(PACK)]
    queue = []
    for item in items:
        queue.append((item, products(*item)))
        if len(queue) > AHEAD:
            first, made = queue.pop(0)
            advanced(*first, *made)
    for first, made in queue:
        advanced(*first, *made)


def propagate(bounds, operands, begin, count, steps, rows, halo):
    _, _, cy, cz = operands[0].shape
    total = 2 * rows + 2 * halo
    whole = pl.BlockSpec(memory_space=pltpu.VMEM)
    grid_spec = pltpu.PrefetchScalarGridSpec(
        num_scalar_prefetch=1,
        grid=(count // PACK,),
        in_specs=[whole] * 2 + [pl.BlockSpec(memory_space=pltpu.HBM)] * 2 + [whole] * (len(operands) - 4),
        out_specs=[whole, whole],
        scratch_shapes=[
            pltpu.VMEM((PACK, total * cy, cz), jnp.float32),
            pltpu.VMEM((steps + steps % 2, total * cy, cz), jnp.float32),
            pltpu.VMEM((total * cy, cz), jnp.float32),
            pltpu.VMEM((total * cy, cz), jnp.float32),
            pltpu.VMEM((PACK, 2, total * cy, cz), jnp.float32),
            pltpu.VMEM((PACK, 2, total * cy, 2 * cz), jnp.bfloat16),
            pltpu.VMEM((SPAN * cy, (SPAN + 8) * cy), jnp.bfloat16),
            pltpu.VMEM((2 * cz, cz), jnp.bfloat16),
            pltpu.VMEM((count, rows, cy, cz), jnp.bfloat16),
            pltpu.VMEM((count, halo - rows, cy, cz), jnp.bfloat16),
            pltpu.SemaphoreType.DMA((2,)),
        ],
    )
    cells = count * total * cy * cz
    return pl.pallas_call(
        functools.partial(march, steps, rows, halo, begin),
        grid_spec=grid_spec,
        out_shape=[
            jax.ShapeDtypeStruct((count, rows, cy, cz), jnp.float32),
            jax.ShapeDtypeStruct((count, rows, cy, cz), jnp.bfloat16),
        ],
        compiler_params=pltpu.CompilerParams(vmem_limit_bytes=16 << 20),
        cost_estimate=pl.CostEstimate(flops=cells * 8000, bytes_accessed=cells * 4, transcendentals=0),
        name="march",
    )(bounds, *operands)


def local(probe_field, bounds, courant, snapshots, snap_times, basis_panels):
    probes_here, rows, cy, cz = probe_field.shape
    steps = snap_times.shape[0]
    half = probes_here // 2
    halo = 4 * (steps - 1)
    far = halo - rows
    devices = lax.axis_size("store")
    place = lax.axis_index("store")
    member = lax.axis_index("probe")
    members = lax.axis_size("probe")
    par = (place % 2).astype(jnp.int32)
    core = (member % 2).astype(jnp.int32)
    swap = [(i, i ^ 1) for i in range(devices)]
    perm_a = [(i, i - 2) for i in range(2, devices, 2)] + [(i, i + 2) for i in range(1, devices - 2, 2)]
    perm_b = [(i, i + 2) for i in range(0, devices - 2, 2)] + [(i, i - 2) for i in range(3, devices, 2)]
    hop = lambda x, pairs: lax.ppermute(x, "store", pairs)
    cores = lambda x: lax.ppermute(x, "probe", [(i, i ^ 1) for i in range(members)])
    cut = lambda x, start: lax.dynamic_slice_in_dim(x, start, far, axis=1)
    near = rows - far

    after = lambda x, *first: lax.optimization_barrier((x, *first))[0]
    trim = lambda x: jnp.concatenate([x[:far_half], x[near_half:]], axis=0)
    planes = lambda *xs: jnp.concatenate([x.reshape(-1, cy, cz) for x in xs], axis=0)
    near_half, far_half = shares(steps, rows, halo)

    def picked(parity):
        chosen = jnp.minimum(2 * jnp.arange(near_half) + parity, steps - 1)
        return jnp.take(snapshots, jnp.take(snap_times, chosen, mode="clip"), axis=0, mode="clip")

    joined = picked(core)
    sent = picked(1 - core)
    gots = []
    span = 1
    while span < members:
        got = lax.ppermute(sent, "probe", [(i, i ^ span) for i in range(members)])
        upper = (member // span) % 2 == 1
        joined = jnp.concatenate([jnp.where(upper, got, joined), jnp.where(upper, joined, got)], axis=2)
        sent = joined
        gots.append(got)
        span *= 2
    high = lax.reduce_precision(courant, 8, 7)
    rate = jnp.where(core == 0, high, courant - high).astype(jnp.bfloat16)[None]
    extra = jnp.concatenate([joined, rate], axis=0)

    mine = lax.dynamic_slice_in_dim(probe_field, half * par, half, axis=0)
    theirs = lax.dynamic_slice_in_dim(probe_field, half * (1 - par), half, axis=0)
    partner = hop(theirs, swap)
    side_a = hop(after(mine, gots[0]), perm_a)
    side_b = hop(cut(after(mine, gots[-1]), near * (1 - par)), perm_b)
    extra_x = hop(after(extra, partner), swap)
    far_own, far_x = cut(trim(extra), near * (1 - par)), cut(trim(extra_x), near * par)
    side_c = hop(after(planes(partner, extra_x, far_own), side_b), perm_b)
    side_d = hop(after(planes(cut(partner, near * par), extra, far_x), side_a), perm_a)
    near_other = cores(planes(extra, extra_x))
    far_other = cores(planes(side_c[half * rows :], side_d[half * far :]))
    operands = (mine, partner, side_a, side_b, side_c, side_d, extra, extra_x, near_other, far_other)
    basis_later = basis_panels
    crossed = lax.ppermute(basis_later, "probe", [(i, i ^ 2) for i in range(members)])
    first = par == 0
    own, back = [], []
    for begin, count in ((0, half // 2), (half // 2, half - half // 2)):
        kept, sent = propagate(bounds, operands, begin, count, steps, rows, halo)
        own.append(kept)
        back.append(hop(sent, swap))
    panels = [basis_later, cores(basis_later)]
    crossed = lax.optimization_barrier((crossed, back[0][0, 0, 0, 0]))[0]
    panels = [jnp.concatenate(panels, axis=0), jnp.concatenate([crossed, cores(crossed)], axis=0)]
    dots = lambda x: jnp.concatenate(
        [
            lax.dot_general(y, x, (((1, 2, 3), (1, 2, 3)), ((), ())), preferred_element_type=jnp.float32)
            for y in panels
        ],
        axis=0,
    )
    own = jnp.concatenate(own, axis=0)
    mine_part = dots(own.astype(jnp.bfloat16))
    back = jnp.concatenate(back, axis=0)
    back_part = dots(back)
    back = back.astype(jnp.float32)
    response = jnp.concatenate([jnp.where(first, own, back), jnp.where(first, back, own)], axis=0)
    product = jnp.concatenate(
        [jnp.where(first, mine_part, back_part), jnp.where(first, back_part, mine_part)], axis=1
    )
    product = product.reshape(members, -1, probes_here)
    span = 1
    while span < members:
        swapped = product.reshape(-1, 2, span, *product.shape[1:])[:, ::-1].reshape(product.shape)
        product = jnp.where((member // span) % 2 == 1, swapped, product)
        span *= 2
    product = product.reshape(-1, probes_here)
    span = 1
    while span < devices:
        product = product + hop(product, [(i, i ^ span) for i in range(devices)])
        span *= 2
    return response, product


def solution(mesh):
    placed = (
        P("probe", "store", None, None),
        P("probe", None),
        P("store", None, None),
        P(None, "store", "probe", None),
        P(),
        P("probe", "store", None, None),
    )
    return jax.shard_map(
        local,
        mesh=mesh,
        in_specs=placed,
        out_specs=(P("probe", "store", None, None), P(None, "probe")),
        check_vma=False,
    )
```

```python
import functools

import jax
import jax.numpy as jnp
import numpy as np
from jax import lax
from jax.experimental import pallas as pl
from jax.experimental.pallas import tpu as pltpu
from jax.sharding import PartitionSpec as P

taps = (-205.0 / 72.0, 8.0 / 5.0, -1.0 / 5.0, 8.0 / 315.0, -1.0 / 560.0)
SPAN = 24
PACK = 2
AHEAD = 1


def tables(cells_y, cells_z):
    def banded(apart, allowed):
        out = jnp.zeros(apart.shape, jnp.float32)
        for d in range(1, 5):
            out = jnp.where(allowed & (apart == d), taps[d] / taps[1], out)
        return out

    shape = (SPAN * cells_y, (SPAN + 8) * cells_y)
    row = lax.broadcasted_iota(jnp.int32, shape, 0)
    column = lax.broadcasted_iota(jnp.int32, shape, 1)
    planes = jnp.abs(column // cells_y - 4 - row // cells_y)
    lines = jnp.abs(column % cells_y - row % cells_y)
    left = banded(planes, lines == 0) + banded(lines, planes == 0)
    shape = (2 * cells_z, cells_z)
    row = lax.broadcasted_iota(jnp.int32, shape, 0) % cells_z
    apart = jnp.abs(row - lax.broadcasted_iota(jnp.int32, shape, 1))
    right = banded(apart, apart > 0)
    return left.astype(jnp.bfloat16), right.astype(jnp.bfloat16)


def spans(rows):
    out = []
    while rows > 0:
        out.append(min(SPAN, rows))
        rows -= out[-1]
    return out


def shares(steps, rows, halo):
    return (steps + 1) // 2, (-(-(halo - rows) // 4) + 1) // 2


def march(steps, rows, halo, begin, bounds_ref, *refs):
    wide, narrow = refs[0:4], refs[4:6]
    c_ref, d_ref = narrow
    near_refs = refs[6:8]
    near_others = refs[8:10]
    far_other, own_ref, send_ref = refs[10:13]
    pert, snap, scale, gain, fields, split, left_ref, right_ref, a_buf, b_buf, sems = refs[13:24]
    count = a_buf.shape[0]
    fetch = [
        pltpu.make_async_copy(wide[j].at[pl.ds(begin, count)], buf, sems.at[j - 2])
        for j, buf in ((2, a_buf), (3, b_buf))
    ]
    total = 2 * rows + 2 * halo
    cy = 8
    far = halo - rows
    place = lax.axis_index("store")
    par, core = place % 2, lax.axis_index("probe") % 2
    base = (place // 2) * 2 * rows - halo
    probes = wide[0].shape[0]
    even = (halo, halo + rows, halo + 2 * rows, 0, halo - rows, halo + 3 * rows)
    odd = (halo + rows, halo, halo - rows, halo + 3 * rows, halo + 2 * rows, 0)
    counts = (rows, rows, rows, far, rows, far)
    starts = [e + par * (o - e) for e, o in zip(even, odd)]
    near_half, far_half = shares(steps, rows, halo)

    @pl.when(pl.program_id(0) == 0)
    def _():
        for copy in fetch:
            copy.start()
        left_ref[...], right_ref[...] = tables(cy, 128)
        near_size, far_size = (near_half + 1) * rows, (far_half + 1) * far
        c_base = c_ref.shape[0] - near_size - far_size
        d_base = d_ref.shape[0] - near_size - far_size
        held = (
            (d_ref, d_base, near_size + far_size),
            (c_ref, c_base + near_size, near_size),
            (c_ref, c_base, 0),
            (d_ref, d_base + near_size, 2 * near_size + far_size),
        )
        for j in range(6):
            kept = far_half if j in (3, 5) else near_half
            where = pl.ds(pl.multiple_of(starts[j] * cy, 32), counts[j] * cy)
            for t in range(kept + 1):
                at = t * counts[j]
                if j < 2:
                    mine, other = near_refs[j][t], near_others[j][t]
                else:
                    source, first, second = held[j - 2]
                    mine = source[first + at : first + at + counts[j]]
                    other = far_other[second + at : second + at + counts[j]]
                mine = mine.reshape(counts[j] * cy, 128).astype(jnp.float32)
                other = other.reshape(counts[j] * cy, 128).astype(jnp.float32)
                if t < kept:
                    snap[2 * t + core, where, :] = mine
                    snap[2 * t + 1 - core, where, :] = other
                else:
                    scale[where, :] = 2.0 + (3.0 * taps[0]) * (mine + other)
                    gain[where, :] = taps[1] * (mine + other)

        for copy in fetch:
            copy.wait()

    for q in range(PACK):
        probe = begin + pl.program_id(0) * PACK + q
        low = bounds_ref[probes * par + probe, 0] - base
        high = bounds_ref[probes * par + probe, 1] - base
        for j in range(6):
            where = pl.ds(pl.multiple_of(starts[j] * cy, 32), counts[j] * cy)
            if j < 2:
                value = wide[j][probe].astype(jnp.float32)
            elif j < 4:
                value = (a_buf, b_buf)[j - 2][probe - begin].astype(jnp.float32)
            else:
                value = narrow[j - 4][pl.ds(probe * counts[j], counts[j])].astype(jnp.float32)
            plane = lax.broadcasted_iota(jnp.int32, value.shape, 0) + starts[j]
            value = jnp.where((plane >= low) & (plane < high), value, 0.0)
            pert[q, where, :] = value.reshape(counts[j] * cy, 128)

    def keep(q, slot, where, value):
        high = value.astype(jnp.bfloat16)
        low = (value - high.astype(jnp.float32)).astype(jnp.bfloat16)
        split[q, slot, where, 0:128] = high
        split[q, slot, where, 128:256] = low

    at = 0
    for m in spans(total):
        where = pl.ds(at * cy, m * cy)
        for q in range(PACK):
            first = pert[q, where, :] * snap[0, where, :]
            fields[q, 0, where, :] = first
            keep(q, 0, where, first)
        at += m

    def slab(row, count):
        if isinstance(row, int):
            return pl.ds(row * cy, count * cy)
        return pl.ds(pl.multiple_of(row * cy, 32), count * cy)

    def products(q, n, row, m):
        now = (n + 1) % 2
        both = jnp.dot(
            left_ref[0 : m * cy, 0 : (m + 8) * cy],
            split[q, now, slab(row - 4, m + 8), :],
            preferred_element_type=jnp.float32,
        )
        along = jnp.dot(split[q, now, slab(row, m), :], right_ref[...], preferred_element_type=jnp.float32)
        return both, along

    def advanced(q, n, row, m, both, along):
        now, before = (n + 1) % 2, n % 2
        where = slab(row, m)
        total_taps = both[:, 0:128] + both[:, 128:256] + along
        value = scale[where, :] * fields[q, now, where, :] + gain[where, :] * total_taps
        value = value + pert[q, where, :] * snap[n, where, :]
        if n > 1:
            value = value - fields[q, before, where, :]
        if n < steps - 1:
            fields[q, before, where, :] = value
            keep(q, before, where, value)
        elif row is starts[0]:
            own_ref[pl.program_id(0) * PACK + q] = value.reshape(rows, cy, 128)
        else:
            send_ref[pl.program_id(0) * PACK + q] = value.reshape(rows, cy, 128).astype(jnp.bfloat16)

    items = []
    for n in range(1, steps - 1):
        at = 4 * n
        for m in spans(total - 8 * n):
            items += [(q, n, at, m) for q in range(PACK)]
            at += m
    for row in starts[0:2]:
        items += [(q, steps - 1, row, rows) for q in range(PACK)]
    queue = []
    for item in items:
        queue.append((item, products(*item)))
        if len(queue) > AHEAD:
            first, made = queue.pop(0)
            advanced(*first, *made)
    for first, made in queue:
        advanced(*first, *made)


def propagate(bounds, operands, begin, count, steps, rows, halo):
    _, _, cy, cz = operands[0].shape
    total = 2 * rows + 2 * halo
    whole = pl.BlockSpec(memory_space=pltpu.VMEM)
    grid_spec = pltpu.PrefetchScalarGridSpec(
        num_scalar_prefetch=1,
        grid=(count // PACK,),
        in_specs=[whole] * 2 + [pl.BlockSpec(memory_space=pltpu.HBM)] * 2 + [whole] * (len(operands) - 4),
        out_specs=[whole, whole],
        scratch_shapes=[
            pltpu.VMEM((PACK, total * cy, cz), jnp.float32),
            pltpu.VMEM((steps + steps % 2, total * cy, cz), jnp.float32),
            pltpu.VMEM((total * cy, cz), jnp.float32),
            pltpu.VMEM((total * cy, cz), jnp.float32),
            pltpu.VMEM((PACK, 2, total * cy, cz), jnp.float32),
            pltpu.VMEM((PACK, 2, total * cy, 2 * cz), jnp.bfloat16),
            pltpu.VMEM((SPAN * cy, (SPAN + 8) * cy), jnp.bfloat16),
            pltpu.VMEM((2 * cz, cz), jnp.bfloat16),
            pltpu.VMEM((count, rows, cy, cz), jnp.bfloat16),
            pltpu.VMEM((count, halo - rows, cy, cz), jnp.bfloat16),
            pltpu.SemaphoreType.DMA((2,)),
        ],
    )
    cells = count * total * cy * cz
    return pl.pallas_call(
        functools.partial(march, steps, rows, halo, begin),
        grid_spec=grid_spec,
        out_shape=[
            jax.ShapeDtypeStruct((count, rows, cy, cz), jnp.float32),
            jax.ShapeDtypeStruct((count, rows, cy, cz), jnp.bfloat16),
        ],
        compiler_params=pltpu.CompilerParams(vmem_limit_bytes=16 << 20),
        cost_estimate=pl.CostEstimate(flops=cells * 8000 if begin else 0, bytes_accessed=cells * 4 if begin else 0, transcendentals=0),
        name="march",
    )(bounds, *operands)


def local(probe_field, bounds, courant, snapshots, snap_times, basis_panels):
    probes_here, rows, cy, cz = probe_field.shape
    steps = snap_times.shape[0]
    half = probes_here // 2
    halo = 4 * (steps - 1)
    far = halo - rows
    devices = lax.axis_size("store")
    place = lax.axis_index("store")
    member = lax.axis_index("probe")
    members = lax.axis_size("probe")
    par = (place % 2).astype(jnp.int32)
    core = (member % 2).astype(jnp.int32)
    swap = [(i, i ^ 1) for i in range(devices)]
    perm_a = [(i, i - 2) for i in range(2, devices, 2)] + [(i, i + 2) for i in range(1, devices - 2, 2)]
    perm_b = [(i, i + 2) for i in range(0, devices - 2, 2)] + [(i, i - 2) for i in range(3, devices, 2)]
    hop = lambda x, pairs: lax.ppermute(x, "store", pairs)
    cores = lambda x: lax.ppermute(x, "probe", [(i, i ^ 1) for i in range(members)])
    cut = lambda x, start: lax.dynamic_slice_in_dim(x, start, far, axis=1)
    near = rows - far

    after = lambda x, *first: lax.optimization_barrier((x, *first))[0]
    trim = lambda x: jnp.concatenate([x[:far_half], x[near_half:]], axis=0)
    planes = lambda *xs: jnp.concatenate([x.reshape(-1, cy, cz) for x in xs], axis=0)
    near_half, far_half = shares(steps, rows, halo)

    def picked(parity):
        chosen = jnp.minimum(2 * jnp.arange(near_half) + parity, steps - 1)
        return jnp.take(snapshots, jnp.take(snap_times, chosen, mode="clip"), axis=0, mode="clip")

    joined = picked(core)
    sent = picked(1 - core)
    gots = []
    span = 1
    while span < members:
        got = lax.ppermute(sent, "probe", [(i, i ^ span) for i in range(members)])
        upper = (member // span) % 2 == 1
        joined = jnp.concatenate([jnp.where(upper, got, joined), jnp.where(upper, joined, got)], axis=2)
        sent = joined
        gots.append(got)
        span *= 2
    high = lax.reduce_precision(courant, 8, 7)
    rate = jnp.where(core == 0, high, courant - high).astype(jnp.bfloat16)[None]
    extra = jnp.concatenate([joined, rate], axis=0)

    mine = lax.dynamic_slice_in_dim(probe_field, half * par, half, axis=0)
    theirs = lax.dynamic_slice_in_dim(probe_field, half * (1 - par), half, axis=0)
    partner = hop(theirs, swap)
    side_a = hop(after(mine, gots[0]), perm_a)
    side_b = hop(cut(after(mine, gots[-1]), near * (1 - par)), perm_b)
    extra_x = hop(after(extra, partner), swap)
    far_own, far_x = cut(trim(extra), near * (1 - par)), cut(trim(extra_x), near * par)
    turned = jnp.transpose(after(basis_panels, extra), (1, 2, 0, 3))
    crossed = lax.ppermute(turned, "probe", [(i, i ^ 2) for i in range(members)])
    side_c = hop(after(planes(partner, extra_x, far_own), side_b, turned), perm_b)
    side_d = hop(after(planes(cut(partner, near * par), extra, far_x), side_a), perm_a)
    far_other = cores(after(planes(side_c[half * rows :], side_d[half * far :]), crossed))
    operands = (mine, partner, side_a, side_b, side_c, side_d, extra, extra_x, cores(extra), cores(extra_x), far_other)
    first = par == 0
    own, back = [], []
    for begin, count in ((0, half // 2), (half // 2, half - half // 2)):
        kept, sent = propagate(bounds, operands, begin, count, steps, rows, halo)
        own.append(kept)
        back.append(hop(sent, swap))
    panels = [turned, cores(turned), crossed, cores(crossed)]
    dots = lambda x: jnp.concatenate(
        [
            lax.dot_general(y, x, (((0, 1, 3), (1, 2, 3)), ((), ())), preferred_element_type=jnp.float32)
            for y in panels
        ],
        axis=0,
    )
    own = jnp.concatenate(own, axis=0)
    mine_part = dots(own.astype(jnp.bfloat16))
    back = jnp.concatenate(back, axis=0)
    back_part = dots(back)
    back = back.astype(jnp.float32)
    response = jnp.concatenate([jnp.where(first, own, back), jnp.where(first, back, own)], axis=0)
    product = jnp.concatenate(
        [jnp.where(first, mine_part, back_part), jnp.where(first, back_part, mine_part)], axis=1
    )
    product = product.reshape(members, -1, probes_here)
    span = 1
    while span < members:
        swapped = product.reshape(-1, 2, span, *product.shape[1:])[:, ::-1].reshape(product.shape)
        product = jnp.where((member // span) % 2 == 1, swapped, product)
        span *= 2
    product = product.reshape(-1, probes_here)
    span = 1
    while span < devices:
        product = product + hop(product, [(i, i ^ span) for i in range(devices)])
        span *= 2
    return response, product


def solution(mesh):
    placed = (
        P("probe", "store", None, None),
        P("probe", None),
        P("store", None, None),
        P(None, "store", "probe", None),
        P(),
        P("probe", "store", None, None),
    )
    return jax.shard_map(
        local,
        mesh=mesh,
        in_specs=placed,
        out_specs=(P("probe", "store", None, None), P(None, "probe")),
        check_vma=False,
    )
```

```python
import functools

import jax
import jax.numpy as jnp
import numpy as np
from jax import lax
from jax.experimental import pallas as pl
from jax.experimental.pallas import tpu as pltpu
from jax.sharding import PartitionSpec as P

taps = (-205.0 / 72.0, 8.0 / 5.0, -1.0 / 5.0, 8.0 / 315.0, -1.0 / 560.0)
SPAN = 24
PACK = 2
AHEAD = 1


def tables(cells_y, cells_z):
    def banded(apart, allowed):
        out = jnp.zeros(apart.shape, jnp.float32)
        for d in range(1, 5):
            out = jnp.where(allowed & (apart == d), taps[d] / taps[1], out)
        return out

    shape = (SPAN * cells_y, (SPAN + 8) * cells_y)
    row = lax.broadcasted_iota(jnp.int32, shape, 0)
    column = lax.broadcasted_iota(jnp.int32, shape, 1)
    planes = jnp.abs(column // cells_y - 4 - row // cells_y)
    lines = jnp.abs(column % cells_y - row % cells_y)
    left = banded(planes, lines == 0) + banded(lines, planes == 0)
    shape = (2 * cells_z, cells_z)
    row = lax.broadcasted_iota(jnp.int32, shape, 0) % cells_z
    apart = jnp.abs(row - lax.broadcasted_iota(jnp.int32, shape, 1))
    right = banded(apart, apart > 0)
    return left.astype(jnp.bfloat16), right.astype(jnp.bfloat16)


def spans(rows):
    out = []
    while rows > 0:
        out.append(min(SPAN, rows))
        rows -= out[-1]
    return out


def shares(steps, rows, halo):
    return (steps + 1) // 2, (-(-(halo - rows) // 4) + 1) // 2


def march(steps, rows, halo, begin, bounds_ref, *refs):
    wide, narrow = refs[0:4], refs[4:6]
    c_ref, d_ref = narrow
    near_refs = refs[6:8]
    near_others = refs[8:10]
    far_other, own_ref, send_ref = refs[10:13]
    pert, snap, scale, gain, fields, split, left_ref, right_ref, a_buf, b_buf, sems = refs[13:24]
    count = a_buf.shape[0]
    fetch = [
        pltpu.make_async_copy(wide[j].at[pl.ds(begin, count)], buf, sems.at[j - 2])
        for j, buf in ((2, a_buf), (3, b_buf))
    ]
    total = 2 * rows + 2 * halo
    cy = 8
    far = halo - rows
    place = lax.axis_index("store")
    par, core = place % 2, lax.axis_index("probe") % 2
    base = (place // 2) * 2 * rows - halo
    probes = wide[0].shape[0]
    even = (halo, halo + rows, halo + 2 * rows, 0, halo - rows, halo + 3 * rows)
    odd = (halo + rows, halo, halo - rows, halo + 3 * rows, halo + 2 * rows, 0)
    counts = (rows, rows, rows, far, rows, far)
    starts = [e + par * (o - e) for e, o in zip(even, odd)]
    near_half, far_half = shares(steps, rows, halo)

    @pl.when(pl.program_id(0) == 0)
    def _():
        for copy in fetch:
            copy.start()
        left_ref[...], right_ref[...] = tables(cy, 128)
        near_size, far_size = (near_half + 1) * rows, (far_half + 1) * far
        c_base = c_ref.shape[0] - near_size - far_size
        d_base = d_ref.shape[0] - near_size - far_size
        held = (
            (d_ref, d_base, near_size + far_size),
            (c_ref, c_base + near_size, near_size),
            (c_ref, c_base, 0),
            (d_ref, d_base + near_size, 2 * near_size + far_size),
        )
        for j in range(6):
            kept = far_half if j in (3, 5) else near_half
            where = pl.ds(pl.multiple_of(starts[j] * cy, 32), counts[j] * cy)
            for t in range(kept + 1):
                at = t * counts[j]
                if j < 2:
                    mine, other = near_refs[j][t], near_others[j][t]
                else:
                    source, first, second = held[j - 2]
                    mine = source[first + at : first + at + counts[j]]
                    other = far_other[second + at : second + at + counts[j]]
                mine = mine.reshape(counts[j] * cy, 128).astype(jnp.float32)
                other = other.reshape(counts[j] * cy, 128).astype(jnp.float32)
                if t < kept:
                    snap[2 * t + core, where, :] = mine
                    snap[2 * t + 1 - core, where, :] = other
                else:
                    scale[where, :] = 2.0 + (3.0 * taps[0]) * (mine + other)
                    gain[where, :] = taps[1] * (mine + other)

        for copy in fetch:
            copy.wait()

    for q in range(PACK):
        probe = begin + pl.program_id(0) * PACK + q
        low = bounds_ref[probes * par + probe, 0] - base
        high = bounds_ref[probes * par + probe, 1] - base
        for j in range(6):
            where = pl.ds(pl.multiple_of(starts[j] * cy, 32), counts[j] * cy)
            if j < 2:
                value = wide[j][probe].astype(jnp.float32)
            elif j < 4:
                value = (a_buf, b_buf)[j - 2][probe - begin].astype(jnp.float32)
            else:
                value = narrow[j - 4][pl.ds(probe * counts[j], counts[j])].astype(jnp.float32)
            plane = lax.broadcasted_iota(jnp.int32, value.shape, 0) + starts[j]
            value = jnp.where((plane >= low) & (plane < high), value, 0.0)
            pert[q, where, :] = value.reshape(counts[j] * cy, 128)

    def keep(q, slot, where, value):
        high = value.astype(jnp.bfloat16)
        low = (value - high.astype(jnp.float32)).astype(jnp.bfloat16)
        split[q, slot, where, 0:128] = high
        split[q, slot, where, 128:256] = low

    at = 0
    for m in spans(total):
        where = pl.ds(at * cy, m * cy)
        for q in range(PACK):
            first = pert[q, where, :] * snap[0, where, :]
            fields[q, 0, where, :] = first
            keep(q, 0, where, first)
        at += m

    def slab(row, count):
        if isinstance(row, int):
            return pl.ds(row * cy, count * cy)
        return pl.ds(pl.multiple_of(row * cy, 32), count * cy)

    def products(q, n, row, m):
        now = (n + 1) % 2
        both = jnp.dot(
            left_ref[0 : m * cy, 0 : (m + 8) * cy],
            split[q, now, slab(row - 4, m + 8), :],
            preferred_element_type=jnp.float32,
        )
        along = jnp.dot(split[q, now, slab(row, m), :], right_ref[...], preferred_element_type=jnp.float32)
        return both, along

    def advanced(q, n, row, m, both, along):
        now, before = (n + 1) % 2, n % 2
        where = slab(row, m)
        total_taps = both[:, 0:128] + both[:, 128:256] + along
        value = scale[where, :] * fields[q, now, where, :] + gain[where, :] * total_taps
        value = value + pert[q, where, :] * snap[n, where, :]
        if n > 1:
            value = value - fields[q, before, where, :]
        if n < steps - 1:
            fields[q, before, where, :] = value
            keep(q, before, where, value)
        elif row is starts[0]:
            own_ref[pl.program_id(0) * PACK + q] = value.reshape(rows, cy, 128)
        else:
            send_ref[pl.program_id(0) * PACK + q] = value.reshape(rows, cy, 128).astype(jnp.bfloat16)

    items = []
    for n in range(1, steps - 1):
        at = 4 * n
        for m in spans(total - 8 * n):
            items += [(q, n, at, m) for q in range(PACK)]
            at += m
    for row in starts[0:2]:
        items += [(q, steps - 1, row, rows) for q in range(PACK)]
    queue = []
    for item in items:
        queue.append((item, products(*item)))
        if len(queue) > AHEAD:
            first, made = queue.pop(0)
            advanced(*first, *made)
    for first, made in queue:
        advanced(*first, *made)


def propagate(bounds, operands, begin, count, steps, rows, halo):
    _, _, cy, cz = operands[0].shape
    total = 2 * rows + 2 * halo
    whole = pl.BlockSpec(memory_space=pltpu.VMEM)
    grid_spec = pltpu.PrefetchScalarGridSpec(
        num_scalar_prefetch=1,
        grid=(count // PACK,),
        in_specs=[whole] * 2 + [pl.BlockSpec(memory_space=pltpu.HBM)] * 2 + [whole] * (len(operands) - 4),
        out_specs=[whole, whole],
        scratch_shapes=[
            pltpu.VMEM((PACK, total * cy, cz), jnp.float32),
            pltpu.VMEM((steps + steps % 2, total * cy, cz), jnp.float32),
            pltpu.VMEM((total * cy, cz), jnp.float32),
            pltpu.VMEM((total * cy, cz), jnp.float32),
            pltpu.VMEM((PACK, 2, total * cy, cz), jnp.float32),
            pltpu.VMEM((PACK, 2, total * cy, 2 * cz), jnp.bfloat16),
            pltpu.VMEM((SPAN * cy, (SPAN + 8) * cy), jnp.bfloat16),
            pltpu.VMEM((2 * cz, cz), jnp.bfloat16),
            pltpu.VMEM((count, rows, cy, cz), jnp.bfloat16),
            pltpu.VMEM((count, halo - rows, cy, cz), jnp.bfloat16),
            pltpu.SemaphoreType.DMA((2,)),
        ],
    )
    cells = count * total * cy * cz
    return pl.pallas_call(
        functools.partial(march, steps, rows, halo, begin),
        grid_spec=grid_spec,
        out_shape=[
            jax.ShapeDtypeStruct((count, rows, cy, cz), jnp.float32),
            jax.ShapeDtypeStruct((count, rows, cy, cz), jnp.bfloat16),
        ],
        compiler_params=pltpu.CompilerParams(vmem_limit_bytes=16 << 20),
        cost_estimate=pl.CostEstimate(flops=cells * 8000 if begin else 0, bytes_accessed=cells * 4 if begin else 0, transcendentals=0),
        name="march",
    )(bounds, *operands)


def local(probe_field, bounds, courant, snapshots, snap_times, basis_panels):
    probes_here, rows, cy, cz = probe_field.shape
    steps = snap_times.shape[0]
    half = probes_here // 2
    halo = 4 * (steps - 1)
    far = halo - rows
    devices = lax.axis_size("store")
    place = lax.axis_index("store")
    member = lax.axis_index("probe")
    members = lax.axis_size("probe")
    par = (place % 2).astype(jnp.int32)
    core = (member % 2).astype(jnp.int32)
    swap = [(i, i ^ 1) for i in range(devices)]
    perm_a = [(i, i - 2) for i in range(2, devices, 2)] + [(i, i + 2) for i in range(1, devices - 2, 2)]
    perm_b = [(i, i + 2) for i in range(0, devices - 2, 2)] + [(i, i - 2) for i in range(3, devices, 2)]
    hop = lambda x, pairs: lax.ppermute(x, "store", pairs)
    cores = lambda x: lax.ppermute(x, "probe", [(i, i ^ 1) for i in range(members)])
    cut = lambda x, start: lax.dynamic_slice_in_dim(x, start, far, axis=1)
    near = rows - far

    after = lambda x, *first: lax.optimization_barrier((x, *first))[0]
    trim = lambda x: jnp.concatenate([x[:far_half], x[near_half:]], axis=0)
    planes = lambda *xs: jnp.concatenate([x.reshape(-1, cy, cz) for x in xs], axis=0)
    near_half, far_half = shares(steps, rows, halo)

    mine = lax.dynamic_slice_in_dim(probe_field, half * par, half, axis=0)
    theirs = lax.dynamic_slice_in_dim(probe_field, half * (1 - par), half, axis=0)
    partner = hop(theirs, swap)

    pairs = jnp.pad(snap_times, (0, steps % 2))
    evens, odds = pairs[0::2], pairs[1::2]
    order = jnp.concatenate([jnp.where(core == 0, evens, odds), jnp.where(core == 0, odds, evens)])
    ordered = jnp.take(after(snapshots, theirs), order, axis=0, mode="clip")
    joined, sent = ordered[:near_half], ordered[near_half:]
    gots = []
    span = 1
    while span < members:
        got = lax.ppermute(sent, "probe", [(i, i ^ span) for i in range(members)])
        upper = (member // span) % 2 == 1
        joined = jnp.concatenate([jnp.where(upper, got, joined), jnp.where(upper, joined, got)], axis=2)
        sent = joined
        gots.append(got)
        span *= 2
    high = lax.reduce_precision(courant, 8, 7)
    rate = jnp.where(core == 0, high, courant - high).astype(jnp.bfloat16)[None]
    extra = jnp.concatenate([joined, rate], axis=0)

    side_a = hop(after(mine, gots[0]), perm_a)
    side_b = hop(cut(after(mine, gots[-1]), near * (1 - par)), perm_b)
    extra_x = hop(after(extra, partner), swap)
    far_own, far_x = cut(trim(extra), near * (1 - par)), cut(trim(extra_x), near * par)
    turned = jnp.transpose(after(basis_panels, extra), (1, 2, 0, 3))
    crossed = lax.ppermute(turned, "probe", [(i, i ^ 2) for i in range(members)])
    message, turned = lax.optimization_barrier((planes(partner, extra_x, far_own), turned, side_b))[:2]
    side_c = hop(message, perm_b)
    side_d = hop(after(planes(cut(partner, near * par), extra, far_x), side_a), perm_a)
    far_other = cores(after(planes(side_c[half * rows :], side_d[half * far :]), crossed))
    operands = (mine, partner, side_a, side_b, side_c, side_d, extra, extra_x, cores(extra), cores(extra_x), far_other)
    first = par == 0
    own, back = [], []
    early = half * 2 // 3 // PACK * PACK
    for begin, count in ((0, early), (early, half - early)):
        kept, sent = propagate(bounds, operands, begin, count, steps, rows, halo)
        own.append(kept)
        back.append(hop(sent, swap))
    panels = [turned, cores(turned), crossed, cores(crossed)]
    own = jnp.concatenate(own, axis=0)
    back = jnp.concatenate(back, axis=0)
    in_order = lambda x, y: jnp.concatenate([jnp.where(first, x, y), jnp.where(first, y, x)], axis=0)
    low = in_order(own.astype(jnp.bfloat16), back)
    parts = [
        lax.dot_general(x, low, (((0, 1, 3), (1, 2, 3)), ((), ())), preferred_element_type=jnp.float32)
        for x in panels
    ]
    rows_of = lambda q: functools.reduce(
        lambda kept, j: jnp.where(member == j, parts[q ^ j], kept), range(1, members), parts[q]
    )
    product = jnp.concatenate([rows_of(q) for q in range(members)], axis=0)
    response = in_order(own, back.astype(jnp.float32))
    span = 1
    while span < devices:
        product = product + hop(product, [(i, i ^ span) for i in range(devices)])
        span *= 2
    return response, product


def solution(mesh):
    placed = (
        P("probe", "store", None, None),
        P("probe", None),
        P("store", None, None),
        P(None, "store", "probe", None),
        P(),
        P("probe", "store", None, None),
    )
    return jax.shard_map(
        local,
        mesh=mesh,
        in_specs=placed,
        out_specs=(P("probe", "store", None, None), P(None, "probe")),
        check_vma=False,
    )
```

```python
import functools

import jax
import jax.numpy as jnp
import numpy as np
from jax import lax
from jax.experimental import pallas as pl
from jax.experimental.pallas import tpu as pltpu
from jax.sharding import PartitionSpec as P

taps = (-205.0 / 72.0, 8.0 / 5.0, -1.0 / 5.0, 8.0 / 315.0, -1.0 / 560.0)
SPAN = 24
PACK = 2
AHEAD = 1


def tables(cells_y, cells_z):
    def banded(apart, allowed):
        out = jnp.zeros(apart.shape, jnp.float32)
        for d in range(1, 5):
            out = jnp.where(allowed & (apart == d), taps[d] / taps[1], out)
        return out

    shape = (SPAN * cells_y, (SPAN + 8) * cells_y)
    row = lax.broadcasted_iota(jnp.int32, shape, 0)
    column = lax.broadcasted_iota(jnp.int32, shape, 1)
    planes = jnp.abs(column // cells_y - 4 - row // cells_y)
    lines = jnp.abs(column % cells_y - row % cells_y)
    left = banded(planes, lines == 0) + banded(lines, planes == 0)
    shape = (2 * cells_z, cells_z)
    row = lax.broadcasted_iota(jnp.int32, shape, 0) % cells_z
    apart = jnp.abs(row - lax.broadcasted_iota(jnp.int32, shape, 1))
    right = banded(apart, apart > 0)
    return left.astype(jnp.bfloat16), right.astype(jnp.bfloat16)


def spans(rows):
    out = []
    while rows > 0:
        out.append(min(SPAN, rows))
        rows -= out[-1]
    return out


def shares(steps, rows, halo):
    return (steps + 1) // 2, (-(-(halo - rows) // 4) + 1) // 2


def march(steps, rows, halo, begin, bounds_ref, *refs):
    wide, narrow = refs[0:4], refs[4:6]
    c_ref, d_ref = narrow
    if begin:
        shared, (own_ref, send_ref) = refs[6:11], refs[11:13]
        pert, fields, split = refs[13:16]
    else:
        near_refs, near_any, far_other = refs[6:8], refs[8:10], refs[10]
        (own_ref, send_ref), shared = refs[11:13], refs[13:18]
        pert, fields, split, near_buf, sems = refs[18:23]
    snap, scale, gain, left_ref, right_ref = shared
    total = 2 * rows + 2 * halo
    cy = 8
    far = halo - rows
    place = lax.axis_index("store")
    par, core = place % 2, lax.axis_index("probe") % 2
    base = (place // 2) * 2 * rows - halo
    probes = wide[0].shape[0]
    even = (halo, halo + rows, halo + 2 * rows, 0, halo - rows, halo + 3 * rows)
    odd = (halo + rows, halo, halo - rows, halo + 3 * rows, halo + 2 * rows, 0)
    counts = (rows, rows, rows, far, rows, far)
    starts = [e + par * (o - e) for e, o in zip(even, odd)]
    near_half, far_half = shares(steps, rows, halo)

    @pl.when((pl.program_id(0) == 0) & (begin == 0))
    def _():
        if begin:
            return
        fetch = [pltpu.make_async_copy(near_any[j], near_buf.at[j], sems.at[j]) for j in range(2)]
        for copy in fetch:
            copy.start()
        left_ref[...], right_ref[...] = tables(cy, 128)
        near_size, far_size = (near_half + 1) * rows, (far_half + 1) * far
        c_base = c_ref.shape[0] - near_size - far_size
        d_base = d_ref.shape[0] - near_size - far_size
        held = (
            (d_ref, d_base, near_size + far_size),
            (c_ref, c_base + near_size, near_size),
            (c_ref, c_base, 0),
            (d_ref, d_base + near_size, 2 * near_size + far_size),
        )
        for j in (2, 3, 4, 5, 0, 1):
            kept = far_half if j in (3, 5) else near_half
            if j < 2:
                fetch[j].wait()
            where = pl.ds(pl.multiple_of(starts[j] * cy, 32), counts[j] * cy)
            for t in range(kept + 1):
                at = t * counts[j]
                if j < 2:
                    mine, other = near_refs[j][t], near_buf[j, t]
                else:
                    source, first, second = held[j - 2]
                    mine = source[first + at : first + at + counts[j]]
                    other = far_other[second + at : second + at + counts[j]]
                mine = mine.reshape(counts[j] * cy, 128).astype(jnp.float32)
                other = other.reshape(counts[j] * cy, 128).astype(jnp.float32)
                if t < kept:
                    snap[2 * t + core, where, :] = mine
                    snap[2 * t + 1 - core, where, :] = other
                else:
                    scale[where, :] = 2.0 + (3.0 * taps[0]) * (mine + other)
                    gain[where, :] = taps[1] * (mine + other)

    for q in range(PACK):
        probe = begin + pl.program_id(0) * PACK + q
        low = bounds_ref[probes * par + probe, 0] - base
        high = bounds_ref[probes * par + probe, 1] - base
        for j in range(6):
            where = pl.ds(pl.multiple_of(starts[j] * cy, 32), counts[j] * cy)
            if j < 4:
                value = wide[j][probe].astype(jnp.float32)
            else:
                value = narrow[j - 4][pl.ds(probe * counts[j], counts[j])].astype(jnp.float32)
            plane = lax.broadcasted_iota(jnp.int32, value.shape, 0) + starts[j]
            value = jnp.where((plane >= low) & (plane < high), value, 0.0)
            pert[q, where, :] = value.reshape(counts[j] * cy, 128)

    def keep(q, slot, where, value):
        high = value.astype(jnp.bfloat16)
        low = (value - high.astype(jnp.float32)).astype(jnp.bfloat16)
        split[q, slot, where, 0:128] = high
        split[q, slot, where, 128:256] = low

    at = 0
    for m in spans(total):
        where = pl.ds(at * cy, m * cy)
        for q in range(PACK):
            first = pert[q, where, :] * snap[0, where, :]
            fields[q, 0, where, :] = first
            keep(q, 0, where, first)
        at += m

    def slab(row, count):
        if isinstance(row, int):
            return pl.ds(row * cy, count * cy)
        return pl.ds(pl.multiple_of(row * cy, 32), count * cy)

    def products(q, n, row, m):
        now = (n + 1) % 2
        both = jnp.dot(
            left_ref[0 : m * cy, 0 : (m + 8) * cy],
            split[q, now, slab(row - 4, m + 8), :],
            preferred_element_type=jnp.float32,
        )
        along = jnp.dot(split[q, now, slab(row, m), :], right_ref[...], preferred_element_type=jnp.float32)
        return both, along

    def advanced(q, n, row, m, both, along):
        now, before = (n + 1) % 2, n % 2
        where = slab(row, m)
        total_taps = both[:, 0:128] + both[:, 128:256] + along
        value = scale[where, :] * fields[q, now, where, :] + gain[where, :] * total_taps
        value = value + pert[q, where, :] * snap[n, where, :]
        if n > 1:
            value = value - fields[q, before, where, :]
        if n < steps - 1:
            fields[q, before, where, :] = value
            keep(q, before, where, value)
        elif row is starts[0]:
            own_ref[pl.program_id(0) * PACK + q] = value.reshape(rows, cy, 128)
        else:
            send_ref[pl.program_id(0) * PACK + q] = value.reshape(rows, cy, 128).astype(jnp.bfloat16)

    items = []
    for n in range(1, steps - 1):
        at = 4 * n
        for m in spans(total - 8 * n):
            items += [(q, n, at, m) for q in range(PACK)]
            at += m
    for row in starts[0:2]:
        items += [(q, steps - 1, row, rows) for q in range(PACK)]
    queue = []
    for item in items:
        queue.append((item, products(*item)))
        if len(queue) > AHEAD:
            first, made = queue.pop(0)
            advanced(*first, *made)
    for first, made in queue:
        advanced(*first, *made)


def propagate(bounds, operands, begin, count, steps, rows, halo):
    _, _, cy, cz = operands[0].shape
    total = 2 * rows + 2 * halo
    whole = pl.BlockSpec(memory_space=pltpu.VMEM)
    specs = [whole] * len(operands)
    outs = [((count, rows, cy, cz), jnp.float32), ((count, rows, cy, cz), jnp.bfloat16)]
    scratch = [
        pltpu.VMEM((PACK, total * cy, cz), jnp.float32),
        pltpu.VMEM((PACK, 2, total * cy, cz), jnp.float32),
        pltpu.VMEM((PACK, 2, total * cy, 2 * cz), jnp.bfloat16),
    ]
    if not begin:
        specs[8:10] = [pl.BlockSpec(memory_space=pl.ANY)] * 2
        outs += [
            ((steps + steps % 2, total * cy, cz), jnp.float32),
            ((total * cy, cz), jnp.float32),
            ((total * cy, cz), jnp.float32),
            ((SPAN * cy, (SPAN + 8) * cy), jnp.bfloat16),
            ((2 * cz, cz), jnp.bfloat16),
        ]
        scratch += [pltpu.VMEM((2, *operands[8].shape), jnp.bfloat16), pltpu.SemaphoreType.DMA((2,))]
    cells = count * total * cy * cz
    return pl.pallas_call(
        functools.partial(march, steps, rows, halo, begin),
        grid_spec=pltpu.PrefetchScalarGridSpec(
            num_scalar_prefetch=1,
            grid=(count // PACK,),
            in_specs=specs,
            out_specs=[whole] * len(outs),
            scratch_shapes=scratch,
        ),
        out_shape=[jax.ShapeDtypeStruct(*x) for x in outs],
        compiler_params=pltpu.CompilerParams(vmem_limit_bytes=16 << 20),
        cost_estimate=pl.CostEstimate(
            flops=cells * 8000 if begin else 0, bytes_accessed=cells * 4 if begin else 0, transcendentals=0
        ),
        name="march",
    )(bounds, *operands)


def local(probe_field, bounds, courant, snapshots, snap_times, basis_panels):
    probes_here, rows, cy, cz = probe_field.shape
    steps = snap_times.shape[0]
    half = probes_here // 2
    halo = 4 * (steps - 1)
    far = halo - rows
    devices = lax.axis_size("store")
    place = lax.axis_index("store")
    member = lax.axis_index("probe")
    members = lax.axis_size("probe")
    par = (place % 2).astype(jnp.int32)
    core = (member % 2).astype(jnp.int32)
    swap = [(i, i ^ 1) for i in range(devices)]
    perm_a = [(i, i - 2) for i in range(2, devices, 2)] + [(i, i + 2) for i in range(1, devices - 2, 2)]
    perm_b = [(i, i + 2) for i in range(0, devices - 2, 2)] + [(i, i - 2) for i in range(3, devices, 2)]
    hop = lambda x, pairs: lax.ppermute(x, "store", pairs)
    cores = lambda x: lax.ppermute(x, "probe", [(i, i ^ 1) for i in range(members)])
    cut = lambda x, start: lax.dynamic_slice_in_dim(x, start, far, axis=1)
    near = rows - far

    after = lambda x, *first: lax.optimization_barrier((x, *first))[0]
    trim = lambda x: jnp.concatenate([x[:far_half], x[near_half:]], axis=0)
    planes = lambda *xs: jnp.concatenate([x.reshape(-1, cy, cz) for x in xs], axis=0)
    near_half, far_half = shares(steps, rows, halo)

    mine = lax.dynamic_slice_in_dim(probe_field, half * par, half, axis=0)
    theirs = lax.dynamic_slice_in_dim(probe_field, half * (1 - par), half, axis=0)
    partner = hop(theirs, swap)

    slot = jnp.arange(2 * near_half)
    turn = 2 * (slot % near_half) + jnp.where(slot < near_half, core, 1 - core)
    order = jnp.sum(jnp.where(turn[:, None] == jnp.arange(steps), snap_times, 0), axis=1)
    ordered = jnp.take(after(snapshots, theirs), order, axis=0, mode="clip")
    joined, sent = ordered[:near_half], ordered[near_half:]
    gots = []
    span = 1
    while span < members:
        got = lax.ppermute(sent, "probe", [(i, i ^ span) for i in range(members)])
        upper = (member // span) % 2 == 1
        joined = jnp.concatenate([jnp.where(upper, got, joined), jnp.where(upper, joined, got)], axis=2)
        sent = joined
        gots.append(got)
        span *= 2
    high = lax.reduce_precision(courant, 8, 7)
    rate = jnp.where(core == 0, high, courant - high).astype(jnp.bfloat16)[None]
    extra = jnp.concatenate([joined, rate], axis=0)

    side_a = hop(after(mine, gots[0]), perm_a)
    side_b = hop(cut(after(mine, gots[-1]), near * (1 - par)), perm_b)
    extra_x = hop(after(extra, partner), swap)
    far_own, far_x = cut(trim(extra), near * (1 - par)), cut(trim(extra_x), near * par)
    turned = jnp.transpose(after(basis_panels, extra), (1, 2, 0, 3))
    crossed = lax.ppermute(turned, "probe", [(i, i ^ 2) for i in range(members)])
    message, turned = lax.optimization_barrier((planes(partner, extra_x, far_own), turned, side_b))[:2]
    side_c = hop(message, perm_b)
    side_d = hop(after(planes(cut(partner, near * par), extra, far_x), side_a), perm_a)
    far_other = cores(after(planes(side_c[half * rows :], side_d[half * far :]), crossed))
    operands = (mine, partner, side_a, side_b, side_c, side_d, extra, extra_x, cores(extra), cores(extra_x), far_other)
    first = par == 0
    own, back = [], []
    early = half * 2 // 3 // PACK * PACK
    for begin, count in ((0, early), (early, half - early)):
        kept, sent, *shared = propagate(bounds, operands, begin, count, steps, rows, halo)
        operands = (*operands[:6], *shared)
        own.append(kept)
        back.append(hop(sent, swap))
    panels = [turned, cores(turned), crossed, cores(crossed)]
    own = jnp.concatenate(own, axis=0)
    back = jnp.concatenate(back, axis=0)
    in_order = lambda x, y: jnp.concatenate([jnp.where(first, x, y), jnp.where(first, y, x)], axis=0)
    low = in_order(own.astype(jnp.bfloat16), back)
    parts = [
        lax.dot_general(x, low, (((0, 1, 3), (1, 2, 3)), ((), ())), preferred_element_type=jnp.float32)
        for x in panels
    ]
    rows_of = lambda q: functools.reduce(
        lambda kept, j: jnp.where(member == j, parts[q ^ j], kept), range(1, members), parts[q]
    )
    product = jnp.concatenate([rows_of(q) for q in range(members)], axis=0)
    response = in_order(own, back.astype(jnp.float32))
    span = 1
    while span < devices:
        product = product + hop(product, [(i, i ^ span) for i in range(devices)])
        span *= 2
    return response, product


def solution(mesh):
    placed = (
        P("probe", "store", None, None),
        P("probe", None),
        P("store", None, None),
        P(None, "store", "probe", None),
        P(),
        P("probe", "store", None, None),
    )
    return jax.shard_map(
        local,
        mesh=mesh,
        in_specs=placed,
        out_specs=(P("probe", "store", None, None), P(None, "probe")),
        check_vma=False,
    )
```

```python
import functools

import jax
import jax.numpy as jnp
import numpy as np
from jax import lax
from jax.experimental import pallas as pl
from jax.experimental.pallas import tpu as pltpu
from jax.sharding import PartitionSpec as P

taps = (-205.0 / 72.0, 8.0 / 5.0, -1.0 / 5.0, 8.0 / 315.0, -1.0 / 560.0)
SPAN = 24
PACK = 2
AHEAD = 1


def tables(cells_y, cells_z):
    def banded(apart, allowed):
        out = jnp.zeros(apart.shape, jnp.float32)
        for d in range(1, 5):
            out = jnp.where(allowed & (apart == d), taps[d] / taps[1], out)
        return out

    shape = (SPAN * cells_y, (SPAN + 8) * cells_y)
    row = lax.broadcasted_iota(jnp.int32, shape, 0)
    column = lax.broadcasted_iota(jnp.int32, shape, 1)
    planes = jnp.abs(column // cells_y - 4 - row // cells_y)
    lines = jnp.abs(column % cells_y - row % cells_y)
    left = banded(planes, lines == 0) + banded(lines, planes == 0)
    shape = (2 * cells_z, cells_z)
    row = lax.broadcasted_iota(jnp.int32, shape, 0) % cells_z
    apart = jnp.abs(row - lax.broadcasted_iota(jnp.int32, shape, 1))
    right = banded(apart, apart > 0)
    return left.astype(jnp.bfloat16), right.astype(jnp.bfloat16)


def spans(rows):
    out = []
    while rows > 0:
        out.append(min(SPAN, rows))
        rows -= out[-1]
    return out


def shares(steps, rows, halo):
    return (steps + 1) // 2, (-(-(halo - rows) // 4) + 1) // 2


def march(steps, rows, halo, begin, bounds_ref, *refs):
    wide, narrow = refs[0:4], refs[4:6]
    c_ref, d_ref = narrow
    near_refs = refs[6:8]
    near_others = refs[8:10]
    far_other, own_ref, send_ref = refs[10:13]
    pert, snap, scale, gain, fields, split, left_ref, right_ref, a_buf, b_buf, sems = refs[13:24]
    count = a_buf.shape[0]
    fetch = [
        pltpu.make_async_copy(wide[j].at[pl.ds(begin, count)], buf, sems.at[j - 2])
        for j, buf in ((2, a_buf), (3, b_buf))
    ]
    total = 2 * rows + 2 * halo
    cy = 8
    far = halo - rows
    place = lax.axis_index("store")
    par, core = place % 2, lax.axis_index("probe") % 2
    base = (place // 2) * 2 * rows - halo
    probes = wide[0].shape[0]
    even = (halo, halo + rows, halo + 2 * rows, 0, halo - rows, halo + 3 * rows)
    odd = (halo + rows, halo, halo - rows, halo + 3 * rows, halo + 2 * rows, 0)
    counts = (rows, rows, rows, far, rows, far)
    starts = [e + par * (o - e) for e, o in zip(even, odd)]
    near_half, far_half = shares(steps, rows, halo)

    @pl.when(pl.program_id(0) == 0)
    def _():
        for copy in fetch:
            copy.start()
        left_ref[...], right_ref[...] = tables(cy, 128)
        near_size, far_size = (near_half + 1) * rows, (far_half + 1) * far
        c_base = c_ref.shape[0] - near_size - far_size
        d_base = d_ref.shape[0] - near_size - far_size
        held = (
            (d_ref, d_base, near_size + far_size),
            (c_ref, c_base + near_size, near_size),
            (c_ref, c_base, 0),
            (d_ref, d_base + near_size, 2 * near_size + far_size),
        )
        for j in range(6):
            kept = far_half if j in (3, 5) else near_half
            where = pl.ds(pl.multiple_of(starts[j] * cy, 32), counts[j] * cy)
            for t in range(kept + 1):
                at = t * counts[j]
                if j < 2:
                    mine, other = near_refs[j][t], near_others[j][t]
                else:
                    source, first, second = held[j - 2]
                    mine = source[first + at : first + at + counts[j]]
                    other = far_other[second + at : second + at + counts[j]]
                mine = mine.reshape(counts[j] * cy, 128).astype(jnp.float32)
                other = other.reshape(counts[j] * cy, 128).astype(jnp.float32)
                if t < kept:
                    snap[2 * t + core, where, :] = mine
                    snap[2 * t + 1 - core, where, :] = other
                else:
                    scale[where, :] = 2.0 + (3.0 * taps[0]) * (mine + other)
                    gain[where, :] = taps[1] * (mine + other)

        for copy in fetch:
            copy.wait()

    for q in range(PACK):
        probe = begin + pl.program_id(0) * PACK + q
        low = bounds_ref[probes * par + probe, 0] - base
        high = bounds_ref[probes * par + probe, 1] - base
        for j in range(6):
            where = pl.ds(pl.multiple_of(starts[j] * cy, 32), counts[j] * cy)
            if j < 2:
                value = wide[j][probe].astype(jnp.float32)
            elif j < 4:
                value = (a_buf, b_buf)[j - 2][probe - begin].astype(jnp.float32)
            else:
                value = narrow[j - 4][pl.ds(probe * counts[j], counts[j])].astype(jnp.float32)
            plane = lax.broadcasted_iota(jnp.int32, value.shape, 0) + starts[j]
            value = jnp.where((plane >= low) & (plane < high), value, 0.0)
            pert[q, where, :] = value.reshape(counts[j] * cy, 128)

    def keep(q, slot, where, value):
        high = value.astype(jnp.bfloat16)
        low = (value - high.astype(jnp.float32)).astype(jnp.bfloat16)
        split[q, slot, where, 0:128] = high
        split[q, slot, where, 128:256] = low

    at = 0
    for m in spans(total):
        where = pl.ds(at * cy, m * cy)
        for q in range(PACK):
            first = pert[q, where, :] * snap[0, where, :]
            fields[q, 0, where, :] = first
            keep(q, 0, where, first)
        at += m

    def slab(row, count):
        if isinstance(row, int):
            return pl.ds(row * cy, count * cy)
        return pl.ds(pl.multiple_of(row * cy, 32), count * cy)

    def products(q, n, row, m):
        now = (n + 1) % 2
        both = jnp.dot(
            left_ref[0 : m * cy, 0 : (m + 8) * cy],
            split[q, now, slab(row - 4, m + 8), :],
            preferred_element_type=jnp.float32,
        )
        along = jnp.dot(split[q, now, slab(row, m), :], right_ref[...], preferred_element_type=jnp.float32)
        return both, along

    def advanced(q, n, row, m, both, along):
        now, before = (n + 1) % 2, n % 2
        where = slab(row, m)
        total_taps = both[:, 0:128] + both[:, 128:256] + along
        value = scale[where, :] * fields[q, now, where, :] + gain[where, :] * total_taps
        value = value + pert[q, where, :] * snap[n, where, :]
        if n > 1:
            value = value - fields[q, before, where, :]
        if n < steps - 1:
            fields[q, before, where, :] = value
            keep(q, before, where, value)
        elif row is starts[0]:
            own_ref[pl.program_id(0) * PACK + q] = value.reshape(rows, cy, 128)
        else:
            send_ref[pl.program_id(0) * PACK + q] = value.reshape(rows, cy, 128).astype(jnp.bfloat16)

    items = []
    for n in range(1, steps - 1):
        at = 4 * n
        for m in spans(total - 8 * n):
            items += [(q, n, at, m) for q in range(PACK)]
            at += m
    for row in starts[0:2]:
        items += [(q, steps - 1, row, rows) for q in range(PACK)]
    queue = []
    for item in items:
        queue.append((item, products(*item)))
        if len(queue) > AHEAD:
            first, made = queue.pop(0)
            advanced(*first, *made)
    for first, made in queue:
        advanced(*first, *made)


def propagate(bounds, operands, begin, count, steps, rows, halo):
    _, _, cy, cz = operands[0].shape
    total = 2 * rows + 2 * halo
    whole = pl.BlockSpec(memory_space=pltpu.VMEM)
    grid_spec = pltpu.PrefetchScalarGridSpec(
        num_scalar_prefetch=1,
        grid=(count // PACK,),
        in_specs=[whole] * 2 + [pl.BlockSpec(memory_space=pltpu.HBM)] * 2 + [whole] * (len(operands) - 4),
        out_specs=[whole, whole],
        scratch_shapes=[
            pltpu.VMEM((PACK, total * cy, cz), jnp.float32),
            pltpu.VMEM((steps + steps % 2, total * cy, cz), jnp.float32),
            pltpu.VMEM((total * cy, cz), jnp.float32),
            pltpu.VMEM((total * cy, cz), jnp.float32),
            pltpu.VMEM((PACK, 2, total * cy, cz), jnp.float32),
            pltpu.VMEM((PACK, 2, total * cy, 2 * cz), jnp.bfloat16),
            pltpu.VMEM((SPAN * cy, (SPAN + 8) * cy), jnp.bfloat16),
            pltpu.VMEM((2 * cz, cz), jnp.bfloat16),
            pltpu.VMEM((count, rows, cy, cz), jnp.bfloat16),
            pltpu.VMEM((count, halo - rows, cy, cz), jnp.bfloat16),
            pltpu.SemaphoreType.DMA((2,)),
        ],
    )
    cells = count * total * cy * cz
    return pl.pallas_call(
        functools.partial(march, steps, rows, halo, begin),
        grid_spec=grid_spec,
        out_shape=[
            jax.ShapeDtypeStruct((count, rows, cy, cz), jnp.float32),
            jax.ShapeDtypeStruct((count, rows, cy, cz), jnp.bfloat16),
        ],
        compiler_params=pltpu.CompilerParams(vmem_limit_bytes=16 << 20),
        cost_estimate=pl.CostEstimate(flops=cells * 8000 if begin else 0, bytes_accessed=cells * 4 if begin else 0, transcendentals=0),
        name="march",
    )(bounds, *operands)


def local(probe_field, bounds, courant, snapshots, snap_times, basis_panels):
    probes_here, rows, cy, cz = probe_field.shape
    steps = snap_times.shape[0]
    half = probes_here // 2
    halo = 4 * (steps - 1)
    far = halo - rows
    devices = lax.axis_size("store")
    place = lax.axis_index("store")
    member = lax.axis_index("probe")
    members = lax.axis_size("probe")
    par = (place % 2).astype(jnp.int32)
    core = (member % 2).astype(jnp.int32)
    swap = [(i, i ^ 1) for i in range(devices)]
    perm_a = [(i, i - 2) for i in range(2, devices, 2)] + [(i, i + 2) for i in range(1, devices - 2, 2)]
    perm_b = [(i, i + 2) for i in range(0, devices - 2, 2)] + [(i, i - 2) for i in range(3, devices, 2)]
    hop = lambda x, pairs: lax.ppermute(x, "store", pairs)
    cores = lambda x: lax.ppermute(x, "probe", [(i, i ^ 1) for i in range(members)])
    cut = lambda x, start: lax.dynamic_slice_in_dim(x, start, far, axis=1)
    near = rows - far

    after = lambda x, *first: lax.optimization_barrier((x, *first))[0]
    trim = lambda x: jnp.concatenate([x[:far_half], x[near_half:]], axis=0)
    planes = lambda *xs: jnp.concatenate([x.reshape(-1, cy, cz) for x in xs], axis=0)
    near_half, far_half = shares(steps, rows, halo)

    mine = lax.dynamic_slice_in_dim(probe_field, half * par, half, axis=0)
    theirs = lax.dynamic_slice_in_dim(probe_field, half * (1 - par), half, axis=0)
    partner = hop(theirs, swap)

    slot = jnp.arange(2 * near_half)
    turn = 2 * (slot % near_half) + jnp.where(slot < near_half, core, 1 - core)
    order = jnp.sum(jnp.where(turn[:, None] == jnp.arange(steps), snap_times, 0), axis=1)
    ordered = jnp.take(after(snapshots, theirs), order, axis=0, mode="clip")
    joined, sent = ordered[:near_half], ordered[near_half:]
    gots = []
    span = 1
    while span < members:
        got = lax.ppermute(sent, "probe", [(i, i ^ span) for i in range(members)])
        upper = (member // span) % 2 == 1
        joined = jnp.concatenate([jnp.where(upper, got, joined), jnp.where(upper, joined, got)], axis=2)
        sent = joined
        gots.append(got)
        span *= 2
    high = lax.reduce_precision(courant, 8, 7)
    rate = jnp.where(core == 0, high, courant - high).astype(jnp.bfloat16)[None]
    extra = jnp.concatenate([joined, rate], axis=0)

    side_a = hop(after(mine, gots[0]), perm_a)
    side_b = hop(cut(after(mine, gots[-1]), near * (1 - par)), perm_b)
    extra_x = hop(extra, swap)
    far_own, far_x = cut(trim(extra), near * (1 - par)), cut(trim(extra_x), near * par)
    turned = jnp.transpose(after(basis_panels, extra), (1, 2, 0, 3))
    crossed = lax.ppermute(turned, "probe", [(i, i ^ 2) for i in range(members)])
    message, turned = lax.optimization_barrier((planes(partner, extra_x, far_own), turned, side_b))[:2]
    side_c = hop(message, perm_b)
    side_d = hop(after(planes(cut(partner, near * par), extra, far_x), side_a), perm_a)
    far_other = cores(after(planes(side_c[half * rows :], side_d[half * far :]), crossed))
    operands = (mine, partner, side_a, side_b, side_c, side_d, extra, extra_x, cores(extra), cores(extra_x), far_other)
    first = par == 0
    own, back = [], []
    early = half * 2 // 3 // PACK * PACK
    for begin, count in ((0, early), (early, half - early)):
        kept, sent = propagate(bounds, operands, begin, count, steps, rows, halo)
        own.append(kept)
        back.append(hop(sent, swap))
    panels = [turned, cores(turned), crossed, cores(crossed)]
    own = jnp.concatenate(own, axis=0)
    back = jnp.concatenate(back, axis=0)
    in_order = lambda x, y: jnp.concatenate([jnp.where(first, x, y), jnp.where(first, y, x)], axis=0)
    low = in_order(own.astype(jnp.bfloat16), back)
    parts = [
        lax.dot_general(x, low, (((0, 1, 3), (1, 2, 3)), ((), ())), preferred_element_type=jnp.float32)
        for x in panels
    ]
    rows_of = lambda q: functools.reduce(
        lambda kept, j: jnp.where(member == j, parts[q ^ j], kept), range(1, members), parts[q]
    )
    product = jnp.concatenate([rows_of(q) for q in range(members)], axis=0)
    response = in_order(own, back.astype(jnp.float32))
    span = 1
    while span < devices:
        product = product + hop(product, [(i, i ^ span) for i in range(devices)])
        span *= 2
    return response, product


def solution(mesh):
    placed = (
        P("probe", "store", None, None),
        P("probe", None),
        P("store", None, None),
        P(None, "store", "probe", None),
        P(),
        P("probe", "store", None, None),
    )
    return jax.shard_map(
        local,
        mesh=mesh,
        in_specs=placed,
        out_specs=(P("probe", "store", None, None), P(None, "probe")),
        check_vma=False,
    )
```

```python
import functools

import jax
import jax.numpy as jnp
import numpy as np
from jax import lax
from jax.experimental import pallas as pl
from jax.experimental.pallas import tpu as pltpu
from jax.sharding import PartitionSpec as P

taps = (-205.0 / 72.0, 8.0 / 5.0, -1.0 / 5.0, 8.0 / 315.0, -1.0 / 560.0)
SPAN = 24
PACK = 4
AHEAD = 1


def tables(cells_y, cells_z):
    def banded(apart, allowed):
        out = jnp.zeros(apart.shape, jnp.float32)
        for d in range(1, 5):
            out = jnp.where(allowed & (apart == d), taps[d] / taps[1], out)
        return out

    shape = (SPAN * cells_y, (SPAN + 8) * cells_y)
    row = lax.broadcasted_iota(jnp.int32, shape, 0)
    column = lax.broadcasted_iota(jnp.int32, shape, 1)
    planes = jnp.abs(column // cells_y - 4 - row // cells_y)
    lines = jnp.abs(column % cells_y - row % cells_y)
    left = banded(planes, lines == 0) + banded(lines, planes == 0)
    shape = (2 * cells_z, cells_z)
    row = lax.broadcasted_iota(jnp.int32, shape, 0) % cells_z
    apart = jnp.abs(row - lax.broadcasted_iota(jnp.int32, shape, 1))
    right = banded(apart, apart > 0)
    return left.astype(jnp.bfloat16), right.astype(jnp.bfloat16)


def spans(rows):
    out = []
    while rows > 0:
        out.append(min(SPAN, rows))
        rows -= out[-1]
    return out


def shares(steps, rows, halo):
    return (steps + 1) // 2, (-(-(halo - rows) // 4) + 1) // 2


def march(steps, rows, halo, begin, bounds_ref, *refs):
    wide, narrow = refs[0:4], refs[4:6]
    c_ref, d_ref = narrow
    near_refs = refs[6:8]
    near_others = refs[8:10]
    far_other, own_ref, send_ref = refs[10:13]
    pert, snap, scale, gain, fields, split, left_ref, right_ref, a_buf, b_buf, sems = refs[13:24]
    count = a_buf.shape[0]
    fetch = [
        pltpu.make_async_copy(wide[j].at[pl.ds(begin, count)], buf, sems.at[j - 2])
        for j, buf in ((2, a_buf), (3, b_buf))
    ]
    total = 2 * rows + 2 * halo
    cy = 8
    far = halo - rows
    place = lax.axis_index("store")
    par, core = place % 2, lax.axis_index("probe") % 2
    base = (place // 2) * 2 * rows - halo
    probes = wide[0].shape[0]
    even = (halo, halo + rows, halo + 2 * rows, 0, halo - rows, halo + 3 * rows)
    odd = (halo + rows, halo, halo - rows, halo + 3 * rows, halo + 2 * rows, 0)
    counts = (rows, rows, rows, far, rows, far)
    starts = [e + par * (o - e) for e, o in zip(even, odd)]
    near_half, far_half = shares(steps, rows, halo)

    @pl.when(pl.program_id(0) == 0)
    def _():
        for copy in fetch:
            copy.start()
        left_ref[...], right_ref[...] = tables(cy, 128)
        near_size, far_size = (near_half + 1) * rows, (far_half + 1) * far
        c_base = c_ref.shape[0] - near_size - far_size
        d_base = d_ref.shape[0] - near_size - far_size
        held = (
            (d_ref, d_base, near_size + far_size),
            (c_ref, c_base + near_size, near_size),
            (c_ref, c_base, 0),
            (d_ref, d_base + near_size, 2 * near_size + far_size),
        )
        for j in range(6):
            kept = far_half if j in (3, 5) else near_half
            where = pl.ds(pl.multiple_of(starts[j] * cy, 32), counts[j] * cy)
            for t in range(kept + 1):
                at = t * counts[j]
                if j < 2:
                    mine, other = near_refs[j][t], near_others[j][t]
                else:
                    source, first, second = held[j - 2]
                    mine = source[first + at : first + at + counts[j]]
                    other = far_other[second + at : second + at + counts[j]]
                mine = mine.reshape(counts[j] * cy, 128).astype(jnp.float32)
                other = other.reshape(counts[j] * cy, 128).astype(jnp.float32)
                if t < kept:
                    snap[2 * t + core, where, :] = mine
                    snap[2 * t + 1 - core, where, :] = other
                else:
                    scale[where, :] = 2.0 + (3.0 * taps[0]) * (mine + other)
                    gain[where, :] = taps[1] * (mine + other)

        for copy in fetch:
            copy.wait()

    for q in range(PACK):
        probe = begin + pl.program_id(0) * PACK + q
        low = bounds_ref[probes * par + probe, 0] - base
        high = bounds_ref[probes * par + probe, 1] - base
        for j in range(6):
            where = pl.ds(pl.multiple_of(starts[j] * cy, 32), counts[j] * cy)
            if j < 2:
                value = wide[j][probe].astype(jnp.float32)
            elif j < 4:
                value = (a_buf, b_buf)[j - 2][probe - begin].astype(jnp.float32)
            else:
                value = narrow[j - 4][pl.ds(probe * counts[j], counts[j])].astype(jnp.float32)
            plane = lax.broadcasted_iota(jnp.int32, value.shape, 0) + starts[j]
            value = jnp.where((plane >= low) & (plane < high), value, 0.0)
            pert[q, where, :] = value.reshape(counts[j] * cy, 128)

    def keep(q, slot, where, value):
        high = value.astype(jnp.bfloat16)
        low = (value - high.astype(jnp.float32)).astype(jnp.bfloat16)
        split[q, slot, where, 0:128] = high
        split[q, slot, where, 128:256] = low

    at = 0
    for m in spans(total):
        where = pl.ds(at * cy, m * cy)
        for q in range(PACK):
            first = pert[q, where, :] * snap[0, where, :]
            fields[q, 0, where, :] = first
            keep(q, 0, where, first)
        at += m

    def slab(row, count):
        if isinstance(row, int):
            return pl.ds(row * cy, count * cy)
        return pl.ds(pl.multiple_of(row * cy, 32), count * cy)

    def products(q, n, row, m):
        now = (n + 1) % 2
        both = jnp.dot(
            left_ref[0 : m * cy, 0 : (m + 8) * cy],
            split[q, now, slab(row - 4, m + 8), :],
            preferred_element_type=jnp.float32,
        )
        along = jnp.dot(split[q, now, slab(row, m), :], right_ref[...], preferred_element_type=jnp.float32)
        return both, along

    def advanced(q, n, row, m, both, along):
        now, before = (n + 1) % 2, n % 2
        where = slab(row, m)
        total_taps = both[:, 0:128] + both[:, 128:256] + along
        value = scale[where, :] * fields[q, now, where, :] + gain[where, :] * total_taps
        value = value + pert[q, where, :] * snap[n, where, :]
        if n > 1:
            value = value - fields[q, before, where, :]
        if n < steps - 1:
            fields[q, before, where, :] = value
            keep(q, before, where, value)
        elif row is starts[0]:
            own_ref[pl.program_id(0) * PACK + q] = value.reshape(rows, cy, 128)
        else:
            send_ref[pl.program_id(0) * PACK + q] = value.reshape(rows, cy, 128).astype(jnp.bfloat16)

    items = []
    for n in range(1, steps - 1):
        at = 4 * n
        for m in spans(total - 8 * n):
            items += [(q, n, at, m) for q in range(PACK)]
            at += m
    for row in starts[0:2]:
        items += [(q, steps - 1, row, rows) for q in range(PACK)]
    queue = []
    for item in items:
        queue.append((item, products(*item)))
        if len(queue) > AHEAD:
            first, made = queue.pop(0)
            advanced(*first, *made)
    for first, made in queue:
        advanced(*first, *made)


def propagate(bounds, operands, begin, count, steps, rows, halo):
    _, _, cy, cz = operands[0].shape
    total = 2 * rows + 2 * halo
    whole = pl.BlockSpec(memory_space=pltpu.VMEM)
    grid_spec = pltpu.PrefetchScalarGridSpec(
        num_scalar_prefetch=1,
        grid=(count // PACK,),
        in_specs=[whole] * 2 + [pl.BlockSpec(memory_space=pltpu.HBM)] * 2 + [whole] * (len(operands) - 4),
        out_specs=[whole, whole],
        scratch_shapes=[
            pltpu.VMEM((PACK, total * cy, cz), jnp.float32),
            pltpu.VMEM((steps + steps % 2, total * cy, cz), jnp.float32),
            pltpu.VMEM((total * cy, cz), jnp.float32),
            pltpu.VMEM((total * cy, cz), jnp.float32),
            pltpu.VMEM((PACK, 2, total * cy, cz), jnp.float32),
            pltpu.VMEM((PACK, 2, total * cy, 2 * cz), jnp.bfloat16),
            pltpu.VMEM((SPAN * cy, (SPAN + 8) * cy), jnp.bfloat16),
            pltpu.VMEM((2 * cz, cz), jnp.bfloat16),
            pltpu.VMEM((count, rows, cy, cz), jnp.bfloat16),
            pltpu.VMEM((count, halo - rows, cy, cz), jnp.bfloat16),
            pltpu.SemaphoreType.DMA((2,)),
        ],
    )
    cells = count * total * cy * cz
    return pl.pallas_call(
        functools.partial(march, steps, rows, halo, begin),
        grid_spec=grid_spec,
        out_shape=[
            jax.ShapeDtypeStruct((count, rows, cy, cz), jnp.float32),
            jax.ShapeDtypeStruct((count, rows, cy, cz), jnp.bfloat16),
        ],
        compiler_params=pltpu.CompilerParams(vmem_limit_bytes=16 << 20),
        cost_estimate=pl.CostEstimate(flops=cells * 8000 if begin else 0, bytes_accessed=cells * 4 if begin else 0, transcendentals=0),
        name="march",
    )(bounds, *operands)


def local(probe_field, bounds, courant, snapshots, snap_times, basis_panels):
    probes_here, rows, cy, cz = probe_field.shape
    steps = snap_times.shape[0]
    half = probes_here // 2
    halo = 4 * (steps - 1)
    far = halo - rows
    devices = lax.axis_size("store")
    place = lax.axis_index("store")
    member = lax.axis_index("probe")
    members = lax.axis_size("probe")
    par = (place % 2).astype(jnp.int32)
    core = (member % 2).astype(jnp.int32)
    swap = [(i, i ^ 1) for i in range(devices)]
    perm_a = [(i, i - 2) for i in range(2, devices, 2)] + [(i, i + 2) for i in range(1, devices - 2, 2)]
    perm_b = [(i, i + 2) for i in range(0, devices - 2, 2)] + [(i, i - 2) for i in range(3, devices, 2)]
    hop = lambda x, pairs: lax.ppermute(x, "store", pairs)
    cores = lambda x: lax.ppermute(x, "probe", [(i, i ^ 1) for i in range(members)])
    cut = lambda x, start: lax.dynamic_slice_in_dim(x, start, far, axis=1)
    near = rows - far

    after = lambda x, *first: lax.optimization_barrier((x, *first))[0]
    trim = lambda x: jnp.concatenate([x[:far_half], x[near_half:]], axis=0)
    planes = lambda *xs: jnp.concatenate([x.reshape(-1, cy, cz) for x in xs], axis=0)
    near_half, far_half = shares(steps, rows, halo)

    mine = lax.dynamic_slice_in_dim(probe_field, half * par, half, axis=0)
    theirs = lax.dynamic_slice_in_dim(probe_field, half * (1 - par), half, axis=0)
    partner = hop(theirs, swap)

    slot = jnp.arange(2 * near_half)
    turn = 2 * (slot % near_half) + jnp.where(slot < near_half, core, 1 - core)
    order = jnp.sum(jnp.where(turn[:, None] == jnp.arange(steps), snap_times, 0), axis=1)
    ordered = jnp.take(after(snapshots, theirs), order, axis=0, mode="clip")
    joined, sent = ordered[:near_half], ordered[near_half:]
    gots = []
    span = 1
    while span < members:
        got = lax.ppermute(sent, "probe", [(i, i ^ span) for i in range(members)])
        upper = (member // span) % 2 == 1
        joined = jnp.concatenate([jnp.where(upper, got, joined), jnp.where(upper, joined, got)], axis=2)
        sent = joined
        gots.append(got)
        span *= 2
    high = lax.reduce_precision(courant, 8, 7)
    rate = jnp.where(core == 0, high, courant - high).astype(jnp.bfloat16)[None]
    extra = jnp.concatenate([joined, rate], axis=0)

    side_a = hop(after(mine, gots[0]), perm_a)
    side_b = hop(cut(after(mine, gots[-1]), near * (1 - par)), perm_b)
    extra_x = hop(extra, swap)
    far_own, far_x = cut(trim(extra), near * (1 - par)), cut(trim(extra_x), near * par)
    turned = jnp.transpose(after(basis_panels, extra), (1, 2, 0, 3))
    crossed = lax.ppermute(turned, "probe", [(i, i ^ 2) for i in range(members)])
    message, turned = lax.optimization_barrier((planes(partner, extra_x, far_own), turned, side_b))[:2]
    side_c = hop(message, perm_b)
    side_d = hop(after(planes(cut(partner, near * par), extra, far_x), side_a), perm_a)
    far_other = cores(after(planes(side_c[half * rows :], side_d[half * far :]), crossed))
    operands = (mine, partner, side_a, side_b, side_c, side_d, extra, extra_x, cores(extra), cores(extra_x), far_other)
    first = par == 0
    own, back = [], []
    early = half * 2 // 3 // PACK * PACK
    for begin, count in ((0, early), (early, half - early)):
        kept, sent = propagate(bounds, operands, begin, count, steps, rows, halo)
        own.append(kept)
        back.append(hop(sent, swap))
    panels = [turned, cores(turned), crossed, cores(crossed)]
    own = jnp.concatenate(own, axis=0)
    back = jnp.concatenate(back, axis=0)
    in_order = lambda x, y: jnp.concatenate([jnp.where(first, x, y), jnp.where(first, y, x)], axis=0)
    low = in_order(own.astype(jnp.bfloat16), back)
    parts = [
        lax.dot_general(x, low, (((0, 1, 3), (1, 2, 3)), ((), ())), preferred_element_type=jnp.float32)
        for x in panels
    ]
    rows_of = lambda q: functools.reduce(
        lambda kept, j: jnp.where(member == j, parts[q ^ j], kept), range(1, members), parts[q]
    )
    product = jnp.concatenate([rows_of(q) for q in range(members)], axis=0)
    response = in_order(own, back.astype(jnp.float32))
    span = 1
    while span < devices:
        product = product + hop(product, [(i, i ^ span) for i in range(devices)])
        span *= 2
    return response, product


def solution(mesh):
    placed = (
        P("probe", "store", None, None),
        P("probe", None),
        P("store", None, None),
        P(None, "store", "probe", None),
        P(),
        P("probe", "store", None, None),
    )
    return jax.shard_map(
        local,
        mesh=mesh,
        in_specs=placed,
        out_specs=(P("probe", "store", None, None), P(None, "probe")),
        check_vma=False,
    )
```

```python
import functools

import jax
import jax.numpy as jnp
import numpy as np
from jax import lax
from jax.experimental import pallas as pl
from jax.experimental.pallas import tpu as pltpu
from jax.sharding import PartitionSpec as P

taps = (-205.0 / 72.0, 8.0 / 5.0, -1.0 / 5.0, 8.0 / 315.0, -1.0 / 560.0)
SPAN = 24
PACK = 4
AHEAD = 1


def tables(cells_y, cells_z):
    def banded(apart, allowed):
        out = jnp.zeros(apart.shape, jnp.float32)
        for d in range(1, 5):
            out = jnp.where(allowed & (apart == d), taps[d] / taps[1], out)
        return out

    shape = (SPAN * cells_y, (SPAN + 8) * cells_y)
    row = lax.broadcasted_iota(jnp.int32, shape, 0)
    column = lax.broadcasted_iota(jnp.int32, shape, 1)
    planes = jnp.abs(column // cells_y - 4 - row // cells_y)
    lines = jnp.abs(column % cells_y - row % cells_y)
    left = banded(planes, lines == 0) + banded(lines, planes == 0)
    shape = (2 * cells_z, cells_z)
    row = lax.broadcasted_iota(jnp.int32, shape, 0) % cells_z
    apart = jnp.abs(row - lax.broadcasted_iota(jnp.int32, shape, 1))
    right = banded(apart, apart > 0)
    return left.astype(jnp.bfloat16), right.astype(jnp.bfloat16)


def spans(rows):
    out = []
    while rows > 0:
        out.append(min(SPAN, rows))
        rows -= out[-1]
    return out


def shares(steps, rows, halo):
    return (steps + 1) // 2, (-(-(halo - rows) // 4) + 1) // 2


def march(steps, rows, halo, begin, bounds_ref, *refs):
    wide, narrow = refs[0:4], refs[4:6]
    c_ref, d_ref = narrow
    near_refs = refs[6:8]
    near_others = refs[8:10]
    far_other, own_ref, send_ref = refs[10:13]
    pert, snap, scale, gain, fields, split, left_ref, right_ref, a_buf, b_buf, sems = refs[13:24]
    count = a_buf.shape[0]
    fetch = [
        pltpu.make_async_copy(wide[j].at[pl.ds(begin, count)], buf, sems.at[j - 2])
        for j, buf in ((2, a_buf), (3, b_buf))
    ]
    total = 2 * rows + 2 * halo
    cy = 8
    far = halo - rows
    place = lax.axis_index("store")
    par, core = place % 2, lax.axis_index("probe") % 2
    base = (place // 2) * 2 * rows - halo
    probes = wide[0].shape[0]
    even = (halo, halo + rows, halo + 2 * rows, 0, halo - rows, halo + 3 * rows)
    odd = (halo + rows, halo, halo - rows, halo + 3 * rows, halo + 2 * rows, 0)
    counts = (rows, rows, rows, far, rows, far)
    starts = [e + par * (o - e) for e, o in zip(even, odd)]
    near_half, far_half = shares(steps, rows, halo)

    @pl.when(pl.program_id(0) == 0)
    def _():
        for copy in fetch:
            copy.start()
        left_ref[...], right_ref[...] = tables(cy, 128)
        near_size, far_size = (near_half + 1) * rows, (far_half + 1) * far
        c_base = c_ref.shape[0] - near_size - far_size
        d_base = d_ref.shape[0] - near_size - far_size
        held = (
            (d_ref, d_base, near_size + far_size),
            (c_ref, c_base + near_size, near_size),
            (c_ref, c_base, 0),
            (d_ref, d_base + near_size, 2 * near_size + far_size),
        )
        for j in range(6):
            kept = far_half if j in (3, 5) else near_half
            where = pl.ds(pl.multiple_of(starts[j] * cy, 32), counts[j] * cy)
            for t in range(kept + 1):
                at = t * counts[j]
                if j < 2:
                    mine, other = near_refs[j][t], near_others[j][t]
                else:
                    source, first, second = held[j - 2]
                    mine = source[first + at : first + at + counts[j]]
                    other = far_other[second + at : second + at + counts[j]]
                mine = mine.reshape(counts[j] * cy, 128).astype(jnp.float32)
                other = other.reshape(counts[j] * cy, 128).astype(jnp.float32)
                if t < kept:
                    snap[2 * t + core, where, :] = mine
                    snap[2 * t + 1 - core, where, :] = other
                else:
                    scale[where, :] = 2.0 + (3.0 * taps[0]) * (mine + other)
                    gain[where, :] = taps[1] * (mine + other)

        for copy in fetch:
            copy.wait()

    for q in range(PACK):
        probe = begin + pl.program_id(0) * PACK + q
        low = bounds_ref[probes * par + probe, 0] - base
        high = bounds_ref[probes * par + probe, 1] - base
        for j in range(6):
            where = pl.ds(pl.multiple_of(starts[j] * cy, 32), counts[j] * cy)
            if j < 2:
                value = wide[j][probe].astype(jnp.float32)
            elif j < 4:
                value = (a_buf, b_buf)[j - 2][probe - begin].astype(jnp.float32)
            else:
                value = narrow[j - 4][pl.ds(probe * counts[j], counts[j])].astype(jnp.float32)
            plane = lax.broadcasted_iota(jnp.int32, value.shape, 0) + starts[j]
            value = jnp.where((plane >= low) & (plane < high), value, 0.0)
            pert[q, where, :] = value.reshape(counts[j] * cy, 128)

    def keep(q, slot, where, value):
        high = value.astype(jnp.bfloat16)
        low = (value - high.astype(jnp.float32)).astype(jnp.bfloat16)
        split[q, slot, where, 0:128] = high
        split[q, slot, where, 128:256] = low

    at = 0
    for m in spans(total):
        where = pl.ds(at * cy, m * cy)
        for q in range(PACK):
            first = pert[q, where, :] * snap[0, where, :]
            fields[q, 0, where, :] = first
            keep(q, 0, where, first)
        at += m

    def slab(row, count):
        if isinstance(row, int):
            return pl.ds(row * cy, count * cy)
        return pl.ds(pl.multiple_of(row * cy, 32), count * cy)

    def products(q, n, row, m):
        now = (n + 1) % 2
        both = jnp.dot(
            left_ref[0 : m * cy, 0 : (m + 8) * cy],
            split[q, now, slab(row - 4, m + 8), :],
            preferred_element_type=jnp.float32,
        )
        along = jnp.dot(split[q, now, slab(row, m), :], right_ref[...], preferred_element_type=jnp.float32)
        return both, along

    def advanced(q, n, row, m, both, along):
        now, before = (n + 1) % 2, n % 2
        where = slab(row, m)
        total_taps = both[:, 0:128] + both[:, 128:256] + along
        value = scale[where, :] * fields[q, now, where, :] + gain[where, :] * total_taps
        value = value + pert[q, where, :] * snap[n, where, :]
        if n > 1:
            value = value - fields[q, before, where, :]
        if n < steps - 1:
            fields[q, before, where, :] = value
            keep(q, before, where, value)
        elif row is starts[0]:
            own_ref[pl.program_id(0) * PACK + q] = value.reshape(rows, cy, 128)
        else:
            send_ref[pl.program_id(0) * PACK + q] = value.reshape(rows, cy, 128).astype(jnp.bfloat16)

    items = []
    for n in range(1, steps - 1):
        at = 4 * n
        for m in spans(total - 8 * n):
            items += [(q, n, at, m) for q in range(PACK)]
            at += m
    for row in starts[0:2]:
        items += [(q, steps - 1, row, rows) for q in range(PACK)]
    queue = []
    for item in items:
        queue.append((item, products(*item)))
        if len(queue) > AHEAD:
            first, made = queue.pop(0)
            advanced(*first, *made)
    for first, made in queue:
        advanced(*first, *made)


def propagate(bounds, operands, begin, count, steps, rows, halo):
    _, _, cy, cz = operands[0].shape
    total = 2 * rows + 2 * halo
    whole = pl.BlockSpec(memory_space=pltpu.VMEM)
    grid_spec = pltpu.PrefetchScalarGridSpec(
        num_scalar_prefetch=1,
        grid=(count // PACK,),
        in_specs=[whole] * 2 + [pl.BlockSpec(memory_space=pltpu.HBM)] * 2 + [whole] * (len(operands) - 4),
        out_specs=[whole, whole],
        scratch_shapes=[
            pltpu.VMEM((PACK, total * cy, cz), jnp.float32),
            pltpu.VMEM((steps + steps % 2, total * cy, cz), jnp.float32),
            pltpu.VMEM((total * cy, cz), jnp.float32),
            pltpu.VMEM((total * cy, cz), jnp.float32),
            pltpu.VMEM((PACK, 2, total * cy, cz), jnp.float32),
            pltpu.VMEM((PACK, 2, total * cy, 2 * cz), jnp.bfloat16),
            pltpu.VMEM((SPAN * cy, (SPAN + 8) * cy), jnp.bfloat16),
            pltpu.VMEM((2 * cz, cz), jnp.bfloat16),
            pltpu.VMEM((count, rows, cy, cz), jnp.bfloat16),
            pltpu.VMEM((count, halo - rows, cy, cz), jnp.bfloat16),
            pltpu.SemaphoreType.DMA((2,)),
        ],
    )
    cells = count * total * cy * cz
    return pl.pallas_call(
        functools.partial(march, steps, rows, halo, begin),
        grid_spec=grid_spec,
        out_shape=[
            jax.ShapeDtypeStruct((count, rows, cy, cz), jnp.float32),
            jax.ShapeDtypeStruct((count, rows, cy, cz), jnp.bfloat16),
        ],
        compiler_params=pltpu.CompilerParams(vmem_limit_bytes=16 << 20),
        cost_estimate=pl.CostEstimate(flops=cells * 8000 if begin else 0, bytes_accessed=cells * 4 if begin else 0, transcendentals=0),
        name="march",
    )(bounds, *operands)


def local(probe_field, bounds, courant, snapshots, snap_times, basis_panels):
    probes_here, rows, cy, cz = probe_field.shape
    steps = snap_times.shape[0]
    half = probes_here // 2
    halo = 4 * (steps - 1)
    far = halo - rows
    devices = lax.axis_size("store")
    place = lax.axis_index("store")
    member = lax.axis_index("probe")
    members = lax.axis_size("probe")
    par = (place % 2).astype(jnp.int32)
    core = (member % 2).astype(jnp.int32)
    swap = [(i, i ^ 1) for i in range(devices)]
    perm_a = [(i, i - 2) for i in range(2, devices, 2)] + [(i, i + 2) for i in range(1, devices - 2, 2)]
    perm_b = [(i, i + 2) for i in range(0, devices - 2, 2)] + [(i, i - 2) for i in range(3, devices, 2)]
    hop = lambda x, pairs: lax.ppermute(x, "store", pairs)
    cores = lambda x: lax.ppermute(x, "probe", [(i, i ^ 1) for i in range(members)])
    cut = lambda x, start: lax.dynamic_slice_in_dim(x, start, far, axis=1)
    near = rows - far

    after = lambda x, *first: lax.optimization_barrier((x, *first))[0]
    trim = lambda x: jnp.concatenate([x[:far_half], x[near_half:]], axis=0)
    planes = lambda *xs: jnp.concatenate([x.reshape(-1, cy, cz) for x in xs], axis=0)
    near_half, far_half = shares(steps, rows, halo)

    mine = lax.dynamic_slice_in_dim(probe_field, half * par, half, axis=0)
    theirs = lax.dynamic_slice_in_dim(probe_field, half * (1 - par), half, axis=0)
    partner = hop(theirs, swap)

    slot = jnp.arange(2 * near_half)
    turn = 2 * (slot % near_half) + jnp.where(slot < near_half, core, 1 - core)
    order = jnp.sum(jnp.where(turn[:, None] == jnp.arange(steps), snap_times, 0), axis=1)
    ordered = jnp.take(after(snapshots, theirs), order, axis=0, mode="clip")
    joined, sent = ordered[:near_half], ordered[near_half:]
    gots = []
    span = 1
    while span < members:
        got = lax.ppermute(sent, "probe", [(i, i ^ span) for i in range(members)])
        upper = (member // span) % 2 == 1
        joined = jnp.concatenate([jnp.where(upper, got, joined), jnp.where(upper, joined, got)], axis=2)
        sent = joined
        gots.append(got)
        span *= 2
    high = lax.reduce_precision(courant, 8, 7)
    rate = jnp.where(core == 0, high, courant - high).astype(jnp.bfloat16)[None]
    extra = jnp.concatenate([joined, rate], axis=0)

    side_a = hop(after(mine, gots[0]), perm_a)
    side_b = hop(cut(after(mine, gots[-1]), near * (1 - par)), perm_b)
    extra_x = hop(extra, swap)
    far_own, far_x = cut(trim(extra), near * (1 - par)), cut(trim(extra_x), near * par)
    turned = jnp.transpose(after(basis_panels, extra), (1, 2, 0, 3))
    crossed = lax.ppermute(turned, "probe", [(i, i ^ 2) for i in range(members)])
    message, turned = lax.optimization_barrier((planes(partner, extra_x, far_own), turned, side_b))[:2]
    side_c = hop(message, perm_b)
    beside = [cores(extra), cores(extra_x)]
    side_d = hop(after(planes(cut(partner, near * par), extra, far_x), side_a, *beside), perm_a)
    far_other = cores(after(planes(side_c[half * rows :], side_d[half * far :]), crossed))
    operands = (mine, partner, side_a, side_b, side_c, side_d, extra, extra_x, *beside, far_other)
    first = par == 0
    own, back = [], []
    early = half * 2 // 3 // PACK * PACK
    for begin, count in ((0, early), (early, half - early)):
        kept, sent = propagate(bounds, operands, begin, count, steps, rows, halo)
        own.append(kept)
        back.append(hop(sent, swap))
    panels = [turned, cores(turned), crossed, cores(crossed)]
    own = jnp.concatenate(own, axis=0)
    back = jnp.concatenate(back, axis=0)
    in_order = lambda x, y: jnp.concatenate([jnp.where(first, x, y), jnp.where(first, y, x)], axis=0)
    low = in_order(own.astype(jnp.bfloat16), back)
    parts = [
        lax.dot_general(x, low, (((0, 1, 3), (1, 2, 3)), ((), ())), preferred_element_type=jnp.float32)
        for x in panels
    ]
    rows_of = lambda q: functools.reduce(
        lambda kept, j: jnp.where(member == j, parts[q ^ j], kept), range(1, members), parts[q]
    )
    product = jnp.concatenate([rows_of(q) for q in range(members)], axis=0)
    response = in_order(own, back.astype(jnp.float32))
    span = 1
    while span < devices:
        product = product + hop(product, [(i, i ^ span) for i in range(devices)])
        span *= 2
    return response, product


def solution(mesh):
    placed = (
        P("probe", "store", None, None),
        P("probe", None),
        P("store", None, None),
        P(None, "store", "probe", None),
        P(),
        P("probe", "store", None, None),
    )
    return jax.shard_map(
        local,
        mesh=mesh,
        in_specs=placed,
        out_specs=(P("probe", "store", None, None), P(None, "probe")),
        check_vma=False,
    )
```
